256 devices in a mesh: grp: 4 (over x_hi, core), gx: 16 (over x_lo, z), gy: 4 (over y).
Axes of the slice: x: 4 (x_hi: 2, x_lo: 2; x = x_hi * 2 + x_lo), y: 4, z: 8, core: 2. Of those that a mesh axis runs over, the one named last changes fastest.
Arguments:
- flow_fields: float32 [4, 32, 32, 512], P('grp', None, 'gx', 'gy'), may hold values from -4 to 4
- level_set: float32 [4, 64, 64, 1024], P('grp', None, 'gx', 'gy'), may hold values from -9 to 9
- band_tiles: int32 [8, 16, 64], P(None, 'gx', 'gy'), may hold values 0 or 1
- nozzle_phase: int32 [64, 1024], P('gx', 'gy'), may hold values from 0 to 2
Outputs:
- flow_next: float32 [4, 32, 32, 512], P('grp', None, 'gx', 'gy')
The draws below stay inside these ranges and needn't reach their ends.
All inputs are finite; a program needn't handle non-finite values. No bound on the sum of `band_tiles` on one device may be relied on, other than what follows from the above.
Results may differ from the reference program's by a relative error of at most 0.0003.
Values sent between devices are 32-bit elements; how exact they have to be, the bound alone decides.
No kernel may reach another device: no remote copies, remote signals or barrier semaphores. Data moves between devices by JAX's collectives and lax.ppermute only.
A program may use at most 64 MiB of HBM per device.

```python
import jax
import jax.numpy as jnp
from jax import lax

NZ = 32
SWEEPS = 3
NX = 32
NY = 512


def draw_level_set(key, part):
    extent = (4, 2 * NZ, 2 * NX, 2 * NY)
    texture = 1.5 * jax.random.normal(key, extent, jnp.float32)
    return jnp.clip(texture, -9.0, 9.0)


def with_ends(drawn, own_key, low, largest):
    longest = drawn.shape.index(max(drawn.shape))
    spots = []
    for shift in (0, 1):
        where = [jax.random.randint(jax.random.fold_in(own_key, axis), (), 0, length) for axis, length in enumerate(drawn.shape)]
        where[longest] = (where[longest] + shift) % drawn.shape[longest]
        spots.append(tuple(where))
    return drawn.at[spots[0]].set(low).at[spots[1]].set(largest)


def block_levels(rng, shape, shards, low, top_value):
    def one(position, blocks):
        steps = jax.random.uniform(jax.random.fold_in(jax.random.fold_in(rng, 6), position), (blocks,), jnp.float32, low / len(shards), top_value / len(shards))
        return jnp.repeat(jnp.exp(steps), shape[position] // blocks).reshape((-1,) + (1,) * (len(shape) - position - 1))

    gain = one(*shards[0])
    for cut in shards[1:]:
        gain = gain * one(*cut)
    return gain


def bell_draw(rng, dims, width, limit, pieces=(), held_as=jnp.bfloat16):
    gain = block_levels(rng, dims, pieces, -0.22, 0.18) if pieces else 1.0
    array = jax.random.normal(rng, dims, jnp.float32) * width * gain
    return jnp.minimum(jnp.maximum(array, -limit), limit).astype(held_as)


def setup_inputs(seed: int = 0) -> dict:
    splits = jax.random.split(jax.random.key(seed), 5)
    return {
        "flow_fields": bell_draw(splits[0], (4, NZ, NX, NY), 0.6, 4.0, ((0, 4), (2, 16), (3, 4)), jnp.float32),
        "level_set": draw_level_set(jax.random.fold_in(splits[4], 71), 0),
        "band_tiles": with_ends((jax.random.randint(splits[2], (2 * NZ // 8, NX // 2, NY // 8), 0, 3) < 2).astype(jnp.int32), jax.random.fold_in(splits[2], 1), 0, 1),
        "nozzle_phase": with_ends(jax.random.randint(splits[3], (2 * NX, 2 * NY), 0, 3), jax.random.fold_in(splits[3], 1), 0, 2).astype(jnp.int32),
    }


WENO_EPS = 1e-06
STEP_FINE = 0.3
STEP_FLOW = 0.2
SURFACE = 6.0
SPREAD = 1.5
IMPLICIT = 0.5

def weno_side(diff_one, diff_two, diff_three, diff_four, diff_five):
    cand_one = diff_one / 3.0 - 7.0 * diff_two / 6.0 + 11.0 * diff_three / 6.0
    cand_two = -diff_two / 6.0 + 5.0 * diff_three / 6.0 + diff_four / 3.0
    cand_three = diff_three / 3.0 + 5.0 * diff_four / 6.0 - diff_five / 6.0
    curve_one = diff_one - 2.0 * diff_two + diff_three
    slope_one = diff_one - 4.0 * diff_two + 3.0 * diff_three
    smooth_one = 13.0 / 12.0 * curve_one * curve_one + 0.25 * slope_one * slope_one
    curve_two = diff_two - 2.0 * diff_three + diff_four
    slope_two = diff_two - diff_four
    smooth_two = 13.0 / 12.0 * curve_two * curve_two + 0.25 * slope_two * slope_two
    curve_three = diff_three - 2.0 * diff_four + diff_five
    slope_three = 3.0 * diff_three - 4.0 * diff_four + diff_five
    smooth_three = 13.0 / 12.0 * curve_three * curve_three + 0.25 * slope_three * slope_three
    weight_one = 0.1 / ((WENO_EPS + smooth_one) * (WENO_EPS + smooth_one))
    weight_two = 0.6 / ((WENO_EPS + smooth_two) * (WENO_EPS + smooth_two))
    weight_three = 0.3 / ((WENO_EPS + smooth_three) * (WENO_EPS + smooth_three))
    return (weight_one * cand_one + weight_two * cand_two + weight_three * cand_three) / (weight_one + weight_two + weight_three)

def section_rate(padded, speeds):
    row_count = padded.shape[1] - 6
    col_count = padded.shape[2] - 6

    def sample(offset, direction):
        if direction == 0:
            return jnp.roll(padded[:, 3:3 + row_count, 3:3 + col_count], -offset, 0)
        if direction == 1:
            return padded[:, 3 + offset:3 + offset + row_count, 3:3 + col_count]
        return padded[:, 3:3 + row_count, 3 + offset:3 + offset + col_count]
    summed = jnp.zeros((padded.shape[0], row_count, col_count), jnp.float32)
    for direction in range(3):
        differences = [sample(offset + 1, direction) - sample(offset, direction) for offset in range(-3, 3)]
        minus_side = weno_side(differences[0], differences[1], differences[2], differences[3], differences[4])
        plus_side = weno_side(differences[5], differences[4], differences[3], differences[2], differences[1])
        upwind = jnp.where(speeds[direction] >= 0.0, minus_side, plus_side)
        summed = summed - speeds[direction] * upwind
    return summed

def refine(coarse):
    plane_count, height, breadth = coarse.shape
    spread_out = jnp.broadcast_to(coarse[:, None, :, None, :, None], (plane_count, 2, height, 2, breadth, 2))
    return spread_out.reshape(2 * plane_count, 2 * height, 2 * breadth)

def coarsen(fine_field):
    plane_count, height, breadth = fine_field.shape
    blocks = fine_field.reshape(plane_count // 2, 2, height // 2, 2, breadth // 2, 2)
    return lax.optimization_barrier(jnp.sum(blocks, axis=(1, 3, 5))) * 0.125

def band_cells(tile_flags):
    planes, height, breadth = tile_flags.shape
    spread_out = jnp.broadcast_to(tile_flags[:, None, :, None, :, None], (planes, 8, height, 4, breadth, 16))
    return spread_out.reshape(planes * 8, height * 4, breadth * 16)

def with_nozzle(banded, phases):
    inflow = jnp.where(phases == 2, 1.5, jnp.where(phases == 1, -1.5, banded[0]))
    return jnp.concatenate([inflow[None], banded[1:]], axis=0)

def surface_terms(padded):
    middle = padded[:, 1:-1, 1:-1]
    grad_x = (padded[:, 2:, 1:-1] - padded[:, :-2, 1:-1]) * 0.5
    grad_y = (padded[:, 1:-1, 2:] - padded[:, 1:-1, :-2]) * 0.5
    grad_z = (jnp.roll(middle, -1, 0) - jnp.roll(middle, 1, 0)) * 0.5
    inverse = 1.0 / jnp.sqrt(grad_x * grad_x + grad_y * grad_y + grad_z * grad_z + 1.0)
    normal_x = grad_x * inverse
    normal_y = grad_y * inverse
    normal_z = grad_z * inverse
    inner_z = normal_z[:, 1:-1, 1:-1]
    curvature = (normal_x[:, 2:, 1:-1] - normal_x[:, :-2, 1:-1]) * 0.5
    curvature = curvature + (normal_y[:, 1:-1, 2:] - normal_y[:, 1:-1, :-2]) * 0.5
    curvature = curvature + (jnp.roll(inner_z, -1, 0) - jnp.roll(inner_z, 1, 0)) * 0.5
    surface_level = padded[:, 2:-2, 2:-2]
    delta_peak = jnp.exp(-surface_level * surface_level / (2.0 * SPREAD * SPREAD)) / (SPREAD * 2.5066282746310002)
    strength = SURFACE * curvature * delta_peak
    fraction = 0.5 + 0.5 * jnp.tanh(surface_level / SPREAD)
    return jnp.stack([coarsen(normal_x[:, 1:-1, 1:-1] * strength), coarsen(normal_y[:, 1:-1, 1:-1] * strength), coarsen(inner_z * strength), coarsen(fraction)])

def centered(padded, direction):
    if direction == 0:
        middle = padded[:, 1:-1, 1:-1]
        return (jnp.roll(middle, -1, 0) - jnp.roll(middle, 1, 0)) * 0.5
    if direction == 1:
        return (padded[:, 2:, 1:-1] - padded[:, :-2, 1:-1]) * 0.5
    return (padded[:, 1:-1, 2:] - padded[:, 1:-1, :-2]) * 0.5

def predictor(padded_fields, component):
    moving = lax.dynamic_index_in_dim(padded_fields, component, 0, keepdims=False)
    inner_u = padded_fields[0, :, 1:-1, 1:-1]
    inner_v = padded_fields[1, :, 1:-1, 1:-1]
    inner_w = padded_fields[2, :, 1:-1, 1:-1]
    advect = -(inner_w * centered(moving, 0) + inner_u * centered(moving, 1) + inner_v * centered(moving, 2))
    pressure = padded_fields[3]
    gradients = jnp.stack([centered(pressure, 1), centered(pressure, 2), centered(pressure, 0)])
    pushed = lax.dynamic_index_in_dim(gradients, component, 0, keepdims=False)
    return moving[:, 1:-1, 1:-1] + STEP_FLOW * (advect - pushed)

def sweep_once(padded, source):
    middle = padded[:, 1:-1, 1:-1]
    beside_all = padded[:, 2:, 1:-1] + padded[:, :-2, 1:-1] + padded[:, 1:-1, 2:] + padded[:, 1:-1, :-2]
    beside_all = beside_all + jnp.roll(middle, -1, 0) + jnp.roll(middle, 1, 0)
    return (source + IMPLICIT * beside_all) / (1.0 + 6.0 * IMPLICIT)

def reference(flow_fields, level_set, band_tiles, nozzle_phase):
    padded_fields = jnp.pad(flow_fields, ((0, 0), (0, 0), (1, 1), (1, 1)), mode='wrap')
    speeds = (refine(flow_fields[2]), refine(flow_fields[0]), refine(flow_fields[1]))
    initial = level_set[3]

    def run_section(current, keep_weight, blend_weight):
        padded = jnp.pad(current, ((0, 0), (3, 3), (3, 3)), mode='wrap')
        return keep_weight * initial + blend_weight * (current + STEP_FINE * section_rate(padded, speeds))
    first_section = run_section(initial, 0.0, 1.0)
    second_section = run_section(first_section, 0.75, 0.25)
    third_section = run_section(second_section, 1.0 / 3.0, 2.0 / 3.0)
    banded = jnp.where(band_cells(band_tiles) == 1, third_section, initial)
    shaped = with_nozzle(banded, nozzle_phase)
    surface = surface_terms(jnp.pad(shaped, ((0, 0), (2, 2), (2, 2)), mode='wrap'))
    outputs = []
    for component in range(3):
        source = predictor(padded_fields, component)
        relaxed = source
        for sweep_number in range(SWEEPS):
            relaxed = sweep_once(jnp.pad(relaxed, ((0, 0), (1, 1), (1, 1)), mode='wrap'), source)
        outputs.append(relaxed + STEP_FLOW * surface[component])
    outputs.append(surface[3])
    return jnp.stack(outputs)
```

```python
import jax
import jax.numpy as jnp
from jax import lax
from jax.experimental import pallas as pl
from jax.experimental.pallas import tpu as pltpu
from jax.sharding import PartitionSpec as P


LANES = 128
FINE = 64
FLOW = 32
SLOT = 40
SHRINK = 0.25
WENO_EPS = 1e-06 * SHRINK * SHRINK
STEP_FINE = 0.3
STEP_FLOW = 0.2
SURFACE = 6.0
SPREAD = 1.5
IMPLICIT = 0.5
F32 = jnp.float32


def lane_ids(rows):
    return lax.broadcasted_iota(jnp.int32, (rows, LANES), 1)


def roll_lanes(value, shift):
    return pltpu.roll(value, shift % LANES, 1)


def exact_dot(left, right):
    return jnp.dot(left, right, precision=lax.Precision.HIGHEST, preferred_element_type=F32)


def chunk(index):
    return pl.multiple_of(index * 8, 8)


def pack_kernel(group_ref, flow_ref, level_ref, band_ref, nozzle_ref, one_ref, two_ref, three_ref, keep_ref, ring):
    group = group_ref[0]
    slot = jnp.where(group == 3, 0, group * SLOT)
    for row in range(4):
        block = level_ref[:, row, :] * SHRINK
        ring[0, row * FINE : (row + 1) * FINE, :] = block[:, :LANES]
        ring[1, row * FINE : (row + 1) * FINE, :] = block[:, LANES:]
    spread_tiles = jnp.where(
        lax.broadcasted_iota(jnp.int32, (16, 256), 1) // 16 == lax.broadcasted_iota(jnp.int32, (16, 256), 0), 1.0, 0.0
    )
    flags = exact_dot(band_ref[...].astype(F32), spread_tiles)
    phases = nozzle_ref[...].astype(F32)

    def quarter(first, second, target):
        offset = jnp.where(target % 2 == 0, 96, 32)
        plain = jnp.logical_or(target == 1, target == 2)
        low = jnp.where(plain, first, second)
        high = jnp.where(plain, second, first)
        joined = jnp.where(lane_ids(first.shape[0]) >= offset, low, high)
        return pltpu.roll(joined, LANES - offset, 1)

    for step, out_ref in enumerate((keep_ref, one_ref, two_ref, three_ref)):
        target = (group + step) % 4
        turn = (slot + 4 - 32 * target + 2 * LANES) % LANES
        for row in range(2):
            out_ref[row * FLOW : (row + 1) * FLOW, :] = pltpu.roll(flow_ref[:, row, :], turn, 1)

        def copy(index, carry, out_ref=out_ref, target=target):
            at = pl.multiple_of(index * 32, 32)
            out_ref[pl.ds(64 + at, 32), :] = quarter(ring[0, pl.ds(at, 32), :], ring[1, pl.ds(at, 32), :], target)
            return carry

        lax.fori_loop(0, 8, copy, 0)
    keep_ref[320:328, :] = quarter(flags[:, :LANES], flags[:, LANES:], group)
    keep_ref[328:332, :] = quarter(phases[:, :LANES], phases[:, LANES:], group)
    keep_ref[332:336, :] = jnp.zeros((4, LANES), F32)


def assemble_kernel(group_ref, keep_ref, one_ref, two_ref, three_ref, tile_ref, edge_ref):
    group = group_ref[0]
    lanes = lane_ids(64)
    parts = (keep_ref, one_ref, two_ref, three_ref)
    owners = [(group - step + 4) % 4 for step in range(4)]
    moving = jnp.zeros((64, LANES), F32)
    for part, owner in zip(parts, owners):
        inside = jnp.logical_and(lanes >= owner * SLOT, lanes < owner * SLOT + SLOT)
        inside = jnp.logical_and(inside, owner < 3)
        moving = jnp.where(inside, part[0:64, :], moving)
    tile_ref[0:64, :] = moving
    tile_ref[384:400, :] = keep_ref[320:336, :]
    for part, owner in zip(parts, owners):

        @pl.when(owner == 3)
        def _(part=part):
            tile_ref[64:128, :] = part[0:64, :]
            tile_ref[128:384, :] = part[64:320, :]

    pressure = tile_ref[64:128, :]
    pushed = jnp.where(lanes >= 124, roll_lanes(pressure, 88), roll_lanes(pressure, 120))
    edge_ref[0:64, :] = jnp.where(lanes >= 120, pushed, moving)
    start = jnp.where(group == 0, 0, 96)
    packed = jnp.zeros((FINE, LANES), F32)
    for row in range(4):
        turned = pltpu.roll(tile_ref[128 + row * FINE : 128 + (row + 1) * FINE, :], (32 * row - start + LANES) % LANES, 1)
        packed = jnp.where(lanes // 32 == row, turned, packed)
    edge_ref[64:128, :] = packed
    edge_ref[128:144, :] = keep_ref[320:336, :]


def edge_kernel(group_ref, tile_ref, edge_ref, fixed_ref, up_ref, down_ref):
    group = group_ref[0]
    lanes = lane_ids(64)
    first, last = group == 0, group == 3
    within = lanes % SLOT
    slots = lanes < 3 * SLOT
    low_edge = jnp.logical_and(jnp.logical_and(within < 4, slots), first)
    high_edge = jnp.logical_and(jnp.logical_and(within >= 36, slots), last)
    received = edge_ref[0:64, :]
    moving = jnp.where(jnp.logical_or(low_edge, high_edge), received, tile_ref[0:64, :])
    pressure = tile_ref[64:128, :]
    pressure = jnp.where(jnp.logical_and(lanes < 4, first), roll_lanes(received, 8), pressure)
    high_pressure = jnp.logical_and(jnp.logical_and(lanes >= 36, lanes < 40), last)
    pressure = jnp.where(high_pressure, roll_lanes(received, 40), pressure)
    fine_edge = jnp.logical_or(jnp.logical_and(lanes < 32, first), jnp.logical_and(lanes >= 96, last))
    start = jnp.where(first, 0, 96)
    fixed_ref[0:64, :] = moving
    fixed_ref[64:128, :] = pressure
    for row in range(4):
        turned = pltpu.roll(edge_ref[64:128, :], (start - 32 * row + LANES) % LANES, 1)
        level = jnp.where(fine_edge, turned, tile_ref[128 + row * FINE : 128 + (row + 1) * FINE, :])
        fixed_ref[128 + row * FINE : 128 + (row + 1) * FINE, :] = level
        if row < 3:
            down_ref[row * FINE : (row + 1) * FINE, :] = level
        if row > 0:
            up_ref[(row - 1) * FINE : row * FINE, :] = level
    marks = jnp.where(fine_edge[0:16, :], edge_ref[128:144, :], tile_ref[384:400, :])
    fixed_ref[384:400, :] = marks
    for out_ref, row in ((up_ref, 1), (down_ref, 0)):
        out_ref[192:224, :] = moving[row * FLOW : (row + 1) * FLOW, :]
        out_ref[224:256, :] = pressure[row * FLOW : (row + 1) * FLOW, :]
        out_ref[256:272, :] = marks


def bent(below, here, above):
    return (above - here) - (here - below)


def upwind_part(far_low, low, mid, high, far_high, slope, speed):
    ahead = speed >= 0.0
    one = jnp.where(ahead, far_low, far_high)
    two = jnp.where(ahead, low, high)
    four = jnp.where(ahead, high, low)
    curve_one = two - one
    curve_two = mid - two
    curve_three = four - mid
    third = 4.0 / 3.0
    smooth_one = (two * two + WENO_EPS) + curve_one * (third * curve_one + two)
    smooth_two = (two * mid + WENO_EPS) + third * (curve_two * curve_two)
    smooth_three = (mid * mid + WENO_EPS) + curve_three * (third * curve_three - mid)
    both_three = smooth_one * smooth_two
    both_two = smooth_one * smooth_three
    both_one = smooth_two * smooth_three
    weight_one = both_one * both_one
    weight_two = 6.0 * (both_two * both_two)
    weight_three = 3.0 * (both_three * both_three)
    top = weight_one * (2.0 * curve_one - 3.0 * curve_two) - (weight_two * curve_two + weight_three * curve_three)
    bottom = weight_one + weight_two + weight_three
    return speed * slope + (jnp.abs(speed) * (1.0 / 6.0)) * (top / bottom)


def fill_wrapped(wrapped, index, source, at):
    wrapped[index, 8:72, :] = source[at : at + FINE, :]
    wrapped[index, 0:8, :] = source[at + 56 : at + 64, :]
    wrapped[index, 72:80, :] = source[at : at + 8, :]


def section(rows, first_row, current, initial, speeds, wrapped, keep, blend, store):
    for index in range(rows):
        fill_wrapped(wrapped, index, *current[index + 3])

    def body(step, carry):
        z = chunk(step)

        def load(place):
            ref, at = place
            return ref[pl.ds(at + z, 8), :]

        values = [load(place) for place in current]
        bends = [bent(values[k - 1], values[k], values[k + 1]) for k in range(1, rows + 5)]
        for index in range(rows):
            here = values[index + 3]
            speed_row = (first_row + index + 2) // 2
            speed_x = speeds[0, speed_row, pl.ds(z, 8), :]
            speed_y = speeds[1, speed_row, pl.ds(z, 8), :]
            speed_z = speeds[2, speed_row, pl.ds(z, 8), :]
            rate = upwind_part(*bends[index : index + 5], (values[index + 4] - values[index + 2]) * 0.5, speed_x)
            after = roll_lanes(here, -1)
            before = roll_lanes(here, 1)
            mid = bent(before, here, after)
            rate = rate + upwind_part(
                roll_lanes(mid, 2),
                roll_lanes(mid, 1),
                mid,
                roll_lanes(mid, -1),
                roll_lanes(mid, -2),
                (after - before) * 0.5,
                speed_y,
            )
            column = [wrapped[index, pl.ds(z + 8 + offset, 8), :] for offset in range(-3, 4)]
            column[3] = here
            column_bends = [bent(column[k - 1], column[k], column[k + 1]) for k in range(1, 6)]
            rate = rate + upwind_part(*column_bends, (column[4] - column[2]) * 0.5, speed_z)
            moved = blend * (here - STEP_FINE * rate)
            if keep:
                moved = moved + keep * load(initial[index])
            store(index, z, moved)
        return carry

    lax.fori_loop(0, 8, body, 0)


def centred(below, above):
    return (above - below) * 0.5


def planes(value):
    return pltpu.roll(value, FLOW - 1, 0), pltpu.roll(value, 1, 0)


def by_slot(lanes, first, second, third):
    return jnp.where(lanes < SLOT, first, jnp.where(lanes < 2 * SLOT, second, third))


def sweep(below, here, above, source):
    up, down = planes(here)
    beside = below + above + roll_lanes(here, 1) + roll_lanes(here, -1) + up + down
    return (source + IMPLICIT * beside) / (1.0 + 6.0 * IMPLICIT)


def first_kernel(fixed_ref, left_ref, right_ref, out_ref, speed_ref, wrapped):
    moving = [
        left_ref[192:224, :],
        fixed_ref[0:32, :],
        fixed_ref[32:64, :],
        right_ref[192:224, :],
    ]
    stacked = jnp.concatenate(moving, axis=0)
    source_lane = lax.broadcasted_iota(jnp.int32, (LANES, LANES), 0)
    fine_lane = lax.broadcasted_iota(jnp.int32, (LANES, LANES), 1)
    covered = jnp.logical_and(fine_lane >= 24, fine_lane < 104)
    for component in range(3):
        pick = jnp.logical_and(source_lane == SLOT * component + fine_lane // 2 - 12, covered)
        spread = exact_dot(stacked, jnp.where(pick, 1.0, 0.0))
        for row in range(4):
            part = spread[row * FLOW : (row + 1) * FLOW, :]
            speed_ref[component, row, pl.ds(0, FLOW, stride=2), :] = part
            speed_ref[component, row, pl.ds(1, FLOW, stride=2), :] = part

    lanes = lane_ids(FLOW)
    pressure = [
        left_ref[224:256, :],
        fixed_ref[64:96, :],
        fixed_ref[96:128, :],
        right_ref[224:256, :],
    ]
    pressure = [by_slot(lanes, p, roll_lanes(p, 40), roll_lanes(p, 80)) for p in pressure]
    for row in range(2):
        here, push = moving[row + 1], pressure[row + 1]
        back, further = roll_lanes(here, 88), roll_lanes(here, 40)
        along_x = by_slot(lanes, here, further, roll_lanes(here, 80))
        along_y = by_slot(lanes, back, here, further)
        along_z = by_slot(lanes, roll_lanes(here, 48), back, here)
        up, down = planes(here)
        push_up, push_down = planes(push)
        advect = -(
            along_x * centred(moving[row], moving[row + 2])
            + along_y * centred(roll_lanes(here, 1), roll_lanes(here, -1))
            + along_z * centred(down, up)
        )
        gradient = by_slot(
            lanes,
            centred(pressure[row], pressure[row + 2]),
            centred(roll_lanes(push, 1), roll_lanes(push, -1)),
            centred(push_down, push_up),
        )
        out_ref[256 + row * FLOW : 256 + (row + 1) * FLOW, :] = here + STEP_FLOW * (advect - gradient)

    places = (
        [(left_ref, FINE * row) for row in range(3)]
        + [(fixed_ref, 128 + FINE * row) for row in range(4)]
        + [(right_ref, FINE * row) for row in range(3)]
    )

    def store(index, z, value):
        out_ref[pl.ds(index * FINE + z, 8), :] = value

    section(4, 0, places, None, speed_ref, wrapped, 0.0, 1.0, store)


def second_kernel(own_ref, left_ref, right_ref, fixed_ref, old_left, old_right, speed_ref, out_ref, up_ref, down_ref, wrapped):
    source = [ref[256 + row * FLOW : 256 + (row + 1) * FLOW, :] for ref in (left_ref, own_ref, right_ref) for row in range(2)]
    for row in range(4):
        done = sweep(source[row], source[row + 1], source[row + 2], source[row + 1])
        out_ref[384 + row * FLOW : 384 + (row + 1) * FLOW, :] = done
        if row == 1:
            up_ref[256:288, :] = done
        if row == 2:
            down_ref[256:288, :] = done
    places = [(ref, FINE * row) for ref in (left_ref, own_ref, right_ref) for row in range(4)]
    initial = [(old_left, 128)] + [(fixed_ref, 128 + FINE * row) for row in range(4)] + [(old_right, 0)]

    def store(index, z, value):
        out_ref[pl.ds(index * FINE + z, 8), :] = value
        if index < 4:
            up_ref[pl.ds(index * FINE + z, 8), :] = value
        if index > 1:
            down_ref[pl.ds((index - 2) * FINE + z, 8), :] = value

    section(6, -1, places, initial, speed_ref, wrapped, 0.75, 0.25, store)


def third_kernel(
    own_ref, left_ref, right_ref, older, older_left, older_right, fixed_ref, old_left, old_right, speed_ref,
    out_ref, wrapped, shaped, normal_x, normal_z, summed,
):
    places = (
        [(left_ref, FINE * row) for row in range(4)]
        + [(own_ref, FINE * row) for row in range(6)]
        + [(right_ref, FINE * row) for row in range(4)]
    )
    initial = (
        [(old_left, 64), (old_left, 128)]
        + [(fixed_ref, 128 + FINE * row) for row in range(4)]
        + [(old_right, 0), (old_right, 64)]
    )
    marks = [(old_left, 256)] * 2 + [(fixed_ref, 384)] * 4 + [(old_right, 256)] * 2

    def store(index, z, value):
        ref, at = initial[index]
        mark_ref, mark_at = marks[index]
        flag = mark_ref[pl.ds(mark_at + z // 8, 1), :]
        value = jnp.where(flag > 0.5, value, ref[pl.ds(at + z, 8), :]) * (1.0 / SHRINK)
        phase = mark_ref[mark_at + 8 + (index + 2) % 4 : mark_at + 9 + (index + 2) % 4, :]
        bottom = jnp.logical_and(lax.broadcasted_iota(jnp.int32, (8, LANES), 0) == 0, z == 0)
        value = jnp.where(jnp.logical_and(bottom, phase == 2.0), SPREAD, value)
        value = jnp.where(jnp.logical_and(bottom, phase == 1.0), -SPREAD, value)
        shaped[index, pl.ds(8 + z, 8), :] = value

    section(8, -2, places, initial, speed_ref, wrapped, 1.0 / 3.0, 2.0 / 3.0, store)
    for index in range(8):
        shaped[index, 0:8, :] = shaped[index, 64:72, :]
        shaped[index, 72:80, :] = shaped[index, 8:16, :]

    def normals(step, carry):
        z = chunk(step)
        middle = [shaped[k, pl.ds(8 + z, 8), :] for k in range(8)]
        for row in range(6):
            here = middle[row + 1]
            slope_x = (middle[row + 2] - middle[row]) * 0.5
            slope_y = (roll_lanes(here, -1) - roll_lanes(here, 1)) * 0.5
            slope_z = (shaped[row + 1, pl.ds(9 + z, 8), :] - shaped[row + 1, pl.ds(7 + z, 8), :]) * 0.5
            inverse = lax.rsqrt(slope_x * slope_x + slope_y * slope_y + slope_z * slope_z + 1.0)
            normal_x[row, pl.ds(z, 8), :] = slope_x * inverse
            if 0 < row < 5:
                wrapped[row, pl.ds(z, 8), :] = slope_y * inverse
                normal_z[row - 1, pl.ds(8 + z, 8), :] = slope_z * inverse
        return carry

    lax.fori_loop(0, 8, normals, 0)
    for row in range(4):
        normal_z[row, 0:8, :] = normal_z[row, 64:72, :]
        normal_z[row, 72:80, :] = normal_z[row, 8:16, :]

    def forces(step, carry):
        z = chunk(step)
        for half in range(2):
            total = None
            for row in (2 * half, 2 * half + 1):
                level = shaped[row + 2, pl.ds(8 + z, 8), :]
                here_x = normal_x[row + 1, pl.ds(z, 8), :]
                here_y = wrapped[row + 1, pl.ds(z, 8), :]
                here_z = normal_z[row, pl.ds(8 + z, 8), :]
                curvature = (normal_x[row + 2, pl.ds(z, 8), :] - normal_x[row, pl.ds(z, 8), :]) * 0.5
                curvature = curvature + (roll_lanes(here_y, -1) - roll_lanes(here_y, 1)) * 0.5
                curvature = (
                    curvature + (normal_z[row, pl.ds(9 + z, 8), :] - normal_z[row, pl.ds(7 + z, 8), :]) * 0.5
                )
                delta = jnp.exp(level * level * (-1.0 / (2.0 * SPREAD * SPREAD))) * (1.0 / (SPREAD * 2.5066282746310002))
                strength = SURFACE * curvature * delta
                fraction = 0.5 + 0.5 * jnp.tanh(level * (1.0 / SPREAD))
                terms = (here_x * strength, here_y * strength, here_z * strength, fraction)
                total = terms if total is None else tuple(a + b for a, b in zip(total, terms))
            for component in range(4):
                summed[component, pl.ds(half * FINE + z, 8), :] = total[component]
        return carry

    lax.fori_loop(0, 8, forces, 0)

    source = [older_left[288:320, :], older[256:288, :], older[288:320, :], older_right[256:288, :]]
    once = [left_ref[256:288, :]] + [own_ref[384 + row * FLOW : 384 + (row + 1) * FLOW, :] for row in range(4)]
    once = once + [right_ref[256:288, :]]
    twice = [sweep(once[row], once[row + 1], once[row + 2], source[row]) for row in range(4)]
    thrice = [sweep(twice[row], twice[row + 1], twice[row + 2], source[row + 1]) for row in range(2)]

    source_lane = lax.broadcasted_iota(jnp.int32, (LANES, LANES), 0)
    out_lane = lax.broadcasted_iota(jnp.int32, (LANES, LANES), 1)
    part, column = out_lane // FLOW, out_lane % FLOW
    take = jnp.logical_and(source_lane == SLOT * part + 4 + column, part < 3)
    done = exact_dot(jnp.concatenate(thrice, axis=0), jnp.where(take, 1.0, 0.0))
    for component in range(4):
        take = jnp.logical_and((source_lane - 32) // 2 == column, part == component)
        take = jnp.logical_and(take, jnp.logical_and(source_lane >= 32, source_lane < 96))
        scale = 0.125 * STEP_FLOW if component < 3 else 0.125
        pairs = jnp.concatenate(
            [
                summed[component, pl.ds(half * FINE, FLOW, stride=2), :]
                + summed[component, pl.ds(half * FINE + 1, FLOW, stride=2), :]
                for half in range(2)
            ],
            axis=0,
        )
        done = done + exact_dot(pairs * scale, jnp.where(take, 1.0, 0.0))
    out_ref[...] = done


def merge_kernel(group_ref, own_ref, one_ref, two_ref, three_ref, out_ref):
    group = group_ref[0]
    lanes = lane_ids(64)
    merged = jnp.zeros((64, LANES), F32)
    for step, ref in enumerate((own_ref, one_ref, two_ref, three_ref)):
        owner = (group - step + 4) % 4
        turned = pltpu.roll(ref[...], (32 * owner - 32 * group + LANES) % LANES, 1)
        merged = jnp.where(lanes // 32 == owner, turned, merged)
    for row in range(2):
        out_ref[:, row, :] = merged[row * FLOW : (row + 1) * FLOW, :]


def call(kernel, outs, scratch, *args, scalars=0):
    vmem = pl.BlockSpec(memory_space=pltpu.VMEM)
    smem = pl.BlockSpec(memory_space=pltpu.SMEM)
    shapes = [jax.ShapeDtypeStruct(shape, F32) for shape in outs]
    return pl.pallas_call(
        kernel,
        out_shape=shapes if len(shapes) > 1 else shapes[0],
        in_specs=[smem] * scalars + [vmem] * (len(args) - scalars),
        out_specs=[vmem] * len(shapes) if len(shapes) > 1 else vmem,
        scratch_shapes=[pltpu.VMEM(shape, F32) for shape in scratch],
        name=kernel.__name__,
    )(*args)


def shifted(value, axis, shift):
    count = lax.axis_size(axis)
    return lax.ppermute(value, axis, [(i, (i + shift) % count) for i in range(count)])


def to_next_block(value):
    groups, blocks = lax.axis_size("grp"), lax.axis_size("gy")
    pairs = [(j, (j + 1) % blocks) for j in range(blocks)]
    base = (groups - 1) * blocks
    pairs += [(base + j, base + (j - 1) % blocks) for j in range(blocks)]
    return lax.ppermute(value, ("grp", "gy"), pairs)


def on_device(flow_fields, level_set, band_tiles, nozzle_phase):
    group = lax.axis_index("grp").astype(jnp.int32)[None]
    message = (320, LANES)
    to_one, to_two, to_three, keep = call(
        pack_kernel,
        [message, message, message, (336, LANES)],
        [(2, 4 * FINE, LANES)],
        group,
        flow_fields[0],
        level_set[0],
        band_tiles[:, 0, :],
        nozzle_phase,
        scalars=1,
    )
    got = [shifted(value, "grp", step + 1) for step, value in enumerate((to_one, to_two, to_three))]
    tile, edge = call(assemble_kernel, [(400, LANES), (144, LANES)], [], group, keep, *got, scalars=1)
    edge = to_next_block(edge)
    fixed, up, down = call(
        edge_kernel, [(400, LANES), (272, LANES), (272, LANES)], [], group, tile, edge, scalars=1
    )
    old_left, old_right = shifted(up, "gx", 1), shifted(down, "gx", -1)
    own, speeds = call(
        first_kernel, [(320, LANES), (3, 4, FINE, LANES)], [(4, 80, LANES)], fixed, old_left, old_right
    )
    left, right = shifted(own, "gx", 1), shifted(own, "gx", -1)
    newer, up, down = call(
        second_kernel,
        [(512, LANES), (288, LANES), (288, LANES)],
        [(6, 80, LANES)],
        own,
        left,
        right,
        fixed,
        old_left,
        old_right,
        speeds,
    )
    newer_left, newer_right = shifted(up, "gx", 1), shifted(down, "gx", -1)
    result = call(
        third_kernel,
        [(64, LANES)],
        [(8, 80, LANES), (8, 80, LANES), (6, FINE, LANES), (4, 80, LANES), (4, 2 * FINE, LANES)],
        newer,
        newer_left,
        newer_right,
        own,
        left,
        right,
        fixed,
        old_left,
        old_right,
        speeds,
    )
    got = [shifted(result, "grp", step + 1) for step in range(3)]
    return call(merge_kernel, [(FLOW, 2, LANES)], [], group, result, *got, scalars=1)[None]


def solution(mesh):
    placed = (
        P("grp", None, "gx", "gy"),
        P("grp", None, "gx", "gy"),
        P(None, "gx", "gy"),
        P("gx", "gy"),
    )
    return jax.shard_map(
        on_device, mesh=mesh, in_specs=placed, out_specs=P("grp", None, "gx", "gy"), check_vma=False
    )
```

```python
import jax
import jax.numpy as jnp
from jax import lax
from jax.experimental import pallas as pl
from jax.experimental.pallas import tpu as pltpu
from jax.sharding import PartitionSpec as P


LANES = 128
FINE = 64
FLOW = 32
SLOT = 40
SHRINK = 0.25
WENO_EPS = 1e-06 * SHRINK * SHRINK
STEP_FINE = 0.3
STEP_FLOW = 0.2
SURFACE = 6.0
SPREAD = 1.5
IMPLICIT = 0.5
F32 = jnp.float32


def lane_ids(rows):
    return lax.broadcasted_iota(jnp.int32, (rows, LANES), 1)


def roll_lanes(value, shift):
    return pltpu.roll(value, shift % LANES, 1)


def exact_dot(left, right):
    return jnp.dot(left, right, precision=lax.Precision.HIGHEST, preferred_element_type=F32)


def chunk(index):
    return pl.multiple_of(index * 8, 8)


def pack_kernel(group_ref, flow_ref, level_ref, band_ref, nozzle_ref, one_ref, two_ref, three_ref, keep_ref, ring):
    group = group_ref[0]
    slot = jnp.where(group == 3, 0, group * SLOT)
    for row in range(4):
        block = level_ref[:, row, :] * SHRINK
        ring[0, row * FINE : (row + 1) * FINE, :] = block[:, :LANES]
        ring[1, row * FINE : (row + 1) * FINE, :] = block[:, LANES:]
    spread_tiles = jnp.where(
        lax.broadcasted_iota(jnp.int32, (16, 256), 1) // 16 == lax.broadcasted_iota(jnp.int32, (16, 256), 0), 1.0, 0.0
    )
    flags = exact_dot(band_ref[...].astype(F32), spread_tiles)
    phases = nozzle_ref[...].astype(F32)

    def quarter(first, second, target):
        offset = jnp.where(target % 2 == 0, 96, 32)
        plain = jnp.logical_or(target == 1, target == 2)
        low = jnp.where(plain, first, second)
        high = jnp.where(plain, second, first)
        joined = jnp.where(lane_ids(first.shape[0]) >= offset, low, high)
        return pltpu.roll(joined, LANES - offset, 1)

    for step, out_ref in enumerate((keep_ref, one_ref, two_ref, three_ref)):
        target = (group + step) % 4
        turn = (slot + 4 - 32 * target + 2 * LANES) % LANES
        for row in range(2):
            out_ref[row * FLOW : (row + 1) * FLOW, :] = pltpu.roll(flow_ref[:, row, :], turn, 1)

        for row in range(4):
            at = row * FINE
            out_ref[64 + at : 128 + at, :] = quarter(ring[0, at : at + FINE, :], ring[1, at : at + FINE, :], target)
    keep_ref[320:328, :] = quarter(flags[:, :LANES], flags[:, LANES:], group)
    keep_ref[328:332, :] = quarter(phases[:, :LANES], phases[:, LANES:], group)
    keep_ref[332:336, :] = jnp.zeros((4, LANES), F32)


def assemble_kernel(group_ref, keep_ref, one_ref, two_ref, three_ref, tile_ref, edge_ref):
    group = group_ref[0]
    lanes = lane_ids(64)
    parts = (keep_ref, one_ref, two_ref, three_ref)
    owners = [(group - step + 4) % 4 for step in range(4)]
    moving = jnp.zeros((64, LANES), F32)
    for part, owner in zip(parts, owners):
        inside = jnp.logical_and(lanes >= owner * SLOT, lanes < owner * SLOT + SLOT)
        inside = jnp.logical_and(inside, owner < 3)
        moving = jnp.where(inside, part[0:64, :], moving)
    tile_ref[0:64, :] = moving
    tile_ref[384:400, :] = keep_ref[320:336, :]
    for part, owner in zip(parts, owners):

        @pl.when(owner == 3)
        def _(part=part):
            tile_ref[64:128, :] = part[0:64, :]
            tile_ref[128:384, :] = part[64:320, :]

    pressure = tile_ref[64:128, :]
    pushed = jnp.where(lanes >= 124, roll_lanes(pressure, 88), roll_lanes(pressure, 120))
    edge_ref[0:64, :] = jnp.where(lanes >= 120, pushed, moving)
    start = jnp.where(group == 0, 0, 96)
    packed = jnp.zeros((FINE, LANES), F32)
    for row in range(4):
        turned = pltpu.roll(tile_ref[128 + row * FINE : 128 + (row + 1) * FINE, :], (32 * row - start + LANES) % LANES, 1)
        packed = jnp.where(lanes // 32 == row, turned, packed)
    edge_ref[64:128, :] = packed
    edge_ref[128:144, :] = keep_ref[320:336, :]


def edge_kernel(group_ref, tile_ref, edge_ref, fixed_ref, up_ref, down_ref):
    group = group_ref[0]
    lanes = lane_ids(64)
    first, last = group == 0, group == 3
    within = lanes % SLOT
    slots = lanes < 3 * SLOT
    low_edge = jnp.logical_and(jnp.logical_and(within < 4, slots), first)
    high_edge = jnp.logical_and(jnp.logical_and(within >= 36, slots), last)
    received = edge_ref[0:64, :]
    moving = jnp.where(jnp.logical_or(low_edge, high_edge), received, tile_ref[0:64, :])
    pressure = tile_ref[64:128, :]
    pressure = jnp.where(jnp.logical_and(lanes < 4, first), roll_lanes(received, 8), pressure)
    high_pressure = jnp.logical_and(jnp.logical_and(lanes >= 36, lanes < 40), last)
    pressure = jnp.where(high_pressure, roll_lanes(received, 40), pressure)
    fine_edge = jnp.logical_or(jnp.logical_and(lanes < 32, first), jnp.logical_and(lanes >= 96, last))
    start = jnp.where(first, 0, 96)
    fixed_ref[0:64, :] = moving
    fixed_ref[64:128, :] = pressure
    for row in range(4):
        turned = pltpu.roll(edge_ref[64:128, :], (start - 32 * row + LANES) % LANES, 1)
        level = jnp.where(fine_edge, turned, tile_ref[128 + row * FINE : 128 + (row + 1) * FINE, :])
        fixed_ref[128 + row * FINE : 128 + (row + 1) * FINE, :] = level
        if row < 3:
            down_ref[row * FINE : (row + 1) * FINE, :] = level
        if row > 0:
            up_ref[(row - 1) * FINE : row * FINE, :] = level
    marks = jnp.where(fine_edge[0:16, :], edge_ref[128:144, :], tile_ref[384:400, :])
    fixed_ref[384:400, :] = marks
    for out_ref, row in ((up_ref, 1), (down_ref, 0)):
        out_ref[192:224, :] = moving[row * FLOW : (row + 1) * FLOW, :]
        out_ref[224:256, :] = pressure[row * FLOW : (row + 1) * FLOW, :]
        out_ref[256:272, :] = marks


def bent(below, here, above):
    return (above - here) - (here - below)


def upwind_part(far_low, low, mid, high, far_high, slope, speed):
    ahead = speed >= 0.0
    one = jnp.where(ahead, far_low, far_high)
    two = jnp.where(ahead, low, high)
    four = jnp.where(ahead, high, low)
    curve_one = two - one
    curve_two = mid - two
    curve_three = four - mid
    third = 4.0 / 3.0
    smooth_one = (two * two + WENO_EPS) + curve_one * (third * curve_one + two)
    smooth_two = (two * mid + WENO_EPS) + third * (curve_two * curve_two)
    smooth_three = (mid * mid + WENO_EPS) + curve_three * (third * curve_three - mid)
    both_three = smooth_one * smooth_two
    both_two = smooth_one * smooth_three
    both_one = smooth_two * smooth_three
    weight_one = both_one * both_one
    weight_two = 6.0 * (both_two * both_two)
    weight_three = 3.0 * (both_three * both_three)
    top = weight_one * (2.0 * curve_one - 3.0 * curve_two) - (weight_two * curve_two + weight_three * curve_three)
    bottom = weight_one + weight_two + weight_three
    return speed * slope + (jnp.abs(speed) * (1.0 / 6.0)) * (top / bottom)


def fill_wrapped(wrapped, index, source, at):
    wrapped[index, 8:72, :] = source[at : at + FINE, :]
    wrapped[index, 0:8, :] = source[at + 56 : at + 64, :]
    wrapped[index, 72:80, :] = source[at : at + 8, :]


def section(rows, first_row, current, initial, speeds, wrapped, keep, blend, store):
    for index in range(rows):
        fill_wrapped(wrapped, index, *current[index + 3])

    def body(step, carry):
        z = chunk(step)

        def load(place):
            ref, at = place
            return ref[pl.ds(at + z, 8), :]

        values = [load(place) for place in current]
        bends = [bent(values[k - 1], values[k], values[k + 1]) for k in range(1, rows + 5)]
        for index in range(rows):
            here = values[index + 3]
            speed_row = (first_row + index + 2) // 2
            speed_x = speeds[0, speed_row, pl.ds(z, 8), :]
            speed_y = speeds[1, speed_row, pl.ds(z, 8), :]
            speed_z = speeds[2, speed_row, pl.ds(z, 8), :]
            rate = upwind_part(*bends[index : index + 5], (values[index + 4] - values[index + 2]) * 0.5, speed_x)
            after = roll_lanes(here, -1)
            before = roll_lanes(here, 1)
            mid = bent(before, here, after)
            rate = rate + upwind_part(
                roll_lanes(mid, 2),
                roll_lanes(mid, 1),
                mid,
                roll_lanes(mid, -1),
                roll_lanes(mid, -2),
                (after - before) * 0.5,
                speed_y,
            )
            column = [wrapped[index, pl.ds(z + 8 + offset, 8), :] for offset in range(-3, 4)]
            column[3] = here
            column_bends = [bent(column[k - 1], column[k], column[k + 1]) for k in range(1, 6)]
            rate = rate + upwind_part(*column_bends, (column[4] - column[2]) * 0.5, speed_z)
            moved = blend * (here - STEP_FINE * rate)
            if keep:
                moved = moved + keep * load(initial[index])
            store(index, z, moved)
        return carry

    lax.fori_loop(0, 8, body, 0)


def centred(below, above):
    return (above - below) * 0.5


def planes(value):
    return pltpu.roll(value, FLOW - 1, 0), pltpu.roll(value, 1, 0)


def by_slot(lanes, first, second, third):
    return jnp.where(lanes < SLOT, first, jnp.where(lanes < 2 * SLOT, second, third))


def sweep(below, here, above, source):
    up, down = planes(here)
    beside = below + above + roll_lanes(here, 1) + roll_lanes(here, -1) + up + down
    return (source + IMPLICIT * beside) / (1.0 + 6.0 * IMPLICIT)


def first_kernel(fixed_ref, left_ref, right_ref, out_ref, speed_ref, wrapped):
    moving = [
        left_ref[192:224, :],
        fixed_ref[0:32, :],
        fixed_ref[32:64, :],
        right_ref[192:224, :],
    ]
    stacked = jnp.concatenate(moving, axis=0)
    source_lane = lax.broadcasted_iota(jnp.int32, (LANES, LANES), 0)
    fine_lane = lax.broadcasted_iota(jnp.int32, (LANES, LANES), 1)
    covered = jnp.logical_and(fine_lane >= 24, fine_lane < 104)
    for component in range(3):
        pick = jnp.logical_and(source_lane == SLOT * component + fine_lane // 2 - 12, covered)
        spread = exact_dot(stacked, jnp.where(pick, 1.0, 0.0))
        for row in range(4):
            part = spread[row * FLOW : (row + 1) * FLOW, :]
            speed_ref[component, row, pl.ds(0, FLOW, stride=2), :] = part
            speed_ref[component, row, pl.ds(1, FLOW, stride=2), :] = part

    lanes = lane_ids(FLOW)
    pressure = [
        left_ref[224:256, :],
        fixed_ref[64:96, :],
        fixed_ref[96:128, :],
        right_ref[224:256, :],
    ]
    pressure = [by_slot(lanes, p, roll_lanes(p, 40), roll_lanes(p, 80)) for p in pressure]
    for row in range(2):
        here, push = moving[row + 1], pressure[row + 1]
        back, further = roll_lanes(here, 88), roll_lanes(here, 40)
        along_x = by_slot(lanes, here, further, roll_lanes(here, 80))
        along_y = by_slot(lanes, back, here, further)
        along_z = by_slot(lanes, roll_lanes(here, 48), back, here)
        up, down = planes(here)
        push_up, push_down = planes(push)
        advect = -(
            along_x * centred(moving[row], moving[row + 2])
            + along_y * centred(roll_lanes(here, 1), roll_lanes(here, -1))
            + along_z * centred(down, up)
        )
        gradient = by_slot(
            lanes,
            centred(pressure[row], pressure[row + 2]),
            centred(roll_lanes(push, 1), roll_lanes(push, -1)),
            centred(push_down, push_up),
        )
        out_ref[256 + row * FLOW : 256 + (row + 1) * FLOW, :] = here + STEP_FLOW * (advect - gradient)

    places = (
        [(left_ref, FINE * row) for row in range(3)]
        + [(fixed_ref, 128 + FINE * row) for row in range(4)]
        + [(right_ref, FINE * row) for row in range(3)]
    )

    def store(index, z, value):
        out_ref[pl.ds(index * FINE + z, 8), :] = value

    section(4, 0, places, None, speed_ref, wrapped, 0.0, 1.0, store)


def second_kernel(own_ref, left_ref, right_ref, fixed_ref, old_left, old_right, speed_ref, out_ref, up_ref, down_ref, wrapped):
    source = [ref[256 + row * FLOW : 256 + (row + 1) * FLOW, :] for ref in (left_ref, own_ref, right_ref) for row in range(2)]
    for row in range(4):
        done = sweep(source[row], source[row + 1], source[row + 2], source[row + 1])
        out_ref[384 + row * FLOW : 384 + (row + 1) * FLOW, :] = done
        if row == 1:
            up_ref[256:288, :] = done
        if row == 2:
            down_ref[256:288, :] = done
    places = [(ref, FINE * row) for ref in (left_ref, own_ref, right_ref) for row in range(4)]
    initial = [(old_left, 128)] + [(fixed_ref, 128 + FINE * row) for row in range(4)] + [(old_right, 0)]

    def store(index, z, value):
        out_ref[pl.ds(index * FINE + z, 8), :] = value
        if index < 4:
            up_ref[pl.ds(index * FINE + z, 8), :] = value
        if index > 1:
            down_ref[pl.ds((index - 2) * FINE + z, 8), :] = value

    section(6, -1, places, initial, speed_ref, wrapped, 0.75, 0.25, store)


def third_kernel(
    own_ref, left_ref, right_ref, older, older_left, older_right, fixed_ref, old_left, old_right, speed_ref,
    out_ref, wrapped, shaped, normal_x, normal_z, summed,
):
    places = (
        [(left_ref, FINE * row) for row in range(4)]
        + [(own_ref, FINE * row) for row in range(6)]
        + [(right_ref, FINE * row) for row in range(4)]
    )
    initial = (
        [(old_left, 64), (old_left, 128)]
        + [(fixed_ref, 128 + FINE * row) for row in range(4)]
        + [(old_right, 0), (old_right, 64)]
    )
    marks = [(old_left, 256)] * 2 + [(fixed_ref, 384)] * 4 + [(old_right, 256)] * 2

    def store(index, z, value):
        ref, at = initial[index]
        mark_ref, mark_at = marks[index]
        flag = mark_ref[pl.ds(mark_at + z // 8, 1), :]
        value = jnp.where(flag > 0.5, value, ref[pl.ds(at + z, 8), :]) * (1.0 / SHRINK)
        phase = mark_ref[mark_at + 8 + (index + 2) % 4 : mark_at + 9 + (index + 2) % 4, :]
        bottom = jnp.logical_and(lax.broadcasted_iota(jnp.int32, (8, LANES), 0) == 0, z == 0)
        value = jnp.where(jnp.logical_and(bottom, phase == 2.0), SPREAD, value)
        value = jnp.where(jnp.logical_and(bottom, phase == 1.0), -SPREAD, value)
        shaped[index, pl.ds(8 + z, 8), :] = value

    section(8, -2, places, initial, speed_ref, wrapped, 1.0 / 3.0, 2.0 / 3.0, store)
    for index in range(8):
        shaped[index, 0:8, :] = shaped[index, 64:72, :]
        shaped[index, 72:80, :] = shaped[index, 8:16, :]

    def normals(step, carry):
        z = chunk(step)
        middle = [shaped[k, pl.ds(8 + z, 8), :] for k in range(8)]
        for row in range(6):
            here = middle[row + 1]
            slope_x = (middle[row + 2] - middle[row]) * 0.5
            slope_y = (roll_lanes(here, -1) - roll_lanes(here, 1)) * 0.5
            slope_z = (shaped[row + 1, pl.ds(9 + z, 8), :] - shaped[row + 1, pl.ds(7 + z, 8), :]) * 0.5
            inverse = lax.rsqrt(slope_x * slope_x + slope_y * slope_y + slope_z * slope_z + 1.0)
            normal_x[row, pl.ds(z, 8), :] = slope_x * inverse
            if 0 < row < 5:
                wrapped[row, pl.ds(z, 8), :] = slope_y * inverse
                normal_z[row - 1, pl.ds(8 + z, 8), :] = slope_z * inverse
        return carry

    lax.fori_loop(0, 8, normals, 0)
    for row in range(4):
        normal_z[row, 0:8, :] = normal_z[row, 64:72, :]
        normal_z[row, 72:80, :] = normal_z[row, 8:16, :]

    def forces(step, carry):
        z = chunk(step)
        for half in range(2):
            total = None
            for row in (2 * half, 2 * half + 1):
                level = shaped[row + 2, pl.ds(8 + z, 8), :]
                here_x = normal_x[row + 1, pl.ds(z, 8), :]
                here_y = wrapped[row + 1, pl.ds(z, 8), :]
                here_z = normal_z[row, pl.ds(8 + z, 8), :]
                curvature = (normal_x[row + 2, pl.ds(z, 8), :] - normal_x[row, pl.ds(z, 8), :]) * 0.5
                curvature = curvature + (roll_lanes(here_y, -1) - roll_lanes(here_y, 1)) * 0.5
                curvature = (
                    curvature + (normal_z[row, pl.ds(9 + z, 8), :] - normal_z[row, pl.ds(7 + z, 8), :]) * 0.5
                )
                delta = jnp.exp(level * level * (-1.0 / (2.0 * SPREAD * SPREAD))) * (1.0 / (SPREAD * 2.5066282746310002))
                strength = SURFACE * curvature * delta
                fraction = 0.5 + 0.5 * jnp.tanh(level * (1.0 / SPREAD))
                terms = (here_x * strength, here_y * strength, here_z * strength, fraction)
                total = terms if total is None else tuple(a + b for a, b in zip(total, terms))
            for component in range(4):
                summed[component, pl.ds(half * FINE + z, 8), :] = total[component]
        return carry

    lax.fori_loop(0, 8, forces, 0)

    source = [older_left[288:320, :], older[256:288, :], older[288:320, :], older_right[256:288, :]]
    once = [left_ref[256:288, :]] + [own_ref[384 + row * FLOW : 384 + (row + 1) * FLOW, :] for row in range(4)]
    once = once + [right_ref[256:288, :]]
    twice = [sweep(once[row], once[row + 1], once[row + 2], source[row]) for row in range(4)]
    thrice = [sweep(twice[row], twice[row + 1], twice[row + 2], source[row + 1]) for row in range(2)]

    source_lane = lax.broadcasted_iota(jnp.int32, (LANES, LANES), 0)
    out_lane = lax.broadcasted_iota(jnp.int32, (LANES, LANES), 1)
    part, column = out_lane // FLOW, out_lane % FLOW
    take = jnp.logical_and(source_lane == SLOT * part + 4 + column, part < 3)
    done = exact_dot(jnp.concatenate(thrice, axis=0), jnp.where(take, 1.0, 0.0))
    for component in range(4):
        take = jnp.logical_and((source_lane - 32) // 2 == column, part == component)
        take = jnp.logical_and(take, jnp.logical_and(source_lane >= 32, source_lane < 96))
        scale = 0.125 * STEP_FLOW if component < 3 else 0.125
        pairs = jnp.concatenate(
            [
                summed[component, pl.ds(half * FINE, FLOW, stride=2), :]
                + summed[component, pl.ds(half * FINE + 1, FLOW, stride=2), :]
                for half in range(2)
            ],
            axis=0,
        )
        done = done + exact_dot(pairs * scale, jnp.where(take, 1.0, 0.0))
    out_ref[...] = done


def merge_kernel(group_ref, own_ref, one_ref, two_ref, three_ref, out_ref):
    group = group_ref[0]
    lanes = lane_ids(64)
    merged = jnp.zeros((64, LANES), F32)
    for step, ref in enumerate((own_ref, one_ref, two_ref, three_ref)):
        owner = (group - step + 4) % 4
        turned = pltpu.roll(ref[...], (32 * owner - 32 * group + LANES) % LANES, 1)
        merged = jnp.where(lanes // 32 == owner, turned, merged)
    for row in range(2):
        out_ref[:, row, :] = merged[row * FLOW : (row + 1) * FLOW, :]


def call(kernel, outs, scratch, *args, scalars=0, outer=False, last=False):
    vmem = pl.BlockSpec(memory_space=pltpu.VMEM)
    smem = pl.BlockSpec(memory_space=pltpu.SMEM)
    shapes = [jax.ShapeDtypeStruct(shape, F32) if last else pltpu.VMEM(shape, F32) for shape in outs]
    held = list(args[scalars:])
    if not outer:
        held = [pltpu.with_memory_space_constraint(value, pltpu.VMEM) for value in held]
    return pl.pallas_call(
        kernel,
        out_shape=shapes if len(shapes) > 1 else shapes[0],
        in_specs=[smem] * scalars + [vmem] * len(held),
        out_specs=[vmem] * len(shapes) if len(shapes) > 1 else vmem,
        scratch_shapes=[pltpu.VMEM(shape, F32) for shape in scratch],
        name=kernel.__name__,
    )(*args[:scalars], *held)


def shifted(value, axis, shift):
    count = lax.axis_size(axis)
    return lax.ppermute(value, axis, [(i, (i + shift) % count) for i in range(count)])


def to_next_block(value):
    groups, blocks = lax.axis_size("grp"), lax.axis_size("gy")
    pairs = [(j, (j + 1) % blocks) for j in range(blocks)]
    base = (groups - 1) * blocks
    pairs += [(base + j, base + (j - 1) % blocks) for j in range(blocks)]
    return lax.ppermute(value, ("grp", "gy"), pairs)


def on_device(flow_fields, level_set, band_tiles, nozzle_phase):
    group = lax.axis_index("grp").astype(jnp.int32)[None]
    message = (320, LANES)
    to_one, to_two, to_three, keep = call(
        pack_kernel,
        [message, message, message, (336, LANES)],
        [(2, 4 * FINE, LANES)],
        group,
        flow_fields[0],
        level_set[0],
        band_tiles[:, 0, :],
        nozzle_phase,
        scalars=1,
        outer=True,
    )
    got = [shifted(value, "grp", step + 1) for step, value in enumerate((to_one, to_two, to_three))]
    tile, edge = call(assemble_kernel, [(400, LANES), (144, LANES)], [], group, keep, *got, scalars=1)
    edge = to_next_block(edge)
    fixed, up, down = call(
        edge_kernel, [(400, LANES), (272, LANES), (272, LANES)], [], group, tile, edge, scalars=1
    )
    old_left, old_right = shifted(up, "gx", 1), shifted(down, "gx", -1)
    own, speeds = call(
        first_kernel, [(320, LANES), (3, 4, FINE, LANES)], [(4, 80, LANES)], fixed, old_left, old_right
    )
    left, right = shifted(own, "gx", 1), shifted(own, "gx", -1)
    newer, up, down = call(
        second_kernel,
        [(512, LANES), (288, LANES), (288, LANES)],
        [(6, 80, LANES)],
        own,
        left,
        right,
        fixed,
        old_left,
        old_right,
        speeds,
    )
    newer_left, newer_right = shifted(up, "gx", 1), shifted(down, "gx", -1)
    result = call(
        third_kernel,
        [(64, LANES)],
        [(8, 80, LANES), (8, 80, LANES), (6, FINE, LANES), (4, 80, LANES), (4, 2 * FINE, LANES)],
        newer,
        newer_left,
        newer_right,
        own,
        left,
        right,
        fixed,
        old_left,
        old_right,
        speeds,
    )
    got = [shifted(result, "grp", step + 1) for step in range(3)]
    return call(merge_kernel, [(FLOW, 2, LANES)], [], group, result, *got, scalars=1, last=True)[None]


def solution(mesh):
    placed = (
        P("grp", None, "gx", "gy"),
        P("grp", None, "gx", "gy"),
        P(None, "gx", "gy"),
        P("gx", "gy"),
    )
    return jax.shard_map(
        on_device, mesh=mesh, in_specs=placed, out_specs=P("grp", None, "gx", "gy"), check_vma=False
    )
```

```python
import jax
import jax.numpy as jnp
from jax import lax
from jax.experimental import pallas as pl
from jax.experimental.pallas import tpu as pltpu
from jax.sharding import PartitionSpec as P


LANES = 128
FINE = 64
FLOW = 32
SLOT = 40
LEVEL = 64
SHRINK = 0.25
WENO_EPS = 1e-06 * SHRINK * SHRINK
STEP_FINE = 0.3
STEP_FLOW = 0.2
SURFACE = 6.0
SPREAD = 1.5
IMPLICIT = 0.5
F32 = jnp.float32


def lane_ids(rows):
    return lax.broadcasted_iota(jnp.int32, (rows, LANES), 1)


def roll_lanes(value, shift):
    return pltpu.roll(value, shift % LANES, 1)


def exact_dot(left, right):
    return jnp.dot(left, right, precision=lax.Precision.HIGHEST, preferred_element_type=F32)


def chunk(index):
    return pl.multiple_of(index * 8, 8)


def pack_kernel(flow_ref, level_ref, band_ref, nozzle_ref, raw_ref, mark_ref):
    for row in range(2):
        raw_ref[row * FLOW : (row + 1) * FLOW, :] = flow_ref[:, row, :]
    for row in range(4):
        block = level_ref[:, row, :] * SHRINK
        raw_ref[LEVEL + row * FINE : LEVEL + (row + 1) * FINE, :] = block[:, :LANES]
        raw_ref[LEVEL + (row + 4) * FINE : LEVEL + (row + 5) * FINE, :] = block[:, LANES:]
    spread_tiles = jnp.where(
        lax.broadcasted_iota(jnp.int32, (16, 256), 1) // 16 == lax.broadcasted_iota(jnp.int32, (16, 256), 0), 1.0, 0.0
    )
    flags = exact_dot(band_ref[...].astype(F32), spread_tiles)
    phases = nozzle_ref[...].astype(F32)
    for half in range(2):
        part = slice(half * LANES, (half + 1) * LANES)
        mark_ref[half, 0:8, :] = flags[:, part]
        mark_ref[half, 8:12, :] = phases[:, part]
        mark_ref[half, 12:16, :] = jnp.zeros((4, LANES), F32)


def level_rows(ref, tile, row):
    at = LEVEL + (4 * tile + row) * FINE
    return ref[at : at + FINE, :]


def split_kernel(group_ref, raw_ref, other_ref, mark_ref, half_ref, edge_ref):
    group = group_ref[0]
    lanes = lane_ids(FINE)
    half_ref[0:64, :] = raw_ref[0:64, :]

    for core in range(2):
        level, (lower, upper) = (
            (raw_ref, (other_ref, raw_ref)) if core else (other_ref, (raw_ref, other_ref))
        )

        @pl.when(group % 2 == core)
        def _(core=core, level=level, lower=lower, upper=upper):
            for row in range(2):
                half_ref[64 + row * FINE : 64 + (row + 1) * FINE, :] = level_rows(level, 0, 2 * core + row)
            beyond = level_rows(level, 1, 0)
            for row in range(1, 4):
                beyond = jnp.where(lanes < 16 * row, beyond, roll_lanes(level_rows(level, 1, row), 16 * row))
            half_ref[192:256, :] = beyond

            def edges(tile, level_start, field_start):
                packed = roll_lanes(level_rows(level, tile, 0), -level_start)
                for row in range(1, 4):
                    turned = roll_lanes(level_rows(level, tile, row), 16 * row - level_start)
                    packed = jnp.where(lanes < 16 * row, packed, turned)
                packed = jnp.where(lanes < 64, packed, roll_lanes(lower[0:64, :], 64 - field_start))
                packed = jnp.where(lanes < 72, packed, roll_lanes(upper[0:64, :], 72 - field_start))
                edge_ref[0:64, :] = packed
                edge_ref[64:80, :] = mark_ref[tile]

            ahead = jnp.logical_or(group == 0, group == 3)

            @pl.when(ahead)
            def _():
                edges(1, 112, 120)

            @pl.when(jnp.logical_not(ahead))
            def _():
                edges(0, 0, 0)


def join_kernel(half_ref, edge_ref, out_ref):
    out_ref[0:256, :] = half_ref[...]
    out_ref[256:336, :] = edge_ref[...]


def assemble_kernel(
    group_ref, raw_ref, other_ref, mark_ref, half_ref, far_half_ref, fixed_ref, up_ref, down_ref
):
    group = group_ref[0]
    lanes = lane_ids(64)

    def assemble(own):
        core, first, last = own % 2, own == 0, own == 3
        local = (raw_ref, other_ref) if core == 0 else (other_ref, raw_ref)
        remote = (half_ref, far_half_ref) if core == 0 else (far_half_ref, half_ref)
        fields = [ref[0:64, :] for ref in ((*local, *remote) if own < 2 else (*remote, *local))]
        near, far = half_ref[256:320, :], far_half_ref[256:320, :]

        def placed(index, lane):
            value = roll_lanes(fields[index], lane + 4 - 32 * own)
            edge = (near, near, far, far)[index]
            source = 64 + 8 * (index % 2)
            if first:
                value = jnp.where(lanes < lane + 4, roll_lanes(edge, lane - source - 4), value)
            if last:
                value = jnp.where(lanes >= lane + 36, roll_lanes(edge, lane + 36 - source), value)
            return value

        parts = [placed(index, SLOT * index) for index in range(3)]
        moving = by_slot(lanes, *parts)
        pressure = placed(3, 0)
        fixed_ref[0:64, :] = moving
        fixed_ref[64:128, :] = pressure
        for row in range(4):
            if own < 2:
                low = remote[row // 2][64 + (row % 2) * FINE : 64 + (row % 2 + 1) * FINE, :]
                high = roll_lanes(far_half_ref[192:256, :] if core == 0 else half_ref[192:256, :], -16 * row)
            else:
                level = raw_ref if core else other_ref
                low, high = level_rows(level, 0, row), level_rows(level, 1, row)
            value = {
                0: lambda: jnp.where(lanes < 32, roll_lanes(far, 16 - 16 * row), roll_lanes(low, 32)),
                1: lambda: roll_lanes(jnp.where(lanes < 32, high, low), 96),
                2: lambda: roll_lanes(jnp.where(lanes < 96, high, low), 32),
                3: lambda: jnp.where(lanes < 96, roll_lanes(high, 96), roll_lanes(far, 96 - 16 * row)),
            }[own]()
            fixed_ref[128 + row * FINE : 128 + (row + 1) * FINE, :] = value
            if row < 3:
                down_ref[row * FINE : (row + 1) * FINE, :] = value
            if row > 0:
                up_ref[(row - 1) * FINE : row * FINE, :] = value
        low, high, beside, few = mark_ref[0], mark_ref[1], half_ref[320:336, :], lane_ids(16)
        marks = {
            0: lambda: roll_lanes(jnp.where(few < 96, low, beside), 32),
            1: lambda: roll_lanes(jnp.where(few < 32, high, low), 96),
            2: lambda: roll_lanes(jnp.where(few < 96, high, low), 32),
            3: lambda: roll_lanes(jnp.where(few < 32, beside, high), 96),
        }[own]()
        fixed_ref[384:400, :] = marks
        for out_ref, row in ((up_ref, 1), (down_ref, 0)):
            out_ref[192:224, :] = moving[row * FLOW : (row + 1) * FLOW, :]
            out_ref[224:256, :] = pressure[row * FLOW : (row + 1) * FLOW, :]
            out_ref[256:272, :] = marks

    for own in range(4):

        @pl.when(group == own)
        def _(own=own):
            assemble(own)


def bent(below, here, above):
    return (above - here) - (here - below)


def upwind_part(far_low, low, mid, high, far_high, slope, speed):
    ahead = speed >= 0.0
    one = jnp.where(ahead, far_low, far_high)
    two = jnp.where(ahead, low, high)
    four = jnp.where(ahead, high, low)
    curve_one = two - one
    curve_two = mid - two
    curve_three = four - mid
    third = 4.0 / 3.0
    smooth_one = (two * two + WENO_EPS) + curve_one * (third * curve_one + two)
    smooth_two = (two * mid + WENO_EPS) + third * (curve_two * curve_two)
    smooth_three = (mid * mid + WENO_EPS) + curve_three * (third * curve_three - mid)
    both_three = smooth_one * smooth_two
    both_two = smooth_one * smooth_three
    both_one = smooth_two * smooth_three
    weight_one = both_one * both_one
    weight_two = 6.0 * (both_two * both_two)
    weight_three = 3.0 * (both_three * both_three)
    top = weight_one * (2.0 * curve_one - 3.0 * curve_two) - (weight_two * curve_two + weight_three * curve_three)
    bottom = weight_one + weight_two + weight_three
    return speed * slope + (jnp.abs(speed) * (1.0 / 6.0)) * (top / bottom)


def fill_wrapped(wrapped, index, source, at):
    wrapped[index, 8:72, :] = source[at : at + FINE, :]
    wrapped[index, 0:8, :] = source[at + 56 : at + 64, :]
    wrapped[index, 72:80, :] = source[at : at + 8, :]


def section(rows, first_row, current, initial, speeds, wrapped, keep, blend, store):
    for index in range(rows):
        fill_wrapped(wrapped, index, *current[index + 3])

    def body(step, carry):
        z = chunk(step)

        def load(place):
            ref, at = place
            return ref[pl.ds(at + z, 8), :]

        values = [load(place) for place in current]
        bends = [bent(values[k - 1], values[k], values[k + 1]) for k in range(1, rows + 5)]
        for index in range(rows):
            here = values[index + 3]
            speed_row = (first_row + index + 2) // 2
            speed_x = speeds[0, speed_row, pl.ds(z, 8), :]
            speed_y = speeds[1, speed_row, pl.ds(z, 8), :]
            speed_z = speeds[2, speed_row, pl.ds(z, 8), :]
            rate = upwind_part(*bends[index : index + 5], (values[index + 4] - values[index + 2]) * 0.5, speed_x)
            after = roll_lanes(here, -1)
            before = roll_lanes(here, 1)
            mid = bent(before, here, after)
            rate = rate + upwind_part(
                roll_lanes(mid, 2),
                roll_lanes(mid, 1),
                mid,
                roll_lanes(mid, -1),
                roll_lanes(mid, -2),
                (after - before) * 0.5,
                speed_y,
            )
            column = [wrapped[index, pl.ds(z + 8 + offset, 8), :] for offset in range(-3, 4)]
            column[3] = here
            column_bends = [bent(column[k - 1], column[k], column[k + 1]) for k in range(1, 6)]
            rate = rate + upwind_part(*column_bends, (column[4] - column[2]) * 0.5, speed_z)
            moved = blend * (here - STEP_FINE * rate)
            if keep:
                moved = moved + keep * load(initial[index])
            store(index, z, moved)
        return carry

    lax.fori_loop(0, 8, body, 0)


def centred(below, above):
    return (above - below) * 0.5


def planes(value):
    return pltpu.roll(value, FLOW - 1, 0), pltpu.roll(value, 1, 0)


def by_slot(lanes, first, second, third):
    return jnp.where(lanes < SLOT, first, jnp.where(lanes < 2 * SLOT, second, third))


def sweep(below, here, above, source):
    up, down = planes(here)
    beside = below + above + roll_lanes(here, 1) + roll_lanes(here, -1) + up + down
    return (source + IMPLICIT * beside) / (1.0 + 6.0 * IMPLICIT)


def first_kernel(fixed_ref, left_ref, right_ref, out_ref, speed_ref, wrapped):
    moving = [
        left_ref[192:224, :],
        fixed_ref[0:32, :],
        fixed_ref[32:64, :],
        right_ref[192:224, :],
    ]
    stacked = jnp.concatenate(moving, axis=0)
    source_lane = lax.broadcasted_iota(jnp.int32, (LANES, LANES), 0)
    fine_lane = lax.broadcasted_iota(jnp.int32, (LANES, LANES), 1)
    covered = jnp.logical_and(fine_lane >= 24, fine_lane < 104)
    for component in range(3):
        pick = jnp.logical_and(source_lane == SLOT * component + fine_lane // 2 - 12, covered)
        spread = exact_dot(stacked, jnp.where(pick, 1.0, 0.0))
        for row in range(4):
            part = spread[row * FLOW : (row + 1) * FLOW, :]
            speed_ref[component, row, pl.ds(0, FLOW, stride=2), :] = part
            speed_ref[component, row, pl.ds(1, FLOW, stride=2), :] = part

    lanes = lane_ids(FLOW)
    pressure = [
        left_ref[224:256, :],
        fixed_ref[64:96, :],
        fixed_ref[96:128, :],
        right_ref[224:256, :],
    ]
    pressure = [by_slot(lanes, p, roll_lanes(p, 40), roll_lanes(p, 80)) for p in pressure]
    for row in range(2):
        here, push = moving[row + 1], pressure[row + 1]
        back, further = roll_lanes(here, 88), roll_lanes(here, 40)
        along_x = by_slot(lanes, here, further, roll_lanes(here, 80))
        along_y = by_slot(lanes, back, here, further)
        along_z = by_slot(lanes, roll_lanes(here, 48), back, here)
        up, down = planes(here)
        push_up, push_down = planes(push)
        advect = -(
            along_x * centred(moving[row], moving[row + 2])
            + along_y * centred(roll_lanes(here, 1), roll_lanes(here, -1))
            + along_z * centred(down, up)
        )
        gradient = by_slot(
            lanes,
            centred(pressure[row], pressure[row + 2]),
            centred(roll_lanes(push, 1), roll_lanes(push, -1)),
            centred(push_down, push_up),
        )
        out_ref[256 + row * FLOW : 256 + (row + 1) * FLOW, :] = here + STEP_FLOW * (advect - gradient)

    places = (
        [(left_ref, FINE * row) for row in range(3)]
        + [(fixed_ref, 128 + FINE * row) for row in range(4)]
        + [(right_ref, FINE * row) for row in range(3)]
    )

    def store(index, z, value):
        out_ref[pl.ds(index * FINE + z, 8), :] = value

    section(4, 0, places, None, speed_ref, wrapped, 0.0, 1.0, store)


def second_kernel(own_ref, left_ref, right_ref, fixed_ref, old_left, old_right, speed_ref, out_ref, up_ref, down_ref, wrapped):
    source = [ref[256 + row * FLOW : 256 + (row + 1) * FLOW, :] for ref in (left_ref, own_ref, right_ref) for row in range(2)]
    for row in range(4):
        done = sweep(source[row], source[row + 1], source[row + 2], source[row + 1])
        out_ref[384 + row * FLOW : 384 + (row + 1) * FLOW, :] = done
        if row == 1:
            up_ref[256:288, :] = done
        if row == 2:
            down_ref[256:288, :] = done
    places = [(ref, FINE * row) for ref in (left_ref, own_ref, right_ref) for row in range(4)]
    initial = [(old_left, 128)] + [(fixed_ref, 128 + FINE * row) for row in range(4)] + [(old_right, 0)]

    def store(index, z, value):
        out_ref[pl.ds(index * FINE + z, 8), :] = value
        if index < 4:
            up_ref[pl.ds(index * FINE + z, 8), :] = value
        if index > 1:
            down_ref[pl.ds((index - 2) * FINE + z, 8), :] = value

    section(6, -1, places, initial, speed_ref, wrapped, 0.75, 0.25, store)


def third_kernel(
    own_ref, left_ref, right_ref, older, older_left, older_right, fixed_ref, old_left, old_right, speed_ref,
    out_ref, wrapped, shaped, normal_x, normal_z, summed,
):
    places = (
        [(left_ref, FINE * row) for row in range(4)]
        + [(own_ref, FINE * row) for row in range(6)]
        + [(right_ref, FINE * row) for row in range(4)]
    )
    initial = (
        [(old_left, 64), (old_left, 128)]
        + [(fixed_ref, 128 + FINE * row) for row in range(4)]
        + [(old_right, 0), (old_right, 64)]
    )
    marks = [(old_left, 256)] * 2 + [(fixed_ref, 384)] * 4 + [(old_right, 256)] * 2

    def store(index, z, value):
        ref, at = initial[index]
        mark_ref, mark_at = marks[index]
        flag = mark_ref[pl.ds(mark_at + z // 8, 1), :]
        value = jnp.where(flag > 0.5, value, ref[pl.ds(at + z, 8), :]) * (1.0 / SHRINK)
        phase = mark_ref[mark_at + 8 + (index + 2) % 4 : mark_at + 9 + (index + 2) % 4, :]
        bottom = jnp.logical_and(lax.broadcasted_iota(jnp.int32, (8, LANES), 0) == 0, z == 0)
        value = jnp.where(jnp.logical_and(bottom, phase == 2.0), SPREAD, value)
        value = jnp.where(jnp.logical_and(bottom, phase == 1.0), -SPREAD, value)
        shaped[index, pl.ds(8 + z, 8), :] = value

    section(8, -2, places, initial, speed_ref, wrapped, 1.0 / 3.0, 2.0 / 3.0, store)
    for index in range(8):
        shaped[index, 0:8, :] = shaped[index, 64:72, :]
        shaped[index, 72:80, :] = shaped[index, 8:16, :]

    def normals(step, carry):
        z = chunk(step)
        middle = [shaped[k, pl.ds(8 + z, 8), :] for k in range(8)]
        for row in range(6):
            here = middle[row + 1]
            slope_x = (middle[row + 2] - middle[row]) * 0.5
            slope_y = (roll_lanes(here, -1) - roll_lanes(here, 1)) * 0.5
            slope_z = (shaped[row + 1, pl.ds(9 + z, 8), :] - shaped[row + 1, pl.ds(7 + z, 8), :]) * 0.5
            inverse = lax.rsqrt(slope_x * slope_x + slope_y * slope_y + slope_z * slope_z + 1.0)
            normal_x[row, pl.ds(z, 8), :] = slope_x * inverse
            if 0 < row < 5:
                wrapped[row, pl.ds(z, 8), :] = slope_y * inverse
                normal_z[row - 1, pl.ds(8 + z, 8), :] = slope_z * inverse
        return carry

    lax.fori_loop(0, 8, normals, 0)
    for row in range(4):
        normal_z[row, 0:8, :] = normal_z[row, 64:72, :]
        normal_z[row, 72:80, :] = normal_z[row, 8:16, :]

    def forces(step, carry):
        z = chunk(step)
        for half in range(2):
            total = None
            for row in (2 * half, 2 * half + 1):
                level = shaped[row + 2, pl.ds(8 + z, 8), :]
                here_x = normal_x[row + 1, pl.ds(z, 8), :]
                here_y = wrapped[row + 1, pl.ds(z, 8), :]
                here_z = normal_z[row, pl.ds(8 + z, 8), :]
                curvature = (normal_x[row + 2, pl.ds(z, 8), :] - normal_x[row, pl.ds(z, 8), :]) * 0.5
                curvature = curvature + (roll_lanes(here_y, -1) - roll_lanes(here_y, 1)) * 0.5
                curvature = (
                    curvature + (normal_z[row, pl.ds(9 + z, 8), :] - normal_z[row, pl.ds(7 + z, 8), :]) * 0.5
                )
                delta = jnp.exp(level * level * (-1.0 / (2.0 * SPREAD * SPREAD))) * (1.0 / (SPREAD * 2.5066282746310002))
                strength = SURFACE * curvature * delta
                fraction = 0.5 + 0.5 * jnp.tanh(level * (1.0 / SPREAD))
                terms = (here_x * strength, here_y * strength, here_z * strength, fraction)
                total = terms if total is None else tuple(a + b for a, b in zip(total, terms))
            for component in range(4):
                summed[component, pl.ds(half * FINE + z, 8), :] = total[component]
        return carry

    lax.fori_loop(0, 8, forces, 0)

    source = [older_left[288:320, :], older[256:288, :], older[288:320, :], older_right[256:288, :]]
    once = [left_ref[256:288, :]] + [own_ref[384 + row * FLOW : 384 + (row + 1) * FLOW, :] for row in range(4)]
    once = once + [right_ref[256:288, :]]
    twice = [sweep(once[row], once[row + 1], once[row + 2], source[row]) for row in range(4)]
    thrice = [sweep(twice[row], twice[row + 1], twice[row + 2], source[row + 1]) for row in range(2)]

    source_lane = lax.broadcasted_iota(jnp.int32, (LANES, LANES), 0)
    out_lane = lax.broadcasted_iota(jnp.int32, (LANES, LANES), 1)
    part, column = out_lane // FLOW, out_lane % FLOW
    take = jnp.logical_and(source_lane == SLOT * part + 4 + column, part < 3)
    done = exact_dot(jnp.concatenate(thrice, axis=0), jnp.where(take, 1.0, 0.0))
    for component in range(4):
        take = jnp.logical_and((source_lane - 32) // 2 == column, part == component)
        take = jnp.logical_and(take, jnp.logical_and(source_lane >= 32, source_lane < 96))
        scale = 0.125 * STEP_FLOW if component < 3 else 0.125
        pairs = jnp.concatenate(
            [
                summed[component, pl.ds(half * FINE, FLOW, stride=2), :]
                + summed[component, pl.ds(half * FINE + 1, FLOW, stride=2), :]
                for half in range(2)
            ],
            axis=0,
        )
        done = done + exact_dot(pairs * scale, jnp.where(take, 1.0, 0.0))
    out_ref[...] = done


def sort_kernel(group_ref, own_ref, other_ref, keep_ref, send_ref):
    group = group_ref[0]
    lanes = lane_ids(64)
    beside = group + 1 - 2 * (group % 2)
    for target, out_ref in ((group, keep_ref), ((group + 2) % 4, send_ref)):
        own = pltpu.roll(own_ref[...], (32 * group - 32 * target + LANES) % LANES, 1)
        other = pltpu.roll(other_ref[...], (32 * beside - 32 * target + LANES) % LANES, 1)
        out_ref[...] = jnp.where(lanes // 32 == group, own, other)


def merge_kernel(group_ref, keep_ref, far_ref, out_ref):
    merged = jnp.where(lane_ids(64) // 64 == group_ref[0] // 2, keep_ref[...], far_ref[...])
    for row in range(2):
        out_ref[:, row, :] = merged[row * FLOW : (row + 1) * FLOW, :]


def call(kernel, outs, scratch, *args, scalars=0, outer=False, last=False):
    vmem = pl.BlockSpec(memory_space=pltpu.VMEM)
    smem = pl.BlockSpec(memory_space=pltpu.SMEM)
    shapes = [jax.ShapeDtypeStruct(shape, F32) if last else pltpu.VMEM(shape, F32) for shape in outs]
    held = list(args[scalars:])
    if not outer:
        held = [pltpu.with_memory_space_constraint(value, pltpu.VMEM) for value in held]
    return pl.pallas_call(
        kernel,
        out_shape=shapes if len(shapes) > 1 else shapes[0],
        in_specs=[smem] * scalars + [vmem] * len(held),
        out_specs=[vmem] * len(shapes) if len(shapes) > 1 else vmem,
        scratch_shapes=[pltpu.VMEM(shape, F32) for shape in scratch],
        name=kernel.__name__,
    )(*args[:scalars], *held)


def shifted(value, axis, shift):
    count = lax.axis_size(axis)
    return lax.ppermute(value, axis, [(i, (i + shift) % count) for i in range(count)])


def crossed(value, bit):
    return lax.ppermute(value, "grp", [(i, i ^ bit) for i in range(lax.axis_size("grp"))])


def to_next_blocks(value):
    blocks = lax.axis_size("gy")
    pairs = []
    for source, target, step in ((0, 0, 1), (1, 3, -1), (2, 2, -1), (3, 1, 1)):
        pairs += [(source * blocks + j, target * blocks + (j + step) % blocks) for j in range(blocks)]
    return lax.ppermute(value, ("grp", "gy"), pairs)


def on_device(flow_fields, level_set, band_tiles, nozzle_phase):
    group = lax.axis_index("grp").astype(jnp.int32)[None]
    raw, marks = call(
        pack_kernel,
        [(LEVEL + 8 * FINE, LANES), (2, 16, LANES)],
        [],
        flow_fields[0],
        level_set[0],
        band_tiles[:, 0, :],
        nozzle_phase,
        outer=True,
    )
    other = crossed(raw, 1)
    half, edge = call(split_kernel, [(256, LANES), (80, LANES)], [], group, raw, other, marks, scalars=1)
    half = call(join_kernel, [(336, LANES)], [], crossed(half, 2), to_next_blocks(edge))
    far_half = crossed(half, 1)
    fixed, up, down = call(
        assemble_kernel,
        [(400, LANES), (272, LANES), (272, LANES)],
        [],
        group,
        raw,
        other,
        marks,
        half,
        far_half,
        scalars=1,
    )
    old_left, old_right = shifted(up, "gx", 1), shifted(down, "gx", -1)
    own, speeds = call(
        first_kernel, [(320, LANES), (3, 4, FINE, LANES)], [(4, 80, LANES)], fixed, old_left, old_right
    )
    left, right = shifted(own, "gx", 1), shifted(own, "gx", -1)
    newer, up, down = call(
        second_kernel,
        [(512, LANES), (288, LANES), (288, LANES)],
        [(6, 80, LANES)],
        own,
        left,
        right,
        fixed,
        old_left,
        old_right,
        speeds,
    )
    newer_left, newer_right = shifted(up, "gx", 1), shifted(down, "gx", -1)
    result = call(
        third_kernel,
        [(64, LANES)],
        [(8, 80, LANES), (8, 80, LANES), (6, FINE, LANES), (4, 80, LANES), (4, 2 * FINE, LANES)],
        newer,
        newer_left,
        newer_right,
        own,
        left,
        right,
        fixed,
        old_left,
        old_right,
        speeds,
    )
    keep, send = call(
        sort_kernel, [(64, LANES), (64, LANES)], [], group, result, crossed(result, 1), scalars=1
    )
    return call(merge_kernel, [(FLOW, 2, LANES)], [], group, keep, crossed(send, 2), scalars=1, last=True)[None]


def solution(mesh):
    placed = (
        P("grp", None, "gx", "gy"),
        P("grp", None, "gx", "gy"),
        P(None, "gx", "gy"),
        P("gx", "gy"),
    )
    return jax.shard_map(
        on_device, mesh=mesh, in_specs=placed, out_specs=P("grp", None, "gx", "gy"), check_vma=False
    )
```

```python
import jax
import jax.numpy as jnp
from jax import lax
from jax.experimental import pallas as pl
from jax.experimental.pallas import tpu as pltpu
from jax.sharding import PartitionSpec as P


LANES = 128
FINE = 64
FLOW = 32
SLOT = 40
LEVEL = 64
SHRINK = 0.25
WENO_EPS = 1e-06 * SHRINK * SHRINK
STEP_FINE = 0.3
STEP_FLOW = 0.2
SURFACE = 6.0
SPREAD = 1.5
IMPLICIT = 0.5
F32 = jnp.float32


def lane_ids(rows):
    return lax.broadcasted_iota(jnp.int32, (rows, LANES), 1)


def roll_lanes(value, shift):
    return pltpu.roll(value, shift % LANES, 1)


def exact_dot(left, right):
    return jnp.dot(left, right, precision=lax.Precision.HIGHEST, preferred_element_type=F32)


def chunk(index):
    return pl.multiple_of(index * 8, 8)


def pack_kernel(flow_ref, level_ref, band_ref, nozzle_ref, raw_ref, mark_ref):
    for row in range(2):
        raw_ref[row * FLOW : (row + 1) * FLOW, :] = flow_ref[:, row, :]
    for row in range(4):
        block = level_ref[:, row, :] * SHRINK
        raw_ref[LEVEL + row * FINE : LEVEL + (row + 1) * FINE, :] = block[:, :LANES]
        raw_ref[LEVEL + (row + 4) * FINE : LEVEL + (row + 5) * FINE, :] = block[:, LANES:]
    spread_tiles = jnp.where(
        lax.broadcasted_iota(jnp.int32, (16, 256), 1) // 16 == lax.broadcasted_iota(jnp.int32, (16, 256), 0), 1.0, 0.0
    )
    flags = exact_dot(band_ref[...].astype(F32), spread_tiles)
    phases = nozzle_ref[...].astype(F32)
    for half in range(2):
        part = slice(half * LANES, (half + 1) * LANES)
        mark_ref[half, 0:8, :] = flags[:, part]
        mark_ref[half, 8:12, :] = phases[:, part]
        mark_ref[half, 12:16, :] = jnp.zeros((4, LANES), F32)


def level_rows(ref, tile, row):
    at = LEVEL + (4 * tile + row) * FINE
    return ref[at : at + FINE, :]


def split_kernel(group_ref, raw_ref, other_ref, mark_ref, half_ref, edge_ref):
    group = group_ref[0]
    lanes = lane_ids(FINE)
    half_ref[0:64, :] = raw_ref[0:64, :]

    for core in range(2):
        level, (lower, upper) = (
            (raw_ref, (other_ref, raw_ref)) if core else (other_ref, (raw_ref, other_ref))
        )

        @pl.when(group % 2 == core)
        def _(core=core, level=level, lower=lower, upper=upper):
            for row in range(2):
                half_ref[64 + row * FINE : 64 + (row + 1) * FINE, :] = level_rows(level, 0, 2 * core + row)
            beyond = level_rows(level, 1, 0)
            for row in range(1, 4):
                beyond = jnp.where(lanes < 16 * row, beyond, roll_lanes(level_rows(level, 1, row), 16 * row))
            half_ref[192:256, :] = beyond

            def edges(tile, level_start, field_start):
                packed = roll_lanes(level_rows(level, tile, 0), -level_start)
                for row in range(1, 4):
                    turned = roll_lanes(level_rows(level, tile, row), 16 * row - level_start)
                    packed = jnp.where(lanes < 16 * row, packed, turned)
                packed = jnp.where(lanes < 64, packed, roll_lanes(lower[0:64, :], 64 - field_start))
                packed = jnp.where(lanes < 72, packed, roll_lanes(upper[0:64, :], 72 - field_start))
                edge_ref[0:64, :] = packed
                edge_ref[64:80, :] = mark_ref[tile]

            ahead = jnp.logical_or(group == 0, group == 3)

            @pl.when(ahead)
            def _():
                edges(1, 112, 120)

            @pl.when(jnp.logical_not(ahead))
            def _():
                edges(0, 0, 0)


def join_kernel(half_ref, edge_ref, out_ref):
    out_ref[0:256, :] = half_ref[...]
    out_ref[256:336, :] = edge_ref[...]


def assemble_kernel(
    group_ref, raw_ref, other_ref, mark_ref, half_ref, far_half_ref, fixed_ref, up_ref, down_ref
):
    group = group_ref[0]
    lanes = lane_ids(64)

    def assemble(own):
        core, first, last = own % 2, own == 0, own == 3
        local = (raw_ref, other_ref) if core == 0 else (other_ref, raw_ref)
        remote = (half_ref, far_half_ref) if core == 0 else (far_half_ref, half_ref)
        fields = [ref[0:64, :] for ref in ((*local, *remote) if own < 2 else (*remote, *local))]
        near, far = half_ref[256:320, :], far_half_ref[256:320, :]

        def placed(index, lane):
            value = roll_lanes(fields[index], lane + 4 - 32 * own)
            edge = (near, near, far, far)[index]
            source = 64 + 8 * (index % 2)
            if first:
                value = jnp.where(lanes < lane + 4, roll_lanes(edge, lane - source - 4), value)
            if last:
                value = jnp.where(lanes >= lane + 36, roll_lanes(edge, lane + 36 - source), value)
            return value

        parts = [placed(index, SLOT * index) for index in range(3)]
        moving = by_slot(lanes, *parts)
        pressure = placed(3, 0)
        fixed_ref[0:64, :] = moving
        fixed_ref[64:128, :] = pressure
        for row in range(4):
            if own < 2:
                low = remote[row // 2][64 + (row % 2) * FINE : 64 + (row % 2 + 1) * FINE, :]
                high = roll_lanes(far_half_ref[192:256, :] if core == 0 else half_ref[192:256, :], -16 * row)
            else:
                level = raw_ref if core else other_ref
                low, high = level_rows(level, 0, row), level_rows(level, 1, row)
            value = {
                0: lambda: jnp.where(lanes < 32, roll_lanes(far, 16 - 16 * row), roll_lanes(low, 32)),
                1: lambda: roll_lanes(jnp.where(lanes < 32, high, low), 96),
                2: lambda: roll_lanes(jnp.where(lanes < 96, high, low), 32),
                3: lambda: jnp.where(lanes < 96, roll_lanes(high, 96), roll_lanes(far, 96 - 16 * row)),
            }[own]()
            fixed_ref[128 + row * FINE : 128 + (row + 1) * FINE, :] = value
            if row < 3:
                down_ref[row * FINE : (row + 1) * FINE, :] = value
            if row > 0:
                up_ref[(row - 1) * FINE : row * FINE, :] = value
        low, high, beside, few = mark_ref[0], mark_ref[1], half_ref[320:336, :], lane_ids(16)
        marks = {
            0: lambda: roll_lanes(jnp.where(few < 96, low, beside), 32),
            1: lambda: roll_lanes(jnp.where(few < 32, high, low), 96),
            2: lambda: roll_lanes(jnp.where(few < 96, high, low), 32),
            3: lambda: roll_lanes(jnp.where(few < 32, beside, high), 96),
        }[own]()
        fixed_ref[384:400, :] = marks
        for out_ref, row in ((up_ref, 1), (down_ref, 0)):
            out_ref[192:224, :] = moving[row * FLOW : (row + 1) * FLOW, :]
            out_ref[224:256, :] = pressure[row * FLOW : (row + 1) * FLOW, :]
            out_ref[256:272, :] = marks

    for own in range(4):

        @pl.when(group == own)
        def _(own=own):
            assemble(own)


def bent(below, here, above):
    return (above - here) - (here - below)


def mixed(smooth_one, smooth_two, smooth_three, curve_one, curve_two, curve_three):
    both_three = smooth_one * smooth_two
    both_two = smooth_one * smooth_three
    both_one = smooth_two * smooth_three
    one = both_one * both_one
    three = both_three * both_three
    bottom = (one + 6.0 * (both_two * both_two)) + 3.0 * three
    top = one * ((curve_one - curve_two) * (1.0 / 3.0)) + three * ((curve_two - curve_three) * 0.5)
    return top / bottom - curve_two * (1.0 / 6.0)


THIRDS = 4.0 / 3.0


def upwind_part(far_low, low, mid, high, far_high, slope, speed):
    ahead = speed >= 0.0
    one = jnp.where(ahead, far_low, far_high)
    two = jnp.where(ahead, low, high)
    four = jnp.where(ahead, high, low)
    curve_one = two - one
    curve_two = mid - two
    curve_three = four - mid
    smooth_one = (two * two + WENO_EPS) + curve_one * (THIRDS * curve_one + two)
    smooth_two = (two * mid + WENO_EPS) + THIRDS * (curve_two * curve_two)
    smooth_three = (mid * mid + WENO_EPS) + curve_three * (THIRDS * curve_three - mid)
    rest = mixed(smooth_one, smooth_two, smooth_three, curve_one, curve_two, curve_three)
    return speed * slope + jnp.abs(speed) * rest


def pair_terms(low, high, low_square, high_square):
    change = high - low
    wide = THIRDS * change
    rising = high_square + change * (wide + high)
    falling = low_square + change * (wide - low)
    level = (low * high + WENO_EPS) + change * wide
    return change, rising, falling, level


def upwind_pairs(one, two, three, four, slope, speed):
    ahead = speed >= 0.0
    rest = mixed(
        jnp.where(ahead, one[1], four[2]),
        jnp.where(ahead, two[3], three[3]),
        jnp.where(ahead, three[2], two[1]),
        jnp.where(ahead, one[0], four[0]),
        jnp.where(ahead, two[0], three[0]),
        jnp.where(ahead, three[0], two[0]),
    )
    return speed * (slope + rest)


def fill_wrapped(wrapped, index, source, at):
    wrapped[index, 8:72, :] = source[at : at + FINE, :]
    wrapped[index, 0:8, :] = source[at + 56 : at + 64, :]
    wrapped[index, 72:80, :] = source[at : at + 8, :]


def load(place, z):
    ref, at = place
    return ref[pl.ds(at + z, 8), :]


def speed_loader(own_ref, rim_ref, first_row):
    def speed(component, index, z):
        row = (first_row + index) // 2
        ref, at = (own_ref, row) if 0 <= row < 2 else (rim_ref, 0 if row < 0 else 1)
        return ref[component, at, pl.ds(z, 8), :]

    return speed


def across(here, wrapped, index, z, speed_y, speed_z):
    after = roll_lanes(here, -1)
    before = roll_lanes(here, 1)
    mid = bent(before, here, after)
    shifts = [roll_lanes(mid, 2), roll_lanes(mid, 1), mid, roll_lanes(mid, -1), roll_lanes(mid, -2)]
    rate = upwind_part(*shifts, (after - before) * 0.5, speed_y)
    column = [wrapped[index, pl.ds(z + 8 + offset, 8), :] for offset in range(-3, 4)]
    column[3] = here
    column_bends = [bent(column[k - 1], column[k], column[k + 1]) for k in range(1, 6)]
    return rate + upwind_part(*column_bends, (column[4] - column[2]) * 0.5, speed_z)


def across_rows(places, speed, wrapped, rate_ref):
    for index, place in enumerate(places):
        fill_wrapped(wrapped, index, *place)

    def body(step, carry):
        z = chunk(step)
        for index, place in enumerate(places):
            rate = across(load(place, z), wrapped, index, z, speed(1, index, z), speed(2, index, z))
            rate_ref[pl.ds(index * FINE + z, 8), :] = rate
        return carry

    lax.fori_loop(0, 8, body, 0)


def section(current, initial, speed, rates, wrapped, keep, blend, store):
    rows = len(rates)
    for index in range(rows):
        if rates[index] is None:
            fill_wrapped(wrapped, index, *current[index + 3])

    def body(step, carry):
        z = chunk(step)
        values = [load(place, z) for place in current]
        steps = [values[k + 1] - values[k] for k in range(rows + 5)]
        bends = [steps[k + 1] - steps[k] for k in range(rows + 4)]
        squares = [value * value + WENO_EPS for value in bends]
        pairs = {}
        for index in range(rows):
            for k in range(index, index + 4):
                if k not in pairs:
                    pairs[k] = pair_terms(bends[k], bends[k + 1], squares[k], squares[k + 1])
            here = values[index + 3]
            slope = (steps[index + 3] + steps[index + 2]) * 0.5
            rate = upwind_pairs(*(pairs[k] for k in range(index, index + 4)), slope, speed(0, index, z))
            if rates[index] is None:
                rate = rate + across(here, wrapped, index, z, speed(1, index, z), speed(2, index, z))
            else:
                rate = rate + load(rates[index], z)
            moved = blend * (here - STEP_FINE * rate)
            if keep:
                moved = moved + keep * load(initial[index], z)
            store(index, z, moved)
        return carry

    lax.fori_loop(0, 8, body, 0)


def spread_speeds(stacked, speed_ref):
    source_lane = lax.broadcasted_iota(jnp.int32, (LANES, LANES), 0)
    fine_lane = lax.broadcasted_iota(jnp.int32, (LANES, LANES), 1)
    covered = jnp.logical_and(fine_lane >= 24, fine_lane < 104)
    for component in range(3):
        pick = jnp.logical_and(source_lane == SLOT * component + fine_lane // 2 - 12, covered)
        spread = exact_dot(stacked, jnp.where(pick, 1.0, 0.0))
        for row in range(2):
            part = spread[row * FLOW : (row + 1) * FLOW, :]
            speed_ref[component, row, pl.ds(0, FLOW, stride=2), :] = part
            speed_ref[component, row, pl.ds(1, FLOW, stride=2), :] = part


def in_pairs(work):
    def body(step, carry):
        for part in range(2):
            work(pl.multiple_of(step * 16 + part * 8, 8))
        return carry

    lax.fori_loop(0, 4, body, 0)


def centred(below, above):
    return (above - below) * 0.5


def planes(value):
    return pltpu.roll(value, FLOW - 1, 0), pltpu.roll(value, 1, 0)


def by_slot(lanes, first, second, third):
    return jnp.where(lanes < SLOT, first, jnp.where(lanes < 2 * SLOT, second, third))


def sweep(below, here, above, source):
    up, down = planes(here)
    beside = below + above + roll_lanes(here, 1) + roll_lanes(here, -1) + up + down
    return (source + IMPLICIT * beside) / (1.0 + 6.0 * IMPLICIT)


def inner_kernel(fixed_ref, speed_ref, rate_ref, wrapped):
    spread_speeds(fixed_ref[0:64, :], speed_ref)
    places = [(fixed_ref, 128 + FINE * row) for row in range(4)]
    across_rows(places, speed_loader(speed_ref, None, 0), wrapped, rate_ref)


def first_kernel(fixed_ref, left_ref, right_ref, speed_ref, rate_ref, out_ref):
    moving = [
        left_ref[192:224, :],
        fixed_ref[0:32, :],
        fixed_ref[32:64, :],
        right_ref[192:224, :],
    ]
    lanes = lane_ids(FLOW)
    pressure = [
        left_ref[224:256, :],
        fixed_ref[64:96, :],
        fixed_ref[96:128, :],
        right_ref[224:256, :],
    ]
    pressure = [by_slot(lanes, p, roll_lanes(p, 40), roll_lanes(p, 80)) for p in pressure]
    for row in range(2):
        here, push = moving[row + 1], pressure[row + 1]
        back, further = roll_lanes(here, 88), roll_lanes(here, 40)
        along_x = by_slot(lanes, here, further, roll_lanes(here, 80))
        along_y = by_slot(lanes, back, here, further)
        along_z = by_slot(lanes, roll_lanes(here, 48), back, here)
        up, down = planes(here)
        push_up, push_down = planes(push)
        advect = -(
            along_x * centred(moving[row], moving[row + 2])
            + along_y * centred(roll_lanes(here, 1), roll_lanes(here, -1))
            + along_z * centred(down, up)
        )
        gradient = by_slot(
            lanes,
            centred(pressure[row], pressure[row + 2]),
            centred(roll_lanes(push, 1), roll_lanes(push, -1)),
            centred(push_down, push_up),
        )
        out_ref[256 + row * FLOW : 256 + (row + 1) * FLOW, :] = here + STEP_FLOW * (advect - gradient)

    places = (
        [(left_ref, FINE * row) for row in range(3)]
        + [(fixed_ref, 128 + FINE * row) for row in range(4)]
        + [(right_ref, FINE * row) for row in range(3)]
    )

    def store(index, z, value):
        out_ref[pl.ds(index * FINE + z, 8), :] = value

    rates = [(rate_ref, FINE * row) for row in range(4)]
    section(places, None, speed_loader(speed_ref, None, 0), rates, None, 0.0, 1.0, store)


def middle_kernel(own_ref, old_left, old_right, speed_ref, rim_ref, rate_ref, wrapped):
    spread_speeds(jnp.concatenate([old_left[192:224, :], old_right[192:224, :]], axis=0), rim_ref)
    places = [(own_ref, FINE * row) for row in range(4)]
    across_rows(places, speed_loader(speed_ref, None, 0), wrapped, rate_ref)


def second_kernel(
    own_ref, left_ref, right_ref, fixed_ref, old_left, old_right, speed_ref, rim_ref, rate_ref,
    out_ref, up_ref, down_ref, wrapped,
):
    source = [ref[256 + row * FLOW : 256 + (row + 1) * FLOW, :] for ref in (left_ref, own_ref, right_ref) for row in range(2)]
    for row in range(4):
        done = sweep(source[row], source[row + 1], source[row + 2], source[row + 1])
        out_ref[384 + row * FLOW : 384 + (row + 1) * FLOW, :] = done
        if row == 1:
            up_ref[256:288, :] = done
        if row == 2:
            down_ref[256:288, :] = done
    places = [(ref, FINE * row) for ref in (left_ref, own_ref, right_ref) for row in range(4)]
    initial = [(old_left, 128)] + [(fixed_ref, 128 + FINE * row) for row in range(4)] + [(old_right, 0)]

    def store(index, z, value):
        out_ref[pl.ds(index * FINE + z, 8), :] = value
        if index < 4:
            up_ref[pl.ds(index * FINE + z, 8), :] = value
        if index > 1:
            down_ref[pl.ds((index - 2) * FINE + z, 8), :] = value

    rates = [None] + [(rate_ref, FINE * row) for row in range(4)] + [None]
    section(places, initial, speed_loader(speed_ref, rim_ref, -1), rates, wrapped, 0.75, 0.25, store)


def late_kernel(own_ref, speed_ref, rim_ref, rate_ref, wrapped):
    places = [(own_ref, FINE * row) for row in range(6)]
    across_rows(places, speed_loader(speed_ref, rim_ref, -1), wrapped, rate_ref)


def third_kernel(
    own_ref, left_ref, right_ref, older, older_left, older_right, fixed_ref, old_left, old_right,
    speed_ref, rim_ref, rate_ref,
    out_ref, wrapped, shaped, normal_x, normal_z, summed,
):
    places = (
        [(left_ref, FINE * row) for row in range(4)]
        + [(own_ref, FINE * row) for row in range(6)]
        + [(right_ref, FINE * row) for row in range(4)]
    )
    initial = (
        [(old_left, 64), (old_left, 128)]
        + [(fixed_ref, 128 + FINE * row) for row in range(4)]
        + [(old_right, 0), (old_right, 64)]
    )
    marks = [(old_left, 256)] * 2 + [(fixed_ref, 384)] * 4 + [(old_right, 256)] * 2

    def store(index, z, value):
        ref, at = initial[index]
        mark_ref, mark_at = marks[index]
        flag = mark_ref[pl.ds(mark_at + z // 8, 1), :]
        value = jnp.where(flag > 0.5, value, ref[pl.ds(at + z, 8), :]) * (1.0 / SHRINK)
        phase = mark_ref[mark_at + 8 + (index + 2) % 4 : mark_at + 9 + (index + 2) % 4, :]
        bottom = jnp.logical_and(lax.broadcasted_iota(jnp.int32, (8, LANES), 0) == 0, z == 0)
        value = jnp.where(jnp.logical_and(bottom, phase == 2.0), SPREAD, value)
        value = jnp.where(jnp.logical_and(bottom, phase == 1.0), -SPREAD, value)
        shaped[index, pl.ds(8 + z, 8), :] = value

    rates = [None] + [(rate_ref, FINE * row) for row in range(6)] + [None]
    section(places, initial, speed_loader(speed_ref, rim_ref, -2), rates, wrapped, 1.0 / 3.0, 2.0 / 3.0, store)
    for index in range(8):
        shaped[index, 0:8, :] = shaped[index, 64:72, :]
        shaped[index, 72:80, :] = shaped[index, 8:16, :]

    def normals(z):
        middle = [shaped[k, pl.ds(8 + z, 8), :] for k in range(8)]
        for row in range(6):
            here = middle[row + 1]
            slope_x = (middle[row + 2] - middle[row]) * 0.5
            slope_y = (roll_lanes(here, -1) - roll_lanes(here, 1)) * 0.5
            slope_z = (shaped[row + 1, pl.ds(9 + z, 8), :] - shaped[row + 1, pl.ds(7 + z, 8), :]) * 0.5
            inverse = lax.rsqrt(slope_x * slope_x + slope_y * slope_y + slope_z * slope_z + 1.0)
            normal_x[row, pl.ds(z, 8), :] = slope_x * inverse
            if 0 < row < 5:
                wrapped[row, pl.ds(z, 8), :] = slope_y * inverse
                normal_z[row - 1, pl.ds(8 + z, 8), :] = slope_z * inverse

    in_pairs(normals)
    for row in range(4):
        normal_z[row, 0:8, :] = normal_z[row, 64:72, :]
        normal_z[row, 72:80, :] = normal_z[row, 8:16, :]

    def forces(z):
        for half in range(2):
            total = None
            for row in (2 * half, 2 * half + 1):
                level = shaped[row + 2, pl.ds(8 + z, 8), :]
                here_x = normal_x[row + 1, pl.ds(z, 8), :]
                here_y = wrapped[row + 1, pl.ds(z, 8), :]
                here_z = normal_z[row, pl.ds(8 + z, 8), :]
                curvature = (normal_x[row + 2, pl.ds(z, 8), :] - normal_x[row, pl.ds(z, 8), :]) * 0.5
                curvature = curvature + (roll_lanes(here_y, -1) - roll_lanes(here_y, 1)) * 0.5
                curvature = (
                    curvature + (normal_z[row, pl.ds(9 + z, 8), :] - normal_z[row, pl.ds(7 + z, 8), :]) * 0.5
                )
                delta = jnp.exp(level * level * (-1.0 / (2.0 * SPREAD * SPREAD))) * (1.0 / (SPREAD * 2.5066282746310002))
                strength = SURFACE * curvature * delta
                fraction = 0.5 + 0.5 * jnp.tanh(level * (1.0 / SPREAD))
                terms = (here_x * strength, here_y * strength, here_z * strength, fraction)
                total = terms if total is None else tuple(a + b for a, b in zip(total, terms))
            for component in range(4):
                summed[component, pl.ds(half * FINE + z, 8), :] = total[component]

    in_pairs(forces)

    source = [older_left[288:320, :], older[256:288, :], older[288:320, :], older_right[256:288, :]]
    once = [left_ref[256:288, :]] + [own_ref[384 + row * FLOW : 384 + (row + 1) * FLOW, :] for row in range(4)]
    once = once + [right_ref[256:288, :]]
    twice = [sweep(once[row], once[row + 1], once[row + 2], source[row]) for row in range(4)]
    thrice = [sweep(twice[row], twice[row + 1], twice[row + 2], source[row + 1]) for row in range(2)]

    source_lane = lax.broadcasted_iota(jnp.int32, (LANES, LANES), 0)
    out_lane = lax.broadcasted_iota(jnp.int32, (LANES, LANES), 1)
    part, column = out_lane // FLOW, out_lane % FLOW
    take = jnp.logical_and(source_lane == SLOT * part + 4 + column, part < 3)
    done = exact_dot(jnp.concatenate(thrice, axis=0), jnp.where(take, 1.0, 0.0))
    for component in range(4):
        take = jnp.logical_and((source_lane - 32) // 2 == column, part == component)
        take = jnp.logical_and(take, jnp.logical_and(source_lane >= 32, source_lane < 96))
        scale = 0.125 * STEP_FLOW if component < 3 else 0.125
        pairs = jnp.concatenate(
            [
                summed[component, pl.ds(half * FINE, FLOW, stride=2), :]
                + summed[component, pl.ds(half * FINE + 1, FLOW, stride=2), :]
                for half in range(2)
            ],
            axis=0,
        )
        done = done + exact_dot(pairs * scale, jnp.where(take, 1.0, 0.0))
    out_ref[...] = done


def sort_kernel(group_ref, own_ref, other_ref, keep_ref, send_ref):
    group = group_ref[0]
    lanes = lane_ids(64)
    beside = group + 1 - 2 * (group % 2)
    for target, out_ref in ((group, keep_ref), ((group + 2) % 4, send_ref)):
        own = pltpu.roll(own_ref[...], (32 * group - 32 * target + LANES) % LANES, 1)
        other = pltpu.roll(other_ref[...], (32 * beside - 32 * target + LANES) % LANES, 1)
        out_ref[...] = jnp.where(lanes // 32 == group, own, other)


def merge_kernel(group_ref, keep_ref, far_ref, out_ref):
    merged = jnp.where(lane_ids(64) // 64 == group_ref[0] // 2, keep_ref[...], far_ref[...])
    for row in range(2):
        out_ref[:, row, :] = merged[row * FLOW : (row + 1) * FLOW, :]


def call(kernel, outs, scratch, *args, scalars=0, outer=False, last=False):
    vmem = pl.BlockSpec(memory_space=pltpu.VMEM)
    smem = pl.BlockSpec(memory_space=pltpu.SMEM)
    shapes = [jax.ShapeDtypeStruct(shape, F32) if last else pltpu.VMEM(shape, F32) for shape in outs]
    held = list(args[scalars:])
    if not outer:
        held = [pltpu.with_memory_space_constraint(value, pltpu.VMEM) for value in held]
    return pl.pallas_call(
        kernel,
        out_shape=shapes if len(shapes) > 1 else shapes[0],
        in_specs=[smem] * scalars + [vmem] * len(held),
        out_specs=[vmem] * len(shapes) if len(shapes) > 1 else vmem,
        scratch_shapes=[pltpu.VMEM(shape, F32) for shape in scratch],
        name=kernel.__name__,
    )(*args[:scalars], *held)


def shifted(value, axis, shift):
    count = lax.axis_size(axis)
    return lax.ppermute(value, axis, [(i, (i + shift) % count) for i in range(count)])


def crossed(value, bit):
    return lax.ppermute(value, "grp", [(i, i ^ bit) for i in range(lax.axis_size("grp"))])


def to_next_blocks(value):
    blocks = lax.axis_size("gy")
    pairs = []
    for source, target, step in ((0, 0, 1), (1, 3, -1), (2, 2, -1), (3, 1, 1)):
        pairs += [(source * blocks + j, target * blocks + (j + step) % blocks) for j in range(blocks)]
    return lax.ppermute(value, ("grp", "gy"), pairs)


def on_device(flow_fields, level_set, band_tiles, nozzle_phase):
    group = lax.axis_index("grp").astype(jnp.int32)[None]
    raw, marks = call(
        pack_kernel,
        [(LEVEL + 8 * FINE, LANES), (2, 16, LANES)],
        [],
        flow_fields[0],
        level_set[0],
        band_tiles[:, 0, :],
        nozzle_phase,
        outer=True,
    )
    other = crossed(raw, 1)
    half, edge = call(split_kernel, [(256, LANES), (80, LANES)], [], group, raw, other, marks, scalars=1)
    half = call(join_kernel, [(336, LANES)], [], crossed(half, 2), to_next_blocks(edge))
    far_half = crossed(half, 1)
    fixed, up, down = call(
        assemble_kernel,
        [(400, LANES), (272, LANES), (272, LANES)],
        [],
        group,
        raw,
        other,
        marks,
        half,
        far_half,
        scalars=1,
    )
    speed_shape = (3, 2, FINE, LANES)
    old_left, old_right = shifted(up, "gx", 1), shifted(down, "gx", -1)
    speeds, rates = call(inner_kernel, [speed_shape, (256, LANES)], [(4, 80, LANES)], fixed)
    own = call(first_kernel, [(320, LANES)], [], fixed, old_left, old_right, speeds, rates)
    left, right = shifted(own, "gx", 1), shifted(own, "gx", -1)
    rim, rates = call(
        middle_kernel, [speed_shape, (256, LANES)], [(4, 80, LANES)], own, old_left, old_right, speeds
    )
    newer, up, down = call(
        second_kernel,
        [(512, LANES), (288, LANES), (288, LANES)],
        [(6, 80, LANES)],
        own,
        left,
        right,
        fixed,
        old_left,
        old_right,
        speeds,
        rim,
        rates,
    )
    newer_left, newer_right = shifted(up, "gx", 1), shifted(down, "gx", -1)
    rates = call(late_kernel, [(384, LANES)], [(6, 80, LANES)], newer, speeds, rim)
    result = call(
        third_kernel,
        [(64, LANES)],
        [(8, 80, LANES), (8, 80, LANES), (6, FINE, LANES), (4, 80, LANES), (4, 2 * FINE, LANES)],
        newer,
        newer_left,
        newer_right,
        own,
        left,
        right,
        fixed,
        old_left,
        old_right,
        speeds,
        rim,
        rates,
    )
    keep, send = call(
        sort_kernel, [(64, LANES), (64, LANES)], [], group, result, crossed(result, 1), scalars=1
    )
    return call(merge_kernel, [(FLOW, 2, LANES)], [], group, keep, crossed(send, 2), scalars=1, last=True)[None]


def solution(mesh):
    placed = (
        P("grp", None, "gx", "gy"),
        P("grp", None, "gx", "gy"),
        P(None, "gx", "gy"),
        P("gx", "gy"),
    )
    return jax.shard_map(
        on_device, mesh=mesh, in_specs=placed, out_specs=P("grp", None, "gx", "gy"), check_vma=False
    )
```

```python
import jax
import jax.numpy as jnp
from jax import lax
from jax.experimental import pallas as pl
from jax.experimental.pallas import tpu as pltpu
from jax.sharding import PartitionSpec as P


LANES = 128
FINE = 64
FLOW = 32
SLOT = 40
LEVEL = 64
SHRINK = 0.25
WENO_EPS = 1e-06 * SHRINK * SHRINK
STEP_FINE = 0.3
STEP_FLOW = 0.2
SURFACE = 6.0
SPREAD = 1.5
IMPLICIT = 0.5
F32 = jnp.float32


def lane_ids(rows):
    return lax.broadcasted_iota(jnp.int32, (rows, LANES), 1)


def roll_lanes(value, shift):
    return pltpu.roll(value, shift % LANES, 1)


def exact_dot(left, right):
    return jnp.dot(left, right, precision=lax.Precision.HIGHEST, preferred_element_type=F32)


def chunk(index):
    return pl.multiple_of(index * 8, 8)


def folded(first, second, last):
    lanes = lane_ids(FINE)
    inside = jnp.logical_and(lanes >= 24, lanes < 104)
    return jnp.where(inside, first, roll_lanes(last, 80)), jnp.where(inside, second, roll_lanes(last, 32))


def unfolded(first, second):
    return jnp.where(lane_ids(FINE) < 72, roll_lanes(first, -80), roll_lanes(second, -32))


def pack_kernel(flow_ref, level_ref, band_ref, nozzle_ref, raw_ref, mark_ref):
    for row in range(2):
        raw_ref[row * FLOW : (row + 1) * FLOW, :] = flow_ref[:, row, :]
    for row in range(4):
        block = level_ref[:, row, :] * SHRINK
        raw_ref[LEVEL + row * FINE : LEVEL + (row + 1) * FINE, :] = block[:, :LANES]
        raw_ref[LEVEL + (row + 4) * FINE : LEVEL + (row + 5) * FINE, :] = block[:, LANES:]
    spread_tiles = jnp.where(
        lax.broadcasted_iota(jnp.int32, (16, 256), 1) // 16 == lax.broadcasted_iota(jnp.int32, (16, 256), 0), 1.0, 0.0
    )
    flags = exact_dot(band_ref[...].astype(F32), spread_tiles)
    phases = nozzle_ref[...].astype(F32)
    for half in range(2):
        part = slice(half * LANES, (half + 1) * LANES)
        mark_ref[half, 0:8, :] = flags[:, part]
        mark_ref[half, 8:12, :] = phases[:, part]
        mark_ref[half, 12:16, :] = jnp.zeros((4, LANES), F32)


def level_rows(ref, tile, row):
    at = LEVEL + (4 * tile + row) * FINE
    return ref[at : at + FINE, :]


def split_kernel(group_ref, raw_ref, other_ref, mark_ref, half_ref, edge_ref):
    group = group_ref[0]
    lanes = lane_ids(FINE)
    half_ref[0:64, :] = raw_ref[0:64, :]

    for core in range(2):
        level, (lower, upper) = (
            (raw_ref, (other_ref, raw_ref)) if core else (other_ref, (raw_ref, other_ref))
        )

        @pl.when(group % 2 == core)
        def _(core=core, level=level, lower=lower, upper=upper):
            for row in range(2):
                half_ref[64 + row * FINE : 64 + (row + 1) * FINE, :] = level_rows(level, 0, 2 * core + row)
            beyond = level_rows(level, 1, 0)
            for row in range(1, 4):
                beyond = jnp.where(lanes < 16 * row, beyond, roll_lanes(level_rows(level, 1, row), 16 * row))
            half_ref[192:256, :] = beyond

            def edges(tile, level_start, field_start):
                packed = roll_lanes(level_rows(level, tile, 0), -level_start)
                for row in range(1, 4):
                    turned = roll_lanes(level_rows(level, tile, row), 16 * row - level_start)
                    packed = jnp.where(lanes < 16 * row, packed, turned)
                packed = jnp.where(lanes < 64, packed, roll_lanes(lower[0:64, :], 64 - field_start))
                packed = jnp.where(lanes < 72, packed, roll_lanes(upper[0:64, :], 72 - field_start))
                edge_ref[0:64, :] = packed
                edge_ref[64:80, :] = mark_ref[tile]

            ahead = jnp.logical_or(group == 0, group == 3)

            @pl.when(ahead)
            def _():
                edges(1, 112, 120)

            @pl.when(jnp.logical_not(ahead))
            def _():
                edges(0, 0, 0)


def join_kernel(half_ref, edge_ref, out_ref):
    out_ref[0:256, :] = half_ref[...]
    out_ref[256:336, :] = edge_ref[...]


def assemble_kernel(
    group_ref, raw_ref, other_ref, mark_ref, half_ref, far_half_ref, fixed_ref, up_ref, down_ref
):
    group = group_ref[0]
    lanes = lane_ids(64)

    def assemble(own):
        core, first, last = own % 2, own == 0, own == 3
        local = (raw_ref, other_ref) if core == 0 else (other_ref, raw_ref)
        remote = (half_ref, far_half_ref) if core == 0 else (far_half_ref, half_ref)
        fields = [ref[0:64, :] for ref in ((*local, *remote) if own < 2 else (*remote, *local))]
        near, far = half_ref[256:320, :], far_half_ref[256:320, :]

        def placed(index, lane):
            value = roll_lanes(fields[index], lane + 4 - 32 * own)
            edge = (near, near, far, far)[index]
            source = 64 + 8 * (index % 2)
            if first:
                value = jnp.where(lanes < lane + 4, roll_lanes(edge, lane - source - 4), value)
            if last:
                value = jnp.where(lanes >= lane + 36, roll_lanes(edge, lane + 36 - source), value)
            return value

        parts = [placed(index, SLOT * index) for index in range(3)]
        moving = by_slot(lanes, *parts)
        pressure = placed(3, 0)
        fixed_ref[0:64, :] = moving
        fixed_ref[64:128, :] = pressure
        level_tiles = []
        for row in range(4):
            if own < 2:
                low = remote[row // 2][64 + (row % 2) * FINE : 64 + (row % 2 + 1) * FINE, :]
                high = roll_lanes(far_half_ref[192:256, :] if core == 0 else half_ref[192:256, :], -16 * row)
            else:
                level = raw_ref if core else other_ref
                low, high = level_rows(level, 0, row), level_rows(level, 1, row)
            value = {
                0: lambda: jnp.where(lanes < 32, roll_lanes(far, 16 - 16 * row), roll_lanes(low, 32)),
                1: lambda: roll_lanes(jnp.where(lanes < 32, high, low), 96),
                2: lambda: roll_lanes(jnp.where(lanes < 96, high, low), 32),
                3: lambda: jnp.where(lanes < 96, roll_lanes(high, 96), roll_lanes(far, 96 - 16 * row)),
            }[own]()
            fixed_ref[128 + row * FINE : 128 + (row + 1) * FINE, :] = value
            level_tiles.append(value)
        for out_ref, (near, next_row, far_row) in ((up_ref, (2, 3, 1)), (down_ref, (0, 1, 2))):
            pair = folded(level_tiles[near], level_tiles[next_row], level_tiles[far_row])
            out_ref[0:64, :], out_ref[64:128, :] = pair
        low, high, beside, few = mark_ref[0], mark_ref[1], half_ref[320:336, :], lane_ids(16)
        marks = {
            0: lambda: roll_lanes(jnp.where(few < 96, low, beside), 32),
            1: lambda: roll_lanes(jnp.where(few < 32, high, low), 96),
            2: lambda: roll_lanes(jnp.where(few < 96, high, low), 32),
            3: lambda: roll_lanes(jnp.where(few < 32, beside, high), 96),
        }[own]()
        fixed_ref[384:400, :] = marks
        for out_ref, row in ((up_ref, 1), (down_ref, 0)):
            out_ref[128:160, :] = moving[row * FLOW : (row + 1) * FLOW, :]
            out_ref[160:192, :] = pressure[row * FLOW : (row + 1) * FLOW, :]
            out_ref[192:208, :] = marks

    for own in range(4):

        @pl.when(group == own)
        def _(own=own):
            assemble(own)


def bent(below, here, above):
    return (above - here) - (here - below)


def mixed(smooth_one, smooth_two, smooth_three, curve_one, curve_two, curve_three):
    both_three = smooth_one * smooth_two
    both_two = smooth_one * smooth_three
    both_one = smooth_two * smooth_three
    one = both_one * both_one
    three = both_three * both_three
    bottom = (one + 6.0 * (both_two * both_two)) + 3.0 * three
    top = one * ((curve_one - curve_two) * (1.0 / 3.0)) + three * ((curve_two - curve_three) * 0.5)
    return top / bottom - curve_two * (1.0 / 6.0)


THIRDS = 4.0 / 3.0


def upwind_part(far_low, low, mid, high, far_high, slope, speed):
    ahead = speed >= 0.0
    one = jnp.where(ahead, far_low, far_high)
    two = jnp.where(ahead, low, high)
    four = jnp.where(ahead, high, low)
    curve_one = two - one
    curve_two = mid - two
    curve_three = four - mid
    smooth_one = (two * two + WENO_EPS) + curve_one * (THIRDS * curve_one + two)
    smooth_two = (two * mid + WENO_EPS) + THIRDS * (curve_two * curve_two)
    smooth_three = (mid * mid + WENO_EPS) + curve_three * (THIRDS * curve_three - mid)
    rest = mixed(smooth_one, smooth_two, smooth_three, curve_one, curve_two, curve_three)
    return speed * slope + jnp.abs(speed) * rest


def pair_terms(low, high, low_square, high_square):
    change = high - low
    wide = THIRDS * change
    rising = high_square + change * (wide + high)
    falling = low_square + change * (wide - low)
    level = (low * high + WENO_EPS) + change * wide
    return change, rising, falling, level


def upwind_pairs(one, two, three, four, slope, speed):
    ahead = speed >= 0.0
    rest = mixed(
        jnp.where(ahead, one[1], four[2]),
        jnp.where(ahead, two[3], three[3]),
        jnp.where(ahead, three[2], two[1]),
        jnp.where(ahead, one[0], four[0]),
        jnp.where(ahead, two[0], three[0]),
        jnp.where(ahead, three[0], two[0]),
    )
    return speed * (slope + rest)


def fill_wrapped(wrapped, index, source, at):
    wrapped[index, 8:72, :] = source[at : at + FINE, :]
    wrapped[index, 0:8, :] = source[at + 56 : at + 64, :]
    wrapped[index, 72:80, :] = source[at : at + 8, :]


def load(place, z):
    ref, at = place
    return ref[pl.ds(at + z, 8), :]


def speed_loader(own_ref, rim_ref, first_row):
    def speed(component, index, z):
        row = (first_row + index) // 2
        ref, at = (own_ref, row) if 0 <= row < 2 else (rim_ref, 0 if row < 0 else 1)
        return ref[component, at, pl.ds(z, 8), :]

    return speed


def across(here, wrapped, index, z, speed_y, speed_z):
    after = roll_lanes(here, -1)
    before = roll_lanes(here, 1)
    mid = bent(before, here, after)
    shifts = [roll_lanes(mid, 2), roll_lanes(mid, 1), mid, roll_lanes(mid, -1), roll_lanes(mid, -2)]
    rate = upwind_part(*shifts, (after - before) * 0.5, speed_y)
    column = [wrapped[index, pl.ds(z + 8 + offset, 8), :] for offset in range(-3, 4)]
    column[3] = here
    column_bends = [bent(column[k - 1], column[k], column[k + 1]) for k in range(1, 6)]
    return rate + upwind_part(*column_bends, (column[4] - column[2]) * 0.5, speed_z)


def across_rows(places, speed, wrapped, rate_ref):
    for index, place in enumerate(places):
        fill_wrapped(wrapped, index, *place)

    def body(step, carry):
        z = chunk(step)
        for index, place in enumerate(places):
            rate = across(load(place, z), wrapped, index, z, speed(1, index, z), speed(2, index, z))
            rate_ref[pl.ds(index * FINE + z, 8), :] = rate
        return carry

    lax.fori_loop(0, 8, body, 0)


def section(current, initial, speed, rates, wrapped, keep, blend, store):
    rows = len(rates)
    for index in range(rows):
        if rates[index] is None:
            fill_wrapped(wrapped, index, *current[index + 3])

    def body(step, carry):
        z = chunk(step)
        values = [load(place, z) for place in current]
        steps = [values[k + 1] - values[k] for k in range(rows + 5)]
        bends = [steps[k + 1] - steps[k] for k in range(rows + 4)]
        squares = [value * value + WENO_EPS for value in bends]
        pairs = {}
        for index in range(rows):
            for k in range(index, index + 4):
                if k not in pairs:
                    pairs[k] = pair_terms(bends[k], bends[k + 1], squares[k], squares[k + 1])
            here = values[index + 3]
            slope = (steps[index + 3] + steps[index + 2]) * 0.5
            rate = upwind_pairs(*(pairs[k] for k in range(index, index + 4)), slope, speed(0, index, z))
            if rates[index] is None:
                rate = rate + across(here, wrapped, index, z, speed(1, index, z), speed(2, index, z))
            else:
                rate = rate + load(rates[index], z)
            moved = blend * (here - STEP_FINE * rate)
            if keep:
                moved = moved + keep * load(initial[index], z)
            store(index, z, moved)
        return carry

    lax.fori_loop(0, 8, body, 0)


def spread_speeds(stacked, speed_ref):
    source_lane = lax.broadcasted_iota(jnp.int32, (LANES, LANES), 0)
    fine_lane = lax.broadcasted_iota(jnp.int32, (LANES, LANES), 1)
    covered = jnp.logical_and(fine_lane >= 24, fine_lane < 104)
    for component in range(3):
        pick = jnp.logical_and(source_lane == SLOT * component + fine_lane // 2 - 12, covered)
        spread = exact_dot(stacked, jnp.where(pick, 1.0, 0.0))
        for row in range(2):
            part = spread[row * FLOW : (row + 1) * FLOW, :]
            speed_ref[component, row, pl.ds(0, FLOW, stride=2), :] = part
            speed_ref[component, row, pl.ds(1, FLOW, stride=2), :] = part


def in_pairs(work):
    def body(step, carry):
        for part in range(2):
            work(pl.multiple_of(step * 16 + part * 8, 8))
        return carry

    lax.fori_loop(0, 4, body, 0)


def centred(below, above):
    return (above - below) * 0.5


def planes(value):
    return pltpu.roll(value, FLOW - 1, 0), pltpu.roll(value, 1, 0)


def by_slot(lanes, first, second, third):
    return jnp.where(lanes < SLOT, first, jnp.where(lanes < 2 * SLOT, second, third))


def sweep(below, here, above, source):
    up, down = planes(here)
    beside = below + above + roll_lanes(here, 1) + roll_lanes(here, -1) + up + down
    return (source + IMPLICIT * beside) / (1.0 + 6.0 * IMPLICIT)


def inner_kernel(fixed_ref, speed_ref, rate_ref, wrapped):
    spread_speeds(fixed_ref[0:64, :], speed_ref)
    places = [(fixed_ref, 128 + FINE * row) for row in range(4)]
    across_rows(places, speed_loader(speed_ref, None, 0), wrapped, rate_ref)


def first_kernel(fixed_ref, left_ref, right_ref, speed_ref, rate_ref, out_ref, send_ref, spare):
    moving = [
        left_ref[128:160, :],
        fixed_ref[0:32, :],
        fixed_ref[32:64, :],
        right_ref[128:160, :],
    ]
    lanes = lane_ids(FLOW)
    pressure = [
        left_ref[160:192, :],
        fixed_ref[64:96, :],
        fixed_ref[96:128, :],
        right_ref[160:192, :],
    ]
    pressure = [by_slot(lanes, p, roll_lanes(p, 40), roll_lanes(p, 80)) for p in pressure]
    for row in range(2):
        here, push = moving[row + 1], pressure[row + 1]
        back, further = roll_lanes(here, 88), roll_lanes(here, 40)
        along_x = by_slot(lanes, here, further, roll_lanes(here, 80))
        along_y = by_slot(lanes, back, here, further)
        along_z = by_slot(lanes, roll_lanes(here, 48), back, here)
        up, down = planes(here)
        push_up, push_down = planes(push)
        advect = -(
            along_x * centred(moving[row], moving[row + 2])
            + along_y * centred(roll_lanes(here, 1), roll_lanes(here, -1))
            + along_z * centred(down, up)
        )
        gradient = by_slot(
            lanes,
            centred(pressure[row], pressure[row + 2]),
            centred(roll_lanes(push, 1), roll_lanes(push, -1)),
            centred(push_down, push_up),
        )
        pushed = here + STEP_FLOW * (advect - gradient)
        out_ref[256 + row * FLOW : 256 + (row + 1) * FLOW, :] = pushed
        send_ref[192 + row * FLOW : 192 + (row + 1) * FLOW, :] = pushed

    spare[0:64, :] = unfolded(left_ref[0:64, :], left_ref[64:128, :])
    spare[64:128, :] = unfolded(right_ref[0:64, :], right_ref[64:128, :])
    places = (
        [(spare, 0), (left_ref, 0), (left_ref, 64)]
        + [(fixed_ref, 128 + FINE * row) for row in range(4)]
        + [(right_ref, 0), (right_ref, 64), (spare, 64)]
    )

    def store(index, z, value):
        out_ref[pl.ds(index * FINE + z, 8), :] = value

    rates = [(rate_ref, FINE * row) for row in range(4)]
    section(places, None, speed_loader(speed_ref, None, 0), rates, None, 0.0, 1.0, store)
    send_ref[0:64, :], send_ref[64:128, :] = folded(out_ref[0:64, :], out_ref[64:128, :], out_ref[192:256, :])
    send_ref[128:192, :] = out_ref[128:192, :]


def middle_kernel(own_ref, old_left, old_right, speed_ref, rim_ref, rate_ref, wrapped):
    spread_speeds(jnp.concatenate([old_left[128:160, :], old_right[128:160, :]], axis=0), rim_ref)
    places = [(own_ref, FINE * row) for row in range(4)]
    across_rows(places, speed_loader(speed_ref, None, 0), wrapped, rate_ref)


def second_kernel(
    own_ref, left_ref, right_ref, fixed_ref, old_left, old_right, speed_ref, rim_ref, rate_ref,
    out_ref, up_ref, down_ref, wrapped, spare,
):
    ends = ((left_ref, 192), (own_ref, 256), (right_ref, 192))
    source = [ref[at + row * FLOW : at + (row + 1) * FLOW, :] for ref, at in ends for row in range(2)]
    for row in range(4):
        done = sweep(source[row], source[row + 1], source[row + 2], source[row + 1])
        out_ref[384 + row * FLOW : 384 + (row + 1) * FLOW, :] = done
        if row == 1:
            up_ref[192:224, :] = done
        if row == 2:
            down_ref[192:224, :] = done
    spare[0:64, :] = unfolded(left_ref[0:64, :], left_ref[64:128, :])
    spare[64:128, :] = unfolded(right_ref[0:64, :], right_ref[64:128, :])
    places = (
        [(left_ref, FINE * row) for row in range(3)]
        + [(spare, 0)]
        + [(own_ref, FINE * row) for row in range(4)]
        + [(right_ref, FINE * row) for row in range(3)]
        + [(spare, 64)]
    )
    initial = [(old_left, 64)] + [(fixed_ref, 128 + FINE * row) for row in range(4)] + [(old_right, 0)]

    def store(index, z, value):
        out_ref[pl.ds(index * FINE + z, 8), :] = value

    rates = [None] + [(rate_ref, FINE * row) for row in range(4)] + [None]
    section(places, initial, speed_loader(speed_ref, rim_ref, -1), rates, wrapped, 0.75, 0.25, store)
    for to_ref, at in ((up_ref, 0), (down_ref, 128)):
        last = out_ref[at + 192 : at + 256, :]
        to_ref[0:64, :], to_ref[64:128, :] = folded(out_ref[at : at + 64, :], out_ref[at + 64 : at + 128, :], last)
        to_ref[128:192, :] = out_ref[at + 128 : at + 192, :]


def late_kernel(own_ref, speed_ref, rim_ref, rate_ref, wrapped):
    places = [(own_ref, FINE * row) for row in range(6)]
    across_rows(places, speed_loader(speed_ref, rim_ref, -1), wrapped, rate_ref)


def third_kernel(
    own_ref, left_ref, right_ref, older, older_left, older_right, fixed_ref, old_left, old_right,
    speed_ref, rim_ref, rate_ref,
    out_ref, wrapped, shaped, normal_x, normal_z, summed, spare,
):
    spare[0:64, :] = unfolded(left_ref[0:64, :], left_ref[64:128, :])
    spare[64:128, :] = unfolded(right_ref[0:64, :], right_ref[64:128, :])
    places = (
        [(left_ref, FINE * row) for row in range(3)]
        + [(spare, 0)]
        + [(own_ref, FINE * row) for row in range(6)]
        + [(right_ref, FINE * row) for row in range(3)]
        + [(spare, 64)]
    )
    initial = (
        [(old_left, 0), (old_left, 64)]
        + [(fixed_ref, 128 + FINE * row) for row in range(4)]
        + [(old_right, 0), (old_right, 64)]
    )
    marks = [(old_left, 192)] * 2 + [(fixed_ref, 384)] * 4 + [(old_right, 192)] * 2

    def store(index, z, value):
        ref, at = initial[index]
        mark_ref, mark_at = marks[index]
        flag = mark_ref[pl.ds(mark_at + z // 8, 1), :]
        value = jnp.where(flag > 0.5, value, ref[pl.ds(at + z, 8), :]) * (1.0 / SHRINK)
        shaped[index, pl.ds(8 + z, 8), :] = value

    rates = [None] + [(rate_ref, FINE * row) for row in range(6)] + [None]
    section(places, initial, speed_loader(speed_ref, rim_ref, -2), rates, wrapped, 1.0 / 3.0, 2.0 / 3.0, store)
    for index, (mark_ref, mark_at) in enumerate(marks):
        at = mark_at + 8 + (index + 2) % 4
        phase = mark_ref[at : at + 1, :]
        inflow = jnp.where(phase == 2.0, SPREAD, jnp.where(phase == 1.0, -SPREAD, shaped[index, 8:9, :]))
        shaped[index, 8:9, :] = inflow
        shaped[index, 0:8, :] = shaped[index, 64:72, :]
        shaped[index, 72:80, :] = shaped[index, 8:16, :]

    def normals(z):
        middle = [shaped[k, pl.ds(8 + z, 8), :] for k in range(8)]
        for row in range(6):
            here = middle[row + 1]
            slope_x = (middle[row + 2] - middle[row]) * 0.5
            slope_y = (roll_lanes(here, -1) - roll_lanes(here, 1)) * 0.5
            slope_z = (shaped[row + 1, pl.ds(9 + z, 8), :] - shaped[row + 1, pl.ds(7 + z, 8), :]) * 0.5
            inverse = lax.rsqrt(slope_x * slope_x + slope_y * slope_y + slope_z * slope_z + 1.0)
            normal_x[row, pl.ds(z, 8), :] = slope_x * inverse
            if 0 < row < 5:
                wrapped[row, pl.ds(z, 8), :] = slope_y * inverse
                normal_z[row - 1, pl.ds(8 + z, 8), :] = slope_z * inverse

    in_pairs(normals)
    for row in range(4):
        normal_z[row, 0:8, :] = normal_z[row, 64:72, :]
        normal_z[row, 72:80, :] = normal_z[row, 8:16, :]

    def forces(z):
        for half in range(2):
            total = None
            for row in (2 * half, 2 * half + 1):
                level = shaped[row + 2, pl.ds(8 + z, 8), :]
                here_x = normal_x[row + 1, pl.ds(z, 8), :]
                here_y = wrapped[row + 1, pl.ds(z, 8), :]
                here_z = normal_z[row, pl.ds(8 + z, 8), :]
                curvature = (normal_x[row + 2, pl.ds(z, 8), :] - normal_x[row, pl.ds(z, 8), :]) * 0.5
                curvature = curvature + (roll_lanes(here_y, -1) - roll_lanes(here_y, 1)) * 0.5
                curvature = (
                    curvature + (normal_z[row, pl.ds(9 + z, 8), :] - normal_z[row, pl.ds(7 + z, 8), :]) * 0.5
                )
                delta = jnp.exp(level * level * (-1.0 / (2.0 * SPREAD * SPREAD))) * (1.0 / (SPREAD * 2.5066282746310002))
                strength = SURFACE * curvature * delta
                fraction = 0.5 + 0.5 * jnp.tanh(level * (1.0 / SPREAD))
                terms = (here_x * strength, here_y * strength, here_z * strength, fraction)
                total = terms if total is None else tuple(a + b for a, b in zip(total, terms))
            for component in range(4):
                summed[component, pl.ds(half * FINE + z, 8), :] = total[component]

    in_pairs(forces)

    source = [older_left[224:256, :], older[256:288, :], older[288:320, :], older_right[192:224, :]]
    once = [left_ref[192:224, :]] + [own_ref[384 + row * FLOW : 384 + (row + 1) * FLOW, :] for row in range(4)]
    once = once + [right_ref[192:224, :]]
    twice = [sweep(once[row], once[row + 1], once[row + 2], source[row]) for row in range(4)]
    thrice = [sweep(twice[row], twice[row + 1], twice[row + 2], source[row + 1]) for row in range(2)]

    source_lane = lax.broadcasted_iota(jnp.int32, (LANES, LANES), 0)
    out_lane = lax.broadcasted_iota(jnp.int32, (LANES, LANES), 1)
    part, column = out_lane // FLOW, out_lane % FLOW
    take = jnp.logical_and(source_lane == SLOT * part + 4 + column, part < 3)
    done = exact_dot(jnp.concatenate(thrice, axis=0), jnp.where(take, 1.0, 0.0))
    for component in range(4):
        take = jnp.logical_and((source_lane - 32) // 2 == column, part == component)
        take = jnp.logical_and(take, jnp.logical_and(source_lane >= 32, source_lane < 96))
        scale = 0.125 * STEP_FLOW if component < 3 else 0.125
        pairs = jnp.concatenate(
            [
                summed[component, pl.ds(half * FINE, FLOW, stride=2), :]
                + summed[component, pl.ds(half * FINE + 1, FLOW, stride=2), :]
                for half in range(2)
            ],
            axis=0,
        )
        done = done + exact_dot(pairs * scale, jnp.where(take, 1.0, 0.0))
    out_ref[...] = done


def sort_kernel(group_ref, own_ref, other_ref, keep_ref, send_ref):
    group = group_ref[0]
    lanes = lane_ids(64)
    beside = group + 1 - 2 * (group % 2)
    for target, out_ref in ((group, keep_ref), ((group + 2) % 4, send_ref)):
        own = pltpu.roll(own_ref[...], (32 * group - 32 * target + LANES) % LANES, 1)
        other = pltpu.roll(other_ref[...], (32 * beside - 32 * target + LANES) % LANES, 1)
        out_ref[...] = jnp.where(lanes // 32 == group, own, other)


def merge_kernel(group_ref, keep_ref, far_ref, out_ref):
    merged = jnp.where(lane_ids(64) // 64 == group_ref[0] // 2, keep_ref[...], far_ref[...])
    for row in range(2):
        out_ref[:, row, :] = merged[row * FLOW : (row + 1) * FLOW, :]


def call(kernel, outs, scratch, *args, scalars=0, outer=False, last=False):
    vmem = pl.BlockSpec(memory_space=pltpu.VMEM)
    smem = pl.BlockSpec(memory_space=pltpu.SMEM)
    shapes = [jax.ShapeDtypeStruct(shape, F32) if last else pltpu.VMEM(shape, F32) for shape in outs]
    held = list(args[scalars:])
    if not outer:
        held = [pltpu.with_memory_space_constraint(value, pltpu.VMEM) for value in held]
    return pl.pallas_call(
        kernel,
        out_shape=shapes if len(shapes) > 1 else shapes[0],
        in_specs=[smem] * scalars + [vmem] * len(held),
        out_specs=[vmem] * len(shapes) if len(shapes) > 1 else vmem,
        scratch_shapes=[pltpu.VMEM(shape, F32) for shape in scratch],
        name=kernel.__name__,
    )(*args[:scalars], *held)


def shifted(value, axis, shift):
    count = lax.axis_size(axis)
    return lax.ppermute(value, axis, [(i, (i + shift) % count) for i in range(count)])


def crossed(value, bit):
    return lax.ppermute(value, "grp", [(i, i ^ bit) for i in range(lax.axis_size("grp"))])


def to_next_blocks(value):
    blocks = lax.axis_size("gy")
    pairs = []
    for source, target, step in ((0, 0, 1), (1, 3, -1), (2, 2, -1), (3, 1, 1)):
        pairs += [(source * blocks + j, target * blocks + (j + step) % blocks) for j in range(blocks)]
    return lax.ppermute(value, ("grp", "gy"), pairs)


def on_device(flow_fields, level_set, band_tiles, nozzle_phase):
    group = lax.axis_index("grp").astype(jnp.int32)[None]
    raw, marks = call(
        pack_kernel,
        [(LEVEL + 8 * FINE, LANES), (2, 16, LANES)],
        [],
        flow_fields[0],
        level_set[0],
        band_tiles[:, 0, :],
        nozzle_phase,
        outer=True,
    )
    other = crossed(raw, 1)
    half, edge = call(split_kernel, [(256, LANES), (80, LANES)], [], group, raw, other, marks, scalars=1)
    half = call(join_kernel, [(336, LANES)], [], crossed(half, 2), to_next_blocks(edge))
    far_half = crossed(half, 1)
    fixed, up, down = call(
        assemble_kernel,
        [(400, LANES), (208, LANES), (208, LANES)],
        [],
        group,
        raw,
        other,
        marks,
        half,
        far_half,
        scalars=1,
    )
    speed_shape = (3, 2, FINE, LANES)
    old_left, old_right = shifted(up, "gx", 1), shifted(down, "gx", -1)
    speeds, rates = call(inner_kernel, [speed_shape, (256, LANES)], [(4, 80, LANES)], fixed)
    own, send = call(
        first_kernel, [(320, LANES), (256, LANES)], [(128, LANES)], fixed, old_left, old_right, speeds, rates
    )
    left, right = shifted(send, "gx", 1), shifted(send, "gx", -1)
    rim, rates = call(
        middle_kernel, [speed_shape, (256, LANES)], [(4, 80, LANES)], own, old_left, old_right, speeds
    )
    newer, up, down = call(
        second_kernel,
        [(512, LANES), (224, LANES), (224, LANES)],
        [(6, 80, LANES), (128, LANES)],
        own,
        left,
        right,
        fixed,
        old_left,
        old_right,
        speeds,
        rim,
        rates,
    )
    newer_left, newer_right = shifted(up, "gx", 1), shifted(down, "gx", -1)
    rates = call(late_kernel, [(384, LANES)], [(6, 80, LANES)], newer, speeds, rim)
    result = call(
        third_kernel,
        [(64, LANES)],
        [(8, 80, LANES), (8, 80, LANES), (6, FINE, LANES), (4, 80, LANES), (4, 2 * FINE, LANES), (128, LANES)],
        newer,
        newer_left,
        newer_right,
        own,
        left,
        right,
        fixed,
        old_left,
        old_right,
        speeds,
        rim,
        rates,
    )
    keep, send = call(
        sort_kernel, [(64, LANES), (64, LANES)], [], group, result, crossed(result, 1), scalars=1
    )
    return call(merge_kernel, [(FLOW, 2, LANES)], [], group, keep, crossed(send, 2), scalars=1, last=True)[None]


def solution(mesh):
    placed = (
        P("grp", None, "gx", "gy"),
        P("grp", None, "gx", "gy"),
        P(None, "gx", "gy"),
        P("gx", "gy"),
    )
    return jax.shard_map(
        on_device, mesh=mesh, in_specs=placed, out_specs=P("grp", None, "gx", "gy"), check_vma=False
    )
```

```python
import jax
import jax.numpy as jnp
from jax import lax
from jax.experimental import pallas as pl
from jax.experimental.pallas import tpu as pltpu
from jax.sharding import PartitionSpec as P


LANES = 128
FINE = 64
FLOW = 32
SLOT = 40
LEVEL = 64
SHRINK = 0.25
WENO_EPS = 1e-06 * SHRINK * SHRINK
STEP_FINE = 0.3
STEP_FLOW = 0.2
SURFACE = 6.0
SPREAD = 1.5
IMPLICIT = 0.5
F32 = jnp.float32


def lane_ids(rows):
    return lax.broadcasted_iota(jnp.int32, (rows, LANES), 1)


def roll_lanes(value, shift):
    return pltpu.roll(value, shift % LANES, 1)


def exact_dot(left, right):
    return jnp.dot(left, right, precision=lax.Precision.HIGHEST, preferred_element_type=F32)


def chunk(index):
    return pl.multiple_of(index * 8, 8)


def folded(first, second, last):
    lanes = lane_ids(FINE)
    inside = jnp.logical_and(lanes >= 24, lanes < 104)
    return jnp.where(inside, first, roll_lanes(last, 80)), jnp.where(inside, second, roll_lanes(last, 32))


def unfolded(first, second):
    return jnp.where(lane_ids(FINE) < 72, roll_lanes(first, -80), roll_lanes(second, -32))


def lay(value, base, first, last, shift):
    lanes = lane_ids(value.shape[0])
    inside = jnp.logical_and(lanes >= first, lanes < last)
    if last > LANES:
        inside = jnp.logical_or(lanes >= first, lanes < last - LANES)
    return jnp.where(inside, roll_lanes(value, shift), base)


def parted(limits, parts):
    lanes = lane_ids(parts[0].shape[0])
    value = parts[-1]
    for limit, part in reversed(list(zip(limits, parts))):
        value = jnp.where(lanes < limit, part, value)
    return value


def sent_pressure(ref):
    return parted((16, 32), (roll_lanes(ref[64:96, :], -8), roll_lanes(ref[96:128, :], 8), roll_lanes(ref[128:160, :], -88)))


def sent_source(ref, row):
    at = row * FLOW
    rest = ref[192:224, :]
    return parted(
        (48, 64),
        (
            roll_lanes(ref[128 + at : 160 + at, :], -104),
            roll_lanes(ref[64 + at : 96 + at, :], 40),
            rest if row else roll_lanes(rest, 64),
        ),
    )


def sent_sweep(ref):
    return parted(
        (48, 96, 112),
        (
            roll_lanes(ref[128:160, :], -104),
            roll_lanes(ref[160:192, :], -56),
            roll_lanes(ref[64:96, :], -40),
            roll_lanes(ref[96:128, :], -24),
        ),
    )


def pack_kernel(flow_ref, level_ref, band_ref, nozzle_ref, raw_ref, mark_ref):
    for row in range(2):
        raw_ref[row * FLOW : (row + 1) * FLOW, :] = flow_ref[:, row, :]
    for row in range(4):
        block = level_ref[:, row, :] * SHRINK
        raw_ref[LEVEL + row * FINE : LEVEL + (row + 1) * FINE, :] = block[:, :LANES]
        raw_ref[LEVEL + (row + 4) * FINE : LEVEL + (row + 5) * FINE, :] = block[:, LANES:]
    spread_tiles = jnp.where(
        lax.broadcasted_iota(jnp.int32, (16, 256), 1) // 16 == lax.broadcasted_iota(jnp.int32, (16, 256), 0), 1.0, 0.0
    )
    flags = exact_dot(band_ref[...].astype(F32), spread_tiles)
    phases = nozzle_ref[...].astype(F32)
    for half in range(2):
        part = slice(half * LANES, (half + 1) * LANES)
        mark_ref[half, 0:8, :] = flags[:, part]
        mark_ref[half, 8:12, :] = phases[:, part]
        mark_ref[half, 12:16, :] = jnp.zeros((4, LANES), F32)


def level_rows(ref, tile, row):
    at = LEVEL + (4 * tile + row) * FINE
    return ref[at : at + FINE, :]


def split_kernel(group_ref, raw_ref, other_ref, mark_ref, half_ref, edge_ref):
    group = group_ref[0]
    lanes = lane_ids(FINE)
    half_ref[0:64, :] = raw_ref[0:64, :]

    for core in range(2):
        level, (lower, upper) = (
            (raw_ref, (other_ref, raw_ref)) if core else (other_ref, (raw_ref, other_ref))
        )

        @pl.when(group % 2 == core)
        def _(core=core, level=level, lower=lower, upper=upper):
            for row in range(2):
                half_ref[64 + row * FINE : 64 + (row + 1) * FINE, :] = level_rows(level, 0, 2 * core + row)
            beyond = level_rows(level, 1, 0)
            for row in range(1, 4):
                beyond = jnp.where(lanes < 16 * row, beyond, roll_lanes(level_rows(level, 1, row), 16 * row))
            half_ref[192:256, :] = beyond

            def edges(tile, level_start, field_start):
                packed = roll_lanes(level_rows(level, tile, 0), -level_start)
                for row in range(1, 4):
                    turned = roll_lanes(level_rows(level, tile, row), 16 * row - level_start)
                    packed = jnp.where(lanes < 16 * row, packed, turned)
                packed = jnp.where(lanes < 64, packed, roll_lanes(lower[0:64, :], 64 - field_start))
                packed = jnp.where(lanes < 72, packed, roll_lanes(upper[0:64, :], 72 - field_start))
                edge_ref[0:64, :] = packed
                edge_ref[64:80, :] = mark_ref[tile]

            ahead = jnp.logical_or(group == 0, group == 3)

            @pl.when(ahead)
            def _():
                edges(1, 112, 120)

            @pl.when(jnp.logical_not(ahead))
            def _():
                edges(0, 0, 0)


def join_kernel(half_ref, edge_ref, out_ref):
    out_ref[0:256, :] = half_ref[...]
    out_ref[256:336, :] = edge_ref[...]


def assemble_kernel(
    group_ref, raw_ref, other_ref, mark_ref, half_ref, far_half_ref, fixed_ref, up_ref, down_ref
):
    group = group_ref[0]
    lanes = lane_ids(64)

    def assemble(own):
        core, first, last = own % 2, own == 0, own == 3
        local = (raw_ref, other_ref) if core == 0 else (other_ref, raw_ref)
        remote = (half_ref, far_half_ref) if core == 0 else (far_half_ref, half_ref)
        fields = [ref[0:64, :] for ref in ((*local, *remote) if own < 2 else (*remote, *local))]
        near, far = half_ref[256:320, :], far_half_ref[256:320, :]

        def placed(index, lane):
            value = roll_lanes(fields[index], lane + 4 - 32 * own)
            edge = (near, near, far, far)[index]
            source = 64 + 8 * (index % 2)
            if first:
                value = jnp.where(lanes < lane + 4, roll_lanes(edge, lane - source - 4), value)
            if last:
                value = jnp.where(lanes >= lane + 36, roll_lanes(edge, lane + 36 - source), value)
            return value

        parts = [placed(index, SLOT * index) for index in range(3)]
        moving = by_slot(lanes, *parts)
        pressure = placed(3, 0)
        fixed_ref[0:64, :] = moving
        fixed_ref[64:128, :] = pressure
        level_tiles = []
        for row in range(4):
            if own < 2:
                low = remote[row // 2][64 + (row % 2) * FINE : 64 + (row % 2 + 1) * FINE, :]
                high = roll_lanes(far_half_ref[192:256, :] if core == 0 else half_ref[192:256, :], -16 * row)
            else:
                level = raw_ref if core else other_ref
                low, high = level_rows(level, 0, row), level_rows(level, 1, row)
            value = {
                0: lambda: jnp.where(lanes < 32, roll_lanes(far, 16 - 16 * row), roll_lanes(low, 32)),
                1: lambda: roll_lanes(jnp.where(lanes < 32, high, low), 96),
                2: lambda: roll_lanes(jnp.where(lanes < 96, high, low), 32),
                3: lambda: jnp.where(lanes < 96, roll_lanes(high, 96), roll_lanes(far, 96 - 16 * row)),
            }[own]()
            fixed_ref[128 + row * FINE : 128 + (row + 1) * FINE, :] = value
            level_tiles.append(value)
        for out_ref, (near, next_row, far_row) in ((up_ref, (2, 3, 1)), (down_ref, (0, 1, 2))):
            pair = folded(level_tiles[near], level_tiles[next_row], level_tiles[far_row])
            out_ref[0:64, :] = pair[0]
            row = 1 if near else 0
            push = pressure[row * FLOW : (row + 1) * FLOW, :]
            out_ref[64:96, :] = lay(push, pair[1][0:32, :], 8, 24, 8)
            out_ref[96:128, :] = lay(push, pair[1][32:64, :], 8, 24, -8)
            out_ref[128:160, :] = lay(push, moving[row * FLOW : (row + 1) * FLOW, :], 120, 128, 88)
        low, high, beside, few = mark_ref[0], mark_ref[1], half_ref[320:336, :], lane_ids(16)
        marks = {
            0: lambda: roll_lanes(jnp.where(few < 96, low, beside), 32),
            1: lambda: roll_lanes(jnp.where(few < 32, high, low), 96),
            2: lambda: roll_lanes(jnp.where(few < 96, high, low), 32),
            3: lambda: roll_lanes(jnp.where(few < 32, beside, high), 96),
        }[own]()
        fixed_ref[384:400, :] = marks
        for out_ref in (up_ref, down_ref):
            out_ref[160:176, :] = marks

    for own in range(4):

        @pl.when(group == own)
        def _(own=own):
            assemble(own)


def bent(below, here, above):
    return (above - here) - (here - below)


def mixed(smooth_one, smooth_two, smooth_three, curve_one, curve_two, curve_three):
    both_three = smooth_one * smooth_two
    both_two = smooth_one * smooth_three
    both_one = smooth_two * smooth_three
    one = both_one * both_one
    three = both_three * both_three
    bottom = (one + 6.0 * (both_two * both_two)) + 3.0 * three
    top = one * ((curve_one - curve_two) * (1.0 / 3.0)) + three * ((curve_two - curve_three) * 0.5)
    return top / bottom - curve_two * (1.0 / 6.0)


THIRDS = 4.0 / 3.0


def upwind_part(far_low, low, mid, high, far_high, slope, speed):
    ahead = speed >= 0.0
    one = jnp.where(ahead, far_low, far_high)
    two = jnp.where(ahead, low, high)
    four = jnp.where(ahead, high, low)
    curve_one = two - one
    curve_two = mid - two
    curve_three = four - mid
    smooth_one = (two * two + WENO_EPS) + curve_one * (THIRDS * curve_one + two)
    smooth_two = (two * mid + WENO_EPS) + THIRDS * (curve_two * curve_two)
    smooth_three = (mid * mid + WENO_EPS) + curve_three * (THIRDS * curve_three - mid)
    rest = mixed(smooth_one, smooth_two, smooth_three, curve_one, curve_two, curve_three)
    return speed * slope + jnp.abs(speed) * rest


def pair_terms(low, high, low_square, high_square):
    change = high - low
    wide = THIRDS * change
    rising = high_square + change * (wide + high)
    falling = low_square + change * (wide - low)
    level = (low * high + WENO_EPS) + change * wide
    return change, rising, falling, level


def upwind_pairs(one, two, three, four, slope, speed):
    ahead = speed >= 0.0
    rest = mixed(
        jnp.where(ahead, one[1], four[2]),
        jnp.where(ahead, two[3], three[3]),
        jnp.where(ahead, three[2], two[1]),
        jnp.where(ahead, one[0], four[0]),
        jnp.where(ahead, two[0], three[0]),
        jnp.where(ahead, three[0], two[0]),
    )
    return speed * (slope + rest)


def fill_wrapped(wrapped, index, source, at):
    wrapped[index, 8:72, :] = source[at : at + FINE, :]
    wrapped[index, 0:8, :] = source[at + 56 : at + 64, :]
    wrapped[index, 72:80, :] = source[at : at + 8, :]


def load(place, z):
    ref, at = place
    return ref[pl.ds(at + z, 8), :]


def speed_loader(own_ref, rim_ref, first_row):
    def speed(component, index, z):
        row = (first_row + index) // 2
        ref, at = (own_ref, row) if 0 <= row < 2 else (rim_ref, 0 if row < 0 else 1)
        return ref[component, at, pl.ds(z, 8), :]

    return speed


def across(here, wrapped, index, z, speed_y, speed_z):
    after = roll_lanes(here, -1)
    before = roll_lanes(here, 1)
    mid = bent(before, here, after)
    shifts = [roll_lanes(mid, 2), roll_lanes(mid, 1), mid, roll_lanes(mid, -1), roll_lanes(mid, -2)]
    rate = upwind_part(*shifts, (after - before) * 0.5, speed_y)
    column = [wrapped[index, pl.ds(z + 8 + offset, 8), :] for offset in range(-3, 4)]
    column[3] = here
    column_bends = [bent(column[k - 1], column[k], column[k + 1]) for k in range(1, 6)]
    return rate + upwind_part(*column_bends, (column[4] - column[2]) * 0.5, speed_z)


def across_rows(places, speed, wrapped, rate_ref):
    for index, place in enumerate(places):
        fill_wrapped(wrapped, index, *place)

    def body(step, carry):
        z = chunk(step)
        for index, place in enumerate(places):
            rate = across(load(place, z), wrapped, index, z, speed(1, index, z), speed(2, index, z))
            rate_ref[pl.ds(index * FINE + z, 8), :] = rate
        return carry

    lax.fori_loop(0, 8, body, 0)


def section(current, initial, speed, rates, wrapped, keep, blend, store):
    rows = len(rates)
    for index in range(rows):
        if rates[index] is None:
            fill_wrapped(wrapped, index, *current[index + 3])

    def body(step, carry):
        z = chunk(step)
        values = [load(place, z) for place in current]
        steps = [values[k + 1] - values[k] for k in range(rows + 5)]
        bends = [steps[k + 1] - steps[k] for k in range(rows + 4)]
        squares = [value * value + WENO_EPS for value in bends]
        pairs = {}
        for index in range(rows):
            for k in range(index, index + 4):
                if k not in pairs:
                    pairs[k] = pair_terms(bends[k], bends[k + 1], squares[k], squares[k + 1])
            here = values[index + 3]
            slope = (steps[index + 3] + steps[index + 2]) * 0.5
            rate = upwind_pairs(*(pairs[k] for k in range(index, index + 4)), slope, speed(0, index, z))
            if rates[index] is None:
                rate = rate + across(here, wrapped, index, z, speed(1, index, z), speed(2, index, z))
            else:
                rate = rate + load(rates[index], z)
            moved = blend * (here - STEP_FINE * rate)
            if keep:
                moved = moved + keep * load(initial[index], z)
            store(index, z, moved)
        return carry

    lax.fori_loop(0, 8, body, 0)


def spread_speeds(stacked, speed_ref):
    source_lane = lax.broadcasted_iota(jnp.int32, (LANES, LANES), 0)
    fine_lane = lax.broadcasted_iota(jnp.int32, (LANES, LANES), 1)
    covered = jnp.logical_and(fine_lane >= 24, fine_lane < 104)
    for component in range(3):
        pick = jnp.logical_and(source_lane == SLOT * component + fine_lane // 2 - 12, covered)
        spread = exact_dot(stacked, jnp.where(pick, 1.0, 0.0))
        for row in range(2):
            part = spread[row * FLOW : (row + 1) * FLOW, :]
            speed_ref[component, row, pl.ds(0, FLOW, stride=2), :] = part
            speed_ref[component, row, pl.ds(1, FLOW, stride=2), :] = part


def in_pairs(work):
    def body(step, carry):
        for part in range(2):
            work(pl.multiple_of(step * 16 + part * 8, 8))
        return carry

    lax.fori_loop(0, 4, body, 0)


def centred(below, above):
    return (above - below) * 0.5


def planes(value):
    return pltpu.roll(value, FLOW - 1, 0), pltpu.roll(value, 1, 0)


def by_slot(lanes, first, second, third):
    return jnp.where(lanes < SLOT, first, jnp.where(lanes < 2 * SLOT, second, third))


def sweep(below, here, above, source):
    up, down = planes(here)
    beside = below + above + roll_lanes(here, 1) + roll_lanes(here, -1) + up + down
    return (source + IMPLICIT * beside) / (1.0 + 6.0 * IMPLICIT)


def inner_kernel(fixed_ref, speed_ref, rate_ref, wrapped):
    spread_speeds(fixed_ref[0:64, :], speed_ref)
    places = [(fixed_ref, 128 + FINE * row) for row in range(4)]
    across_rows(places, speed_loader(speed_ref, None, 0), wrapped, rate_ref)


def first_kernel(fixed_ref, left_ref, right_ref, speed_ref, rate_ref, out_ref, send_ref, spare):
    moving = [
        left_ref[128:160, :],
        fixed_ref[0:32, :],
        fixed_ref[32:64, :],
        right_ref[128:160, :],
    ]
    lanes = lane_ids(FLOW)
    pressure = [
        sent_pressure(left_ref),
        fixed_ref[64:96, :],
        fixed_ref[96:128, :],
        sent_pressure(right_ref),
    ]
    pressure = [by_slot(lanes, p, roll_lanes(p, 40), roll_lanes(p, 80)) for p in pressure]
    for row in range(2):
        here, push = moving[row + 1], pressure[row + 1]
        back, further = roll_lanes(here, 88), roll_lanes(here, 40)
        along_x = by_slot(lanes, here, further, roll_lanes(here, 80))
        along_y = by_slot(lanes, back, here, further)
        along_z = by_slot(lanes, roll_lanes(here, 48), back, here)
        up, down = planes(here)
        push_up, push_down = planes(push)
        advect = -(
            along_x * centred(moving[row], moving[row + 2])
            + along_y * centred(roll_lanes(here, 1), roll_lanes(here, -1))
            + along_z * centred(down, up)
        )
        gradient = by_slot(
            lanes,
            centred(pressure[row], pressure[row + 2]),
            centred(roll_lanes(push, 1), roll_lanes(push, -1)),
            centred(push_down, push_up),
        )
        out_ref[256 + row * FLOW : 256 + (row + 1) * FLOW, :] = here + STEP_FLOW * (advect - gradient)

    spare[0:64, :] = unfolded(left_ref[0:64, :], left_ref[64:128, :])
    spare[64:128, :] = unfolded(right_ref[0:64, :], right_ref[64:128, :])
    places = (
        [(spare, 0), (left_ref, 0), (left_ref, 64)]
        + [(fixed_ref, 128 + FINE * row) for row in range(4)]
        + [(right_ref, 0), (right_ref, 64), (spare, 64)]
    )

    def store(index, z, value):
        out_ref[pl.ds(index * FINE + z, 8), :] = value

    rates = [(rate_ref, FINE * row) for row in range(4)]
    section(places, None, speed_loader(speed_ref, None, 0), rates, None, 0.0, 1.0, store)
    source = out_ref[256:320, :]
    send_ref[0:64, :], beside = folded(out_ref[0:64, :], out_ref[64:128, :], out_ref[192:256, :])
    send_ref[64:128, :] = lay(source, beside, 8, 24, -40)
    send_ref[128:192, :] = lay(source, out_ref[128:192, :], 104, 152, 104)
    send_ref[192:224, :] = lay(source[0:32, :], source[32:64, :], 0, 64, 64)


def middle_kernel(own_ref, old_left, old_right, speed_ref, rim_ref, rate_ref, wrapped):
    spread_speeds(jnp.concatenate([old_left[128:160, :], old_right[128:160, :]], axis=0), rim_ref)
    places = [(own_ref, FINE * row) for row in range(4)]
    across_rows(places, speed_loader(speed_ref, None, 0), wrapped, rate_ref)


def second_kernel(
    own_ref, left_ref, right_ref, fixed_ref, old_left, old_right, speed_ref, rim_ref, rate_ref,
    out_ref, up_ref, down_ref, wrapped, spare,
):
    source = [sent_source(left_ref, row) for row in range(2)]
    source += [own_ref[256 + row * FLOW : 256 + (row + 1) * FLOW, :] for row in range(2)]
    source += [sent_source(right_ref, row) for row in range(2)]
    for row in range(4):
        done = sweep(source[row], source[row + 1], source[row + 2], source[row + 1])
        out_ref[384 + row * FLOW : 384 + (row + 1) * FLOW, :] = done
    spare[0:64, :] = unfolded(left_ref[0:64, :], left_ref[64:128, :])
    spare[64:128, :] = unfolded(right_ref[0:64, :], right_ref[64:128, :])
    places = (
        [(left_ref, FINE * row) for row in range(3)]
        + [(spare, 0)]
        + [(own_ref, FINE * row) for row in range(4)]
        + [(right_ref, FINE * row) for row in range(3)]
        + [(spare, 64)]
    )
    initial = [(old_left, 64)] + [(fixed_ref, 128 + FINE * row) for row in range(4)] + [(old_right, 0)]

    def store(index, z, value):
        out_ref[pl.ds(index * FINE + z, 8), :] = value

    rates = [None] + [(rate_ref, FINE * row) for row in range(4)] + [None]
    section(places, initial, speed_loader(speed_ref, rim_ref, -1), rates, wrapped, 0.75, 0.25, store)
    for to_ref, at in ((up_ref, 0), (down_ref, 128)):
        last = out_ref[at + 192 : at + 256, :]
        to_ref[0:64, :], beside = folded(out_ref[at : at + 64, :], out_ref[at + 64 : at + 128, :], last)
        done = out_ref[448:480, :] if at else out_ref[416:448, :]
        to_ref[64:96, :] = lay(done, beside[0:32, :], 8, 24, 40)
        to_ref[96:128, :] = lay(done, beside[32:64, :], 8, 16, 24)
        to_ref[128:160, :] = lay(done, out_ref[at + 128 : at + 160, :], 104, 152, 104)
        to_ref[160:192, :] = lay(done, out_ref[at + 160 : at + 192, :], 104, 152, 56)


def late_kernel(own_ref, speed_ref, rim_ref, rate_ref, wrapped):
    places = [(own_ref, FINE * row) for row in range(6)]
    across_rows(places, speed_loader(speed_ref, rim_ref, -1), wrapped, rate_ref)


def third_kernel(
    own_ref, left_ref, right_ref, older, older_left, older_right, fixed_ref, old_left, old_right,
    speed_ref, rim_ref, rate_ref,
    out_ref, wrapped, shaped, normal_x, normal_z, summed, spare,
):
    spare[0:64, :] = unfolded(left_ref[0:64, :], left_ref[64:128, :])
    spare[64:128, :] = unfolded(right_ref[0:64, :], right_ref[64:128, :])
    places = (
        [(left_ref, FINE * row) for row in range(3)]
        + [(spare, 0)]
        + [(own_ref, FINE * row) for row in range(6)]
        + [(right_ref, FINE * row) for row in range(3)]
        + [(spare, 64)]
    )
    initial = (
        [(old_left, 0), (old_left, 64)]
        + [(fixed_ref, 128 + FINE * row) for row in range(4)]
        + [(old_right, 0), (old_right, 64)]
    )
    marks = [(old_left, 160)] * 2 + [(fixed_ref, 384)] * 4 + [(old_right, 160)] * 2

    def store(index, z, value):
        ref, at = initial[index]
        mark_ref, mark_at = marks[index]
        flag = mark_ref[pl.ds(mark_at + z // 8, 1), :]
        value = jnp.where(flag > 0.5, value, ref[pl.ds(at + z, 8), :]) * (1.0 / SHRINK)
        shaped[index, pl.ds(8 + z, 8), :] = value

    rates = [None] + [(rate_ref, FINE * row) for row in range(6)] + [None]
    section(places, initial, speed_loader(speed_ref, rim_ref, -2), rates, wrapped, 1.0 / 3.0, 2.0 / 3.0, store)
    for index, (mark_ref, mark_at) in enumerate(marks):
        at = mark_at + 8 + (index + 2) % 4
        phase = mark_ref[at : at + 1, :]
        inflow = jnp.where(phase == 2.0, SPREAD, jnp.where(phase == 1.0, -SPREAD, shaped[index, 8:9, :]))
        shaped[index, 8:9, :] = inflow
        shaped[index, 0:8, :] = shaped[index, 64:72, :]
        shaped[index, 72:80, :] = shaped[index, 8:16, :]

    def normals(z):
        middle = [shaped[k, pl.ds(8 + z, 8), :] for k in range(8)]
        for row in range(6):
            here = middle[row + 1]
            slope_x = (middle[row + 2] - middle[row]) * 0.5
            slope_y = (roll_lanes(here, -1) - roll_lanes(here, 1)) * 0.5
            slope_z = (shaped[row + 1, pl.ds(9 + z, 8), :] - shaped[row + 1, pl.ds(7 + z, 8), :]) * 0.5
            inverse = lax.rsqrt(slope_x * slope_x + slope_y * slope_y + slope_z * slope_z + 1.0)
            normal_x[row, pl.ds(z, 8), :] = slope_x * inverse
            if 0 < row < 5:
                wrapped[row, pl.ds(z, 8), :] = slope_y * inverse
                normal_z[row - 1, pl.ds(8 + z, 8), :] = slope_z * inverse

    in_pairs(normals)
    for row in range(4):
        normal_z[row, 0:8, :] = normal_z[row, 64:72, :]
        normal_z[row, 72:80, :] = normal_z[row, 8:16, :]

    def forces(z):
        for half in range(2):
            total = None
            for row in (2 * half, 2 * half + 1):
                level = shaped[row + 2, pl.ds(8 + z, 8), :]
                here_x = normal_x[row + 1, pl.ds(z, 8), :]
                here_y = wrapped[row + 1, pl.ds(z, 8), :]
                here_z = normal_z[row, pl.ds(8 + z, 8), :]
                curvature = (normal_x[row + 2, pl.ds(z, 8), :] - normal_x[row, pl.ds(z, 8), :]) * 0.5
                curvature = curvature + (roll_lanes(here_y, -1) - roll_lanes(here_y, 1)) * 0.5
                curvature = (
                    curvature + (normal_z[row, pl.ds(9 + z, 8), :] - normal_z[row, pl.ds(7 + z, 8), :]) * 0.5
                )
                delta = jnp.exp(level * level * (-1.0 / (2.0 * SPREAD * SPREAD))) * (1.0 / (SPREAD * 2.5066282746310002))
                strength = SURFACE * curvature * delta
                fraction = 0.5 + 0.5 * jnp.tanh(level * (1.0 / SPREAD))
                terms = (here_x * strength, here_y * strength, here_z * strength, fraction)
                total = terms if total is None else tuple(a + b for a, b in zip(total, terms))
            for component in range(4):
                summed[component, pl.ds(half * FINE + z, 8), :] = total[component]

    in_pairs(forces)

    source = [sent_source(older_left, 1), older[256:288, :], older[288:320, :], sent_source(older_right, 0)]
    once = [sent_sweep(left_ref)] + [own_ref[384 + row * FLOW : 384 + (row + 1) * FLOW, :] for row in range(4)]
    once = once + [sent_sweep(right_ref)]
    twice = [sweep(once[row], once[row + 1], once[row + 2], source[row]) for row in range(4)]
    thrice = [sweep(twice[row], twice[row + 1], twice[row + 2], source[row + 1]) for row in range(2)]

    source_lane = lax.broadcasted_iota(jnp.int32, (LANES, LANES), 0)
    out_lane = lax.broadcasted_iota(jnp.int32, (LANES, LANES), 1)
    part, column = out_lane // FLOW, out_lane % FLOW
    take = jnp.logical_and(source_lane == SLOT * part + 4 + column, part < 3)
    done = exact_dot(jnp.concatenate(thrice, axis=0), jnp.where(take, 1.0, 0.0))
    for component in range(4):
        take = jnp.logical_and((source_lane - 32) // 2 == column, part == component)
        take = jnp.logical_and(take, jnp.logical_and(source_lane >= 32, source_lane < 96))
        scale = 0.125 * STEP_FLOW if component < 3 else 0.125
        pairs = jnp.concatenate(
            [
                summed[component, pl.ds(half * FINE, FLOW, stride=2), :]
                + summed[component, pl.ds(half * FINE + 1, FLOW, stride=2), :]
                for half in range(2)
            ],
            axis=0,
        )
        done = done + exact_dot(pairs * scale, jnp.where(take, 1.0, 0.0))
    out_ref[...] = done


def sort_kernel(group_ref, own_ref, other_ref, keep_ref, send_ref):
    group = group_ref[0]
    lanes = lane_ids(64)
    beside = group + 1 - 2 * (group % 2)
    for target, out_ref in ((group, keep_ref), ((group + 2) % 4, send_ref)):
        own = pltpu.roll(own_ref[...], (32 * group - 32 * target + LANES) % LANES, 1)
        other = pltpu.roll(other_ref[...], (32 * beside - 32 * target + LANES) % LANES, 1)
        out_ref[...] = jnp.where(lanes // 32 == group, own, other)


def merge_kernel(group_ref, keep_ref, far_ref, out_ref):
    merged = jnp.where(lane_ids(64) // 64 == group_ref[0] // 2, keep_ref[...], far_ref[...])
    for row in range(2):
        out_ref[:, row, :] = merged[row * FLOW : (row + 1) * FLOW, :]


def call(kernel, outs, scratch, *args, scalars=0, outer=False, last=False):
    vmem = pl.BlockSpec(memory_space=pltpu.VMEM)
    smem = pl.BlockSpec(memory_space=pltpu.SMEM)
    shapes = [jax.ShapeDtypeStruct(shape, F32) if last else pltpu.VMEM(shape, F32) for shape in outs]
    held = list(args[scalars:])
    if not outer:
        held = [pltpu.with_memory_space_constraint(value, pltpu.VMEM) for value in held]
    return pl.pallas_call(
        kernel,
        out_shape=shapes if len(shapes) > 1 else shapes[0],
        in_specs=[smem] * scalars + [vmem] * len(held),
        out_specs=[vmem] * len(shapes) if len(shapes) > 1 else vmem,
        scratch_shapes=[pltpu.VMEM(shape, F32) for shape in scratch],
        name=kernel.__name__,
    )(*args[:scalars], *held)


def shifted(value, axis, shift):
    count = lax.axis_size(axis)
    return lax.ppermute(value, axis, [(i, (i + shift) % count) for i in range(count)])


def crossed(value, bit):
    return lax.ppermute(value, "grp", [(i, i ^ bit) for i in range(lax.axis_size("grp"))])


def to_next_blocks(value):
    blocks = lax.axis_size("gy")
    pairs = []
    for source, target, step in ((0, 0, 1), (1, 3, -1), (2, 2, -1), (3, 1, 1)):
        pairs += [(source * blocks + j, target * blocks + (j + step) % blocks) for j in range(blocks)]
    return lax.ppermute(value, ("grp", "gy"), pairs)


def on_device(flow_fields, level_set, band_tiles, nozzle_phase):
    group = lax.axis_index("grp").astype(jnp.int32)[None]
    raw, marks = call(
        pack_kernel,
        [(LEVEL + 8 * FINE, LANES), (2, 16, LANES)],
        [],
        flow_fields[0],
        level_set[0],
        band_tiles[:, 0, :],
        nozzle_phase,
        outer=True,
    )
    other = crossed(raw, 1)
    half, edge = call(split_kernel, [(256, LANES), (80, LANES)], [], group, raw, other, marks, scalars=1)
    half = call(join_kernel, [(336, LANES)], [], crossed(half, 2), to_next_blocks(edge))
    far_half = crossed(half, 1)
    fixed, up, down = call(
        assemble_kernel,
        [(400, LANES), (176, LANES), (176, LANES)],
        [],
        group,
        raw,
        other,
        marks,
        half,
        far_half,
        scalars=1,
    )
    speed_shape = (3, 2, FINE, LANES)
    old_left, old_right = shifted(up, "gx", 1), shifted(down, "gx", -1)
    speeds, rates = call(inner_kernel, [speed_shape, (256, LANES)], [(4, 80, LANES)], fixed)
    own, send = call(
        first_kernel, [(320, LANES), (224, LANES)], [(128, LANES)], fixed, old_left, old_right, speeds, rates
    )
    left, right = shifted(send, "gx", 1), shifted(send, "gx", -1)
    rim, rates = call(
        middle_kernel, [speed_shape, (256, LANES)], [(4, 80, LANES)], own, old_left, old_right, speeds
    )
    newer, up, down = call(
        second_kernel,
        [(512, LANES), (192, LANES), (192, LANES)],
        [(6, 80, LANES), (128, LANES)],
        own,
        left,
        right,
        fixed,
        old_left,
        old_right,
        speeds,
        rim,
        rates,
    )
    newer_left, newer_right = shifted(up, "gx", 1), shifted(down, "gx", -1)
    rates = call(late_kernel, [(384, LANES)], [(6, 80, LANES)], newer, speeds, rim)
    result = call(
        third_kernel,
        [(64, LANES)],
        [(8, 80, LANES), (8, 80, LANES), (6, FINE, LANES), (4, 80, LANES), (4, 2 * FINE, LANES), (128, LANES)],
        newer,
        newer_left,
        newer_right,
        own,
        left,
        right,
        fixed,
        old_left,
        old_right,
        speeds,
        rim,
        rates,
    )
    keep, send = call(
        sort_kernel, [(64, LANES), (64, LANES)], [], group, result, crossed(result, 1), scalars=1
    )
    return call(merge_kernel, [(FLOW, 2, LANES)], [], group, keep, crossed(send, 2), scalars=1, last=True)[None]


def solution(mesh):
    placed = (
        P("grp", None, "gx", "gy"),
        P("grp", None, "gx", "gy"),
        P(None, "gx", "gy"),
        P("gx", "gy"),
    )
    return jax.shard_map(
        on_device, mesh=mesh, in_specs=placed, out_specs=P("grp", None, "gx", "gy"), check_vma=False
    )
```

```python
import jax
import jax.numpy as jnp
from jax import lax
from jax.experimental import pallas as pl
from jax.experimental.pallas import tpu as pltpu
from jax.sharding import PartitionSpec as P


LANES = 128
FINE = 64
FLOW = 32
SLOT = 40
LEVEL = 64
SHRINK = 0.25
WENO_EPS = 1e-06 * SHRINK * SHRINK
STEP_FINE = 0.3
STEP_FLOW = 0.2
SURFACE = 6.0
SPREAD = 1.5
IMPLICIT = 0.5
F32 = jnp.float32


def lane_ids(rows):
    return lax.broadcasted_iota(jnp.int32, (rows, LANES), 1)


def roll_lanes(value, shift):
    return pltpu.roll(value, shift % LANES, 1)


def exact_dot(left, right):
    return jnp.dot(left, right, precision=lax.Precision.HIGHEST, preferred_element_type=F32)


def chunk(index):
    return pl.multiple_of(index * 8, 8)


def folded(first, second, last):
    lanes = lane_ids(FINE)
    inside = jnp.logical_and(lanes >= 24, lanes < 104)
    return jnp.where(inside, first, roll_lanes(last, 80)), jnp.where(inside, second, roll_lanes(last, 32))


def unfolded(first, second):
    return jnp.where(lane_ids(FINE) < 72, roll_lanes(first, -80), roll_lanes(second, -32))


def lay(value, base, first, last, shift):
    lanes = lane_ids(value.shape[0])
    inside = jnp.logical_and(lanes >= first, lanes < last)
    if last > LANES:
        inside = jnp.logical_or(lanes >= first, lanes < last - LANES)
    return jnp.where(inside, roll_lanes(value, shift), base)


def parted(limits, parts):
    lanes = lane_ids(parts[0].shape[0])
    value = parts[-1]
    for limit, part in reversed(list(zip(limits, parts))):
        value = jnp.where(lanes < limit, part, value)
    return value


def sent_pressure(ref):
    return parted((16, 32), (roll_lanes(ref[64:96, :], -8), roll_lanes(ref[96:128, :], 8), roll_lanes(ref[128:160, :], -88)))


def sent_source(ref, row):
    at = row * FLOW
    rest = ref[192:224, :]
    return parted(
        (48, 64),
        (
            roll_lanes(ref[128 + at : 160 + at, :], -104),
            roll_lanes(ref[64 + at : 96 + at, :], 40),
            rest if row else roll_lanes(rest, 64),
        ),
    )


def sent_sweep(ref):
    return parted(
        (48, 96, 112),
        (
            roll_lanes(ref[128:160, :], -104),
            roll_lanes(ref[160:192, :], -56),
            roll_lanes(ref[64:96, :], -40),
            roll_lanes(ref[96:128, :], -24),
        ),
    )


def by_side(place_ref, first_ref, second_ref, left_ref, right_ref):
    odd = place_ref[0] % 2 == 1

    @pl.when(odd)
    def _():
        left_ref[...] = first_ref[...]
        right_ref[...] = second_ref[...]

    @pl.when(jnp.logical_not(odd))
    def _():
        left_ref[...] = second_ref[...]
        right_ref[...] = first_ref[...]


def pack_kernel(flow_ref, level_ref, band_ref, nozzle_ref, raw_ref, mark_ref):
    for row in range(2):
        raw_ref[row * FLOW : (row + 1) * FLOW, :] = flow_ref[:, row, :]
    for row in range(4):
        block = level_ref[:, row, :] * SHRINK
        raw_ref[LEVEL + row * FINE : LEVEL + (row + 1) * FINE, :] = block[:, :LANES]
        raw_ref[LEVEL + (row + 4) * FINE : LEVEL + (row + 5) * FINE, :] = block[:, LANES:]
    spread_tiles = jnp.where(
        lax.broadcasted_iota(jnp.int32, (16, 256), 1) // 16 == lax.broadcasted_iota(jnp.int32, (16, 256), 0), 1.0, 0.0
    )
    flags = exact_dot(band_ref[...].astype(F32), spread_tiles)
    phases = nozzle_ref[...].astype(F32)
    for half in range(2):
        part = slice(half * LANES, (half + 1) * LANES)
        mark_ref[half, 0:8, :] = flags[:, part]
        mark_ref[half, 8:12, :] = phases[:, part]
        mark_ref[half, 12:16, :] = jnp.zeros((4, LANES), F32)


def level_rows(ref, tile, row):
    at = LEVEL + (4 * tile + row) * FINE
    return ref[at : at + FINE, :]


def split_kernel(group_ref, raw_ref, other_ref, mark_ref, half_ref, edge_ref):
    group = group_ref[0]
    lanes = lane_ids(FINE)
    half_ref[0:64, :] = raw_ref[0:64, :]

    for core in range(2):
        level, (lower, upper) = (
            (raw_ref, (other_ref, raw_ref)) if core else (other_ref, (raw_ref, other_ref))
        )

        @pl.when(group % 2 == core)
        def _(core=core, level=level, lower=lower, upper=upper):
            for row in range(2):
                half_ref[64 + row * FINE : 64 + (row + 1) * FINE, :] = level_rows(level, 0, 2 * core + row)
            beyond = level_rows(level, 1, 0)
            for row in range(1, 4):
                beyond = jnp.where(lanes < 16 * row, beyond, roll_lanes(level_rows(level, 1, row), 16 * row))
            half_ref[192:256, :] = beyond

            def edges(tile, level_start, field_start):
                packed = roll_lanes(level_rows(level, tile, 0), -level_start)
                for row in range(1, 4):
                    turned = roll_lanes(level_rows(level, tile, row), 16 * row - level_start)
                    packed = jnp.where(lanes < 16 * row, packed, turned)
                packed = jnp.where(lanes < 64, packed, roll_lanes(lower[0:64, :], 64 - field_start))
                packed = jnp.where(lanes < 72, packed, roll_lanes(upper[0:64, :], 72 - field_start))
                edge_ref[0:64, :] = packed
                edge_ref[64:80, :] = mark_ref[tile]

            ahead = jnp.logical_or(group == 0, group == 3)

            @pl.when(ahead)
            def _():
                edges(1, 112, 120)

            @pl.when(jnp.logical_not(ahead))
            def _():
                edges(0, 0, 0)


def join_kernel(half_ref, edge_ref, out_ref):
    out_ref[0:256, :] = half_ref[...]
    out_ref[256:336, :] = edge_ref[...]


def assemble_kernel(
    group_ref, place_ref, raw_ref, other_ref, mark_ref, half_ref, far_half_ref,
    fixed_ref, first_ref, second_ref, up_ref, down_ref,
):
    group = group_ref[0]
    lanes = lane_ids(64)

    def assemble(own):
        core, first, last = own % 2, own == 0, own == 3
        local = (raw_ref, other_ref) if core == 0 else (other_ref, raw_ref)
        remote = (half_ref, far_half_ref) if core == 0 else (far_half_ref, half_ref)
        fields = [ref[0:64, :] for ref in ((*local, *remote) if own < 2 else (*remote, *local))]
        near, far = half_ref[256:320, :], far_half_ref[256:320, :]

        def placed(index, lane):
            value = roll_lanes(fields[index], lane + 4 - 32 * own)
            edge = (near, near, far, far)[index]
            source = 64 + 8 * (index % 2)
            if first:
                value = jnp.where(lanes < lane + 4, roll_lanes(edge, lane - source - 4), value)
            if last:
                value = jnp.where(lanes >= lane + 36, roll_lanes(edge, lane + 36 - source), value)
            return value

        parts = [placed(index, SLOT * index) for index in range(3)]
        moving = by_slot(lanes, *parts)
        pressure = placed(3, 0)
        fixed_ref[0:64, :] = moving
        fixed_ref[64:128, :] = pressure
        level_tiles = []
        for row in range(4):
            if own < 2:
                low = remote[row // 2][64 + (row % 2) * FINE : 64 + (row % 2 + 1) * FINE, :]
                high = roll_lanes(far_half_ref[192:256, :] if core == 0 else half_ref[192:256, :], -16 * row)
            else:
                level = raw_ref if core else other_ref
                low, high = level_rows(level, 0, row), level_rows(level, 1, row)
            value = {
                0: lambda: jnp.where(lanes < 32, roll_lanes(far, 16 - 16 * row), roll_lanes(low, 32)),
                1: lambda: roll_lanes(jnp.where(lanes < 32, high, low), 96),
                2: lambda: roll_lanes(jnp.where(lanes < 96, high, low), 32),
                3: lambda: jnp.where(lanes < 96, roll_lanes(high, 96), roll_lanes(far, 96 - 16 * row)),
            }[own]()
            fixed_ref[128 + row * FINE : 128 + (row + 1) * FINE, :] = value
            level_tiles.append(value)
        for out_ref, (near, next_row, far_row) in ((up_ref, (2, 3, 1)), (down_ref, (0, 1, 2))):
            pair = folded(level_tiles[near], level_tiles[next_row], level_tiles[far_row])
            out_ref[0:64, :] = pair[0]
            row = 1 if near else 0
            push = pressure[row * FLOW : (row + 1) * FLOW, :]
            out_ref[64:96, :] = lay(push, pair[1][0:32, :], 8, 24, 8)
            out_ref[96:128, :] = lay(push, pair[1][32:64, :], 8, 24, -8)
            out_ref[128:160, :] = lay(push, moving[row * FLOW : (row + 1) * FLOW, :], 120, 128, 88)
        low, high, beside, few = mark_ref[0], mark_ref[1], half_ref[320:336, :], lane_ids(16)
        marks = {
            0: lambda: roll_lanes(jnp.where(few < 96, low, beside), 32),
            1: lambda: roll_lanes(jnp.where(few < 32, high, low), 96),
            2: lambda: roll_lanes(jnp.where(few < 96, high, low), 32),
            3: lambda: roll_lanes(jnp.where(few < 32, beside, high), 96),
        }[own]()
        fixed_ref[384:400, :] = marks
        for out_ref in (up_ref, down_ref):
            out_ref[160:176, :] = marks

    for own in range(4):

        @pl.when(group == own)
        def _(own=own):
            assemble(own)

    by_side(place_ref, down_ref, up_ref, first_ref, second_ref)


def bent(below, here, above):
    return (above - here) - (here - below)


def mixed(smooth_one, smooth_two, smooth_three, curve_one, curve_two, curve_three):
    both_three = smooth_one * smooth_two
    both_two = smooth_one * smooth_three
    both_one = smooth_two * smooth_three
    one = both_one * both_one
    three = both_three * both_three
    bottom = (one + 6.0 * (both_two * both_two)) + 3.0 * three
    top = one * ((curve_one - curve_two) * (1.0 / 3.0)) + three * ((curve_two - curve_three) * 0.5)
    return top / bottom - curve_two * (1.0 / 6.0)


THIRDS = 4.0 / 3.0


def upwind_part(far_low, low, mid, high, far_high, slope, speed):
    ahead = speed >= 0.0
    one = jnp.where(ahead, far_low, far_high)
    two = jnp.where(ahead, low, high)
    four = jnp.where(ahead, high, low)
    curve_one = two - one
    curve_two = mid - two
    curve_three = four - mid
    smooth_one = (two * two + WENO_EPS) + curve_one * (THIRDS * curve_one + two)
    smooth_two = (two * mid + WENO_EPS) + THIRDS * (curve_two * curve_two)
    smooth_three = (mid * mid + WENO_EPS) + curve_three * (THIRDS * curve_three - mid)
    rest = mixed(smooth_one, smooth_two, smooth_three, curve_one, curve_two, curve_three)
    return speed * slope + jnp.abs(speed) * rest


def pair_terms(low, high, low_square, high_square):
    change = high - low
    wide = THIRDS * change
    rising = high_square + change * (wide + high)
    falling = low_square + change * (wide - low)
    level = (low * high + WENO_EPS) + change * wide
    return change, rising, falling, level


def upwind_pairs(one, two, three, four, slope, speed):
    ahead = speed >= 0.0
    rest = mixed(
        jnp.where(ahead, one[1], four[2]),
        jnp.where(ahead, two[3], three[3]),
        jnp.where(ahead, three[2], two[1]),
        jnp.where(ahead, one[0], four[0]),
        jnp.where(ahead, two[0], three[0]),
        jnp.where(ahead, three[0], two[0]),
    )
    return speed * (slope + rest)


def fill_wrapped(wrapped, index, source, at):
    wrapped[index, 8:72, :] = source[at : at + FINE, :]
    wrapped[index, 0:8, :] = source[at + 56 : at + 64, :]
    wrapped[index, 72:80, :] = source[at : at + 8, :]


def load(place, z):
    ref, at = place
    return ref[pl.ds(at + z, 8), :]


def speed_loader(own_ref, rim_ref, first_row):
    def speed(component, index, z):
        row = (first_row + index) // 2
        ref, at = (own_ref, row) if 0 <= row < 2 else (rim_ref, 0 if row < 0 else 1)
        return ref[component, at, pl.ds(z, 8), :]

    return speed


def across(here, wrapped, index, z, speed_y, speed_z):
    after = roll_lanes(here, -1)
    before = roll_lanes(here, 1)
    mid = bent(before, here, after)
    shifts = [roll_lanes(mid, 2), roll_lanes(mid, 1), mid, roll_lanes(mid, -1), roll_lanes(mid, -2)]
    rate = upwind_part(*shifts, (after - before) * 0.5, speed_y)
    column = [wrapped[index, pl.ds(z + 8 + offset, 8), :] for offset in range(-3, 4)]
    column[3] = here
    column_bends = [bent(column[k - 1], column[k], column[k + 1]) for k in range(1, 6)]
    return rate + upwind_part(*column_bends, (column[4] - column[2]) * 0.5, speed_z)


def across_rows(places, speed, wrapped, rate_ref):
    for index, place in enumerate(places):
        fill_wrapped(wrapped, index, *place)

    def body(step, carry):
        z = chunk(step)
        for index, place in enumerate(places):
            rate = across(load(place, z), wrapped, index, z, speed(1, index, z), speed(2, index, z))
            rate_ref[pl.ds(index * FINE + z, 8), :] = rate
        return carry

    lax.fori_loop(0, 8, body, 0)


def section(current, initial, speed, rates, wrapped, keep, blend, store):
    rows = len(rates)
    for index in range(rows):
        if rates[index] is None:
            fill_wrapped(wrapped, index, *current[index + 3])

    def body(step, carry):
        z = chunk(step)
        values = [load(place, z) for place in current]
        steps = [values[k + 1] - values[k] for k in range(rows + 5)]
        bends = [steps[k + 1] - steps[k] for k in range(rows + 4)]
        squares = [value * value + WENO_EPS for value in bends]
        pairs = {}
        for index in range(rows):
            for k in range(index, index + 4):
                if k not in pairs:
                    pairs[k] = pair_terms(bends[k], bends[k + 1], squares[k], squares[k + 1])
            here = values[index + 3]
            slope = (steps[index + 3] + steps[index + 2]) * 0.5
            rate = upwind_pairs(*(pairs[k] for k in range(index, index + 4)), slope, speed(0, index, z))
            if rates[index] is None:
                rate = rate + across(here, wrapped, index, z, speed(1, index, z), speed(2, index, z))
            else:
                rate = rate + load(rates[index], z)
            moved = blend * (here - STEP_FINE * rate)
            if keep:
                moved = moved + keep * load(initial[index], z)
            store(index, z, moved)
        return carry

    lax.fori_loop(0, 8, body, 0)


def spread_speeds(stacked, speed_ref):
    source_lane = lax.broadcasted_iota(jnp.int32, (LANES, LANES), 0)
    fine_lane = lax.broadcasted_iota(jnp.int32, (LANES, LANES), 1)
    covered = jnp.logical_and(fine_lane >= 24, fine_lane < 104)
    for component in range(3):
        pick = jnp.logical_and(source_lane == SLOT * component + fine_lane // 2 - 12, covered)
        spread = exact_dot(stacked, jnp.where(pick, 1.0, 0.0))
        for row in range(2):
            part = spread[row * FLOW : (row + 1) * FLOW, :]
            speed_ref[component, row, pl.ds(0, FLOW, stride=2), :] = part
            speed_ref[component, row, pl.ds(1, FLOW, stride=2), :] = part


def in_pairs(work):
    def body(step, carry):
        for part in range(2):
            work(pl.multiple_of(step * 16 + part * 8, 8))
        return carry

    lax.fori_loop(0, 4, body, 0)


def centred(below, above):
    return (above - below) * 0.5


def planes(value):
    return pltpu.roll(value, FLOW - 1, 0), pltpu.roll(value, 1, 0)


def by_slot(lanes, first, second, third):
    return jnp.where(lanes < SLOT, first, jnp.where(lanes < 2 * SLOT, second, third))


def sweep(below, here, above, source):
    up, down = planes(here)
    beside = below + above + roll_lanes(here, 1) + roll_lanes(here, -1) + up + down
    return (source + IMPLICIT * beside) / (1.0 + 6.0 * IMPLICIT)


def inner_kernel(fixed_ref, speed_ref, rate_ref, wrapped):
    spread_speeds(fixed_ref[0:64, :], speed_ref)
    places = [(fixed_ref, 128 + FINE * row) for row in range(4)]
    across_rows(places, speed_loader(speed_ref, None, 0), wrapped, rate_ref)


def first_kernel(
    place_ref, fixed_ref, one_ref, two_ref, speed_ref, rate_ref, out_ref, send_ref, left_ref, right_ref, spare
):
    by_side(place_ref, one_ref, two_ref, left_ref, right_ref)
    moving = [
        left_ref[128:160, :],
        fixed_ref[0:32, :],
        fixed_ref[32:64, :],
        right_ref[128:160, :],
    ]
    lanes = lane_ids(FLOW)
    pressure = [
        sent_pressure(left_ref),
        fixed_ref[64:96, :],
        fixed_ref[96:128, :],
        sent_pressure(right_ref),
    ]
    pressure = [by_slot(lanes, p, roll_lanes(p, 40), roll_lanes(p, 80)) for p in pressure]
    for row in range(2):
        here, push = moving[row + 1], pressure[row + 1]
        back, further = roll_lanes(here, 88), roll_lanes(here, 40)
        along_x = by_slot(lanes, here, further, roll_lanes(here, 80))
        along_y = by_slot(lanes, back, here, further)
        along_z = by_slot(lanes, roll_lanes(here, 48), back, here)
        up, down = planes(here)
        push_up, push_down = planes(push)
        advect = -(
            along_x * centred(moving[row], moving[row + 2])
            + along_y * centred(roll_lanes(here, 1), roll_lanes(here, -1))
            + along_z * centred(down, up)
        )
        gradient = by_slot(
            lanes,
            centred(pressure[row], pressure[row + 2]),
            centred(roll_lanes(push, 1), roll_lanes(push, -1)),
            centred(push_down, push_up),
        )
        out_ref[256 + row * FLOW : 256 + (row + 1) * FLOW, :] = here + STEP_FLOW * (advect - gradient)

    spare[0:64, :] = unfolded(left_ref[0:64, :], left_ref[64:128, :])
    spare[64:128, :] = unfolded(right_ref[0:64, :], right_ref[64:128, :])
    places = (
        [(spare, 0), (left_ref, 0), (left_ref, 64)]
        + [(fixed_ref, 128 + FINE * row) for row in range(4)]
        + [(right_ref, 0), (right_ref, 64), (spare, 64)]
    )

    def store(index, z, value):
        out_ref[pl.ds(index * FINE + z, 8), :] = value

    rates = [(rate_ref, FINE * row) for row in range(4)]
    section(places, None, speed_loader(speed_ref, None, 0), rates, None, 0.0, 1.0, store)
    source = out_ref[256:320, :]
    send_ref[0:64, :], beside = folded(out_ref[0:64, :], out_ref[64:128, :], out_ref[192:256, :])
    send_ref[64:128, :] = lay(source, beside, 8, 24, -40)
    send_ref[128:192, :] = lay(source, out_ref[128:192, :], 104, 152, 104)
    send_ref[192:224, :] = lay(source[0:32, :], source[32:64, :], 0, 64, 64)


def middle_kernel(own_ref, old_left, old_right, speed_ref, rim_ref, rate_ref, wrapped):
    spread_speeds(jnp.concatenate([old_left[128:160, :], old_right[128:160, :]], axis=0), rim_ref)
    places = [(own_ref, FINE * row) for row in range(4)]
    across_rows(places, speed_loader(speed_ref, None, 0), wrapped, rate_ref)


def second_kernel(
    place_ref, own_ref, one_ref, two_ref, fixed_ref, old_left, old_right, speed_ref, rim_ref, rate_ref,
    out_ref, first_ref, second_ref, wrapped, spare, left_ref, right_ref, up_ref, down_ref,
):
    by_side(place_ref, one_ref, two_ref, left_ref, right_ref)
    source = [sent_source(left_ref, row) for row in range(2)]
    source += [own_ref[256 + row * FLOW : 256 + (row + 1) * FLOW, :] for row in range(2)]
    source += [sent_source(right_ref, row) for row in range(2)]
    out_ref[512:544, :], out_ref[544:576, :] = source[1], source[4]
    for row in range(4):
        done = sweep(source[row], source[row + 1], source[row + 2], source[row + 1])
        out_ref[384 + row * FLOW : 384 + (row + 1) * FLOW, :] = done
    spare[0:64, :] = unfolded(left_ref[0:64, :], left_ref[64:128, :])
    spare[64:128, :] = unfolded(right_ref[0:64, :], right_ref[64:128, :])
    places = (
        [(left_ref, FINE * row) for row in range(3)]
        + [(spare, 0)]
        + [(own_ref, FINE * row) for row in range(4)]
        + [(right_ref, FINE * row) for row in range(3)]
        + [(spare, 64)]
    )
    initial = [(old_left, 64)] + [(fixed_ref, 128 + FINE * row) for row in range(4)] + [(old_right, 0)]

    def store(index, z, value):
        out_ref[pl.ds(index * FINE + z, 8), :] = value

    rates = [None] + [(rate_ref, FINE * row) for row in range(4)] + [None]
    section(places, initial, speed_loader(speed_ref, rim_ref, -1), rates, wrapped, 0.75, 0.25, store)
    for to_ref, at in ((up_ref, 0), (down_ref, 128)):
        last = out_ref[at + 192 : at + 256, :]
        to_ref[0:64, :], beside = folded(out_ref[at : at + 64, :], out_ref[at + 64 : at + 128, :], last)
        done = out_ref[448:480, :] if at else out_ref[416:448, :]
        to_ref[64:96, :] = lay(done, beside[0:32, :], 8, 24, 40)
        to_ref[96:128, :] = lay(done, beside[32:64, :], 8, 16, 24)
        to_ref[128:160, :] = lay(done, out_ref[at + 128 : at + 160, :], 104, 152, 104)
        to_ref[160:192, :] = lay(done, out_ref[at + 160 : at + 192, :], 104, 152, 56)
    by_side(place_ref, down_ref, up_ref, first_ref, second_ref)


def late_kernel(own_ref, speed_ref, rim_ref, rate_ref, wrapped):
    places = [(own_ref, FINE * row) for row in range(6)]
    across_rows(places, speed_loader(speed_ref, rim_ref, -1), wrapped, rate_ref)


def third_kernel(
    place_ref, own_ref, one_ref, two_ref, older, fixed_ref, old_left, old_right,
    speed_ref, rim_ref, rate_ref,
    out_ref, wrapped, shaped, normal_x, normal_z, summed, spare, left_ref, right_ref,
):
    by_side(place_ref, one_ref, two_ref, left_ref, right_ref)
    spare[0:64, :] = unfolded(left_ref[0:64, :], left_ref[64:128, :])
    spare[64:128, :] = unfolded(right_ref[0:64, :], right_ref[64:128, :])
    places = (
        [(left_ref, FINE * row) for row in range(3)]
        + [(spare, 0)]
        + [(own_ref, FINE * row) for row in range(6)]
        + [(right_ref, FINE * row) for row in range(3)]
        + [(spare, 64)]
    )
    initial = (
        [(old_left, 0), (old_left, 64)]
        + [(fixed_ref, 128 + FINE * row) for row in range(4)]
        + [(old_right, 0), (old_right, 64)]
    )
    marks = [(old_left, 160)] * 2 + [(fixed_ref, 384)] * 4 + [(old_right, 160)] * 2

    def store(index, z, value):
        ref, at = initial[index]
        mark_ref, mark_at = marks[index]
        flag = mark_ref[pl.ds(mark_at + z // 8, 1), :]
        value = jnp.where(flag > 0.5, value, ref[pl.ds(at + z, 8), :]) * (1.0 / SHRINK)
        shaped[index, pl.ds(8 + z, 8), :] = value

    rates = [None] + [(rate_ref, FINE * row) for row in range(6)] + [None]
    section(places, initial, speed_loader(speed_ref, rim_ref, -2), rates, wrapped, 1.0 / 3.0, 2.0 / 3.0, store)
    for index, (mark_ref, mark_at) in enumerate(marks):
        at = mark_at + 8 + (index + 2) % 4
        phase = mark_ref[at : at + 1, :]
        inflow = jnp.where(phase == 2.0, SPREAD, jnp.where(phase == 1.0, -SPREAD, shaped[index, 8:9, :]))
        shaped[index, 8:9, :] = inflow
        shaped[index, 0:8, :] = shaped[index, 64:72, :]
        shaped[index, 72:80, :] = shaped[index, 8:16, :]

    def normals(z):
        middle = [shaped[k, pl.ds(8 + z, 8), :] for k in range(8)]
        for row in range(6):
            here = middle[row + 1]
            slope_x = (middle[row + 2] - middle[row]) * 0.5
            slope_y = (roll_lanes(here, -1) - roll_lanes(here, 1)) * 0.5
            slope_z = (shaped[row + 1, pl.ds(9 + z, 8), :] - shaped[row + 1, pl.ds(7 + z, 8), :]) * 0.5
            inverse = lax.rsqrt(slope_x * slope_x + slope_y * slope_y + slope_z * slope_z + 1.0)
            normal_x[row, pl.ds(z, 8), :] = slope_x * inverse
            if 0 < row < 5:
                wrapped[row, pl.ds(z, 8), :] = slope_y * inverse
                normal_z[row - 1, pl.ds(8 + z, 8), :] = slope_z * inverse

    in_pairs(normals)
    for row in range(4):
        normal_z[row, 0:8, :] = normal_z[row, 64:72, :]
        normal_z[row, 72:80, :] = normal_z[row, 8:16, :]

    def forces(z):
        for half in range(2):
            total = None
            for row in (2 * half, 2 * half + 1):
                level = shaped[row + 2, pl.ds(8 + z, 8), :]
                here_x = normal_x[row + 1, pl.ds(z, 8), :]
                here_y = wrapped[row + 1, pl.ds(z, 8), :]
                here_z = normal_z[row, pl.ds(8 + z, 8), :]
                curvature = (normal_x[row + 2, pl.ds(z, 8), :] - normal_x[row, pl.ds(z, 8), :]) * 0.5
                curvature = curvature + (roll_lanes(here_y, -1) - roll_lanes(here_y, 1)) * 0.5
                curvature = (
                    curvature + (normal_z[row, pl.ds(9 + z, 8), :] - normal_z[row, pl.ds(7 + z, 8), :]) * 0.5
                )
                delta = jnp.exp(level * level * (-1.0 / (2.0 * SPREAD * SPREAD))) * (1.0 / (SPREAD * 2.5066282746310002))
                strength = SURFACE * curvature * delta
                fraction = 0.5 + 0.5 * jnp.tanh(level * (1.0 / SPREAD))
                terms = (here_x * strength, here_y * strength, here_z * strength, fraction)
                total = terms if total is None else tuple(a + b for a, b in zip(total, terms))
            for component in range(4):
                summed[component, pl.ds(half * FINE + z, 8), :] = total[component]

    in_pairs(forces)

    source = [own_ref[512:544, :], older[256:288, :], older[288:320, :], own_ref[544:576, :]]
    once = [sent_sweep(left_ref)] + [own_ref[384 + row * FLOW : 384 + (row + 1) * FLOW, :] for row in range(4)]
    once = once + [sent_sweep(right_ref)]
    twice = [sweep(once[row], once[row + 1], once[row + 2], source[row]) for row in range(4)]
    thrice = [sweep(twice[row], twice[row + 1], twice[row + 2], source[row + 1]) for row in range(2)]

    source_lane = lax.broadcasted_iota(jnp.int32, (LANES, LANES), 0)
    out_lane = lax.broadcasted_iota(jnp.int32, (LANES, LANES), 1)
    part, column = out_lane // FLOW, out_lane % FLOW
    take = jnp.logical_and(source_lane == SLOT * part + 4 + column, part < 3)
    done = exact_dot(jnp.concatenate(thrice, axis=0), jnp.where(take, 1.0, 0.0))
    for component in range(4):
        take = jnp.logical_and((source_lane - 32) // 2 == column, part == component)
        take = jnp.logical_and(take, jnp.logical_and(source_lane >= 32, source_lane < 96))
        scale = 0.125 * STEP_FLOW if component < 3 else 0.125
        pairs = jnp.concatenate(
            [
                summed[component, pl.ds(half * FINE, FLOW, stride=2), :]
                + summed[component, pl.ds(half * FINE + 1, FLOW, stride=2), :]
                for half in range(2)
            ],
            axis=0,
        )
        done = done + exact_dot(pairs * scale, jnp.where(take, 1.0, 0.0))
    out_ref[...] = done


def sort_kernel(group_ref, own_ref, other_ref, keep_ref, send_ref):
    group = group_ref[0]
    lanes = lane_ids(64)
    beside = group + 1 - 2 * (group % 2)
    for target, out_ref in ((group, keep_ref), ((group + 2) % 4, send_ref)):
        own = pltpu.roll(own_ref[...], (32 * group - 32 * target + LANES) % LANES, 1)
        other = pltpu.roll(other_ref[...], (32 * beside - 32 * target + LANES) % LANES, 1)
        out_ref[...] = jnp.where(lanes // 32 == group, own, other)


def merge_kernel(group_ref, keep_ref, far_ref, out_ref):
    merged = jnp.where(lane_ids(64) // 64 == group_ref[0] // 2, keep_ref[...], far_ref[...])
    for row in range(2):
        out_ref[:, row, :] = merged[row * FLOW : (row + 1) * FLOW, :]


def call(kernel, outs, scratch, *args, scalars=0, outer=False, last=False):
    vmem = pl.BlockSpec(memory_space=pltpu.VMEM)
    smem = pl.BlockSpec(memory_space=pltpu.SMEM)
    shapes = [jax.ShapeDtypeStruct(shape, F32) if last else pltpu.VMEM(shape, F32) for shape in outs]
    held = list(args[scalars:])
    if not outer:
        held = [pltpu.with_memory_space_constraint(value, pltpu.VMEM) for value in held]
    return pl.pallas_call(
        kernel,
        out_shape=shapes if len(shapes) > 1 else shapes[0],
        in_specs=[smem] * scalars + [vmem] * len(held),
        out_specs=[vmem] * len(shapes) if len(shapes) > 1 else vmem,
        scratch_shapes=[pltpu.VMEM(shape, F32) for shape in scratch],
    )(*args[:scalars], *held)


def swapped(first, second):
    count = lax.axis_size("gx")
    near = [(i, i ^ 1) for i in range(count)]
    far = [(i, (i + (1 if i % 2 else -1)) % count) for i in range(count)]
    first = lax.ppermute(first, "gx", near)
    second = lax.ppermute(second, "gx", far)
    return first, second


def crossed(value, bit):
    return lax.ppermute(value, "grp", [(i, i ^ bit) for i in range(lax.axis_size("grp"))])


def to_next_blocks(value):
    blocks = lax.axis_size("gy")
    pairs = []
    for source, target, step in ((0, 0, 1), (1, 3, -1), (2, 2, -1), (3, 1, 1)):
        pairs += [(source * blocks + j, target * blocks + (j + step) % blocks) for j in range(blocks)]
    return lax.ppermute(value, ("grp", "gy"), pairs)


def on_device(flow_fields, level_set, band_tiles, nozzle_phase):
    group = lax.axis_index("grp").astype(jnp.int32)[None]
    place = lax.axis_index("gx").astype(jnp.int32)[None]
    raw, marks = call(
        pack_kernel,
        [(LEVEL + 8 * FINE, LANES), (2, 16, LANES)],
        [],
        flow_fields[0],
        level_set[0],
        band_tiles[:, 0, :],
        nozzle_phase,
        outer=True,
    )
    other = crossed(raw, 1)
    half, edge = call(split_kernel, [(256, LANES), (80, LANES)], [], group, raw, other, marks, scalars=1)
    half = call(join_kernel, [(336, LANES)], [], crossed(half, 2), to_next_blocks(edge))
    far_half = crossed(half, 1)
    fixed, first, second = call(
        assemble_kernel,
        [(400, LANES), (176, LANES), (176, LANES)],
        [(176, LANES), (176, LANES)],
        group,
        place,
        raw,
        other,
        marks,
        half,
        far_half,
        scalars=2,
    )
    speed_shape = (3, 2, FINE, LANES)
    first, second = swapped(first, second)
    speeds, rates = call(inner_kernel, [speed_shape, (256, LANES)], [(4, 80, LANES)], fixed)
    own, send, old_left, old_right = call(
        first_kernel,
        [(320, LANES), (224, LANES), (176, LANES), (176, LANES)],
        [(128, LANES)],
        place,
        fixed,
        first,
        second,
        speeds,
        rates,
        scalars=1,
    )
    first, second = swapped(send, send)
    rim, rates = call(
        middle_kernel, [speed_shape, (256, LANES)], [(4, 80, LANES)], own, old_left, old_right, speeds
    )
    newer, first, second = call(
        second_kernel,
        [(576, LANES), (192, LANES), (192, LANES)],
        [(6, 80, LANES), (128, LANES), (224, LANES), (224, LANES), (192, LANES), (192, LANES)],
        place,
        own,
        first,
        second,
        fixed,
        old_left,
        old_right,
        speeds,
        rim,
        rates,
        scalars=1,
    )
    first, second = swapped(first, second)
    rates = call(late_kernel, [(384, LANES)], [(6, 80, LANES)], newer, speeds, rim)
    result = call(
        third_kernel,
        [(64, LANES)],
        [
            (8, 80, LANES),
            (8, 80, LANES),
            (6, FINE, LANES),
            (4, 80, LANES),
            (4, 2 * FINE, LANES),
            (128, LANES),
            (192, LANES),
            (192, LANES),
        ],
        place,
        newer,
        first,
        second,
        own,
        fixed,
        old_left,
        old_right,
        speeds,
        rim,
        rates,
        scalars=1,
    )
    keep, send = call(
        sort_kernel, [(64, LANES), (64, LANES)], [], group, result, crossed(result, 1), scalars=1
    )
    return call(merge_kernel, [(FLOW, 2, LANES)], [], group, keep, crossed(send, 2), scalars=1, last=True)[None]


def solution(mesh):
    placed = (
        P("grp", None, "gx", "gy"),
        P("grp", None, "gx", "gy"),
        P(None, "gx", "gy"),
        P("gx", "gy"),
    )
    return jax.shard_map(
        on_device, mesh=mesh, in_specs=placed, out_specs=P("grp", None, "gx", "gy"), check_vma=False
    )
```

```python
import jax
import jax.numpy as jnp
from jax import lax
from jax.experimental import pallas as pl
from jax.experimental.pallas import tpu as pltpu
from jax.sharding import PartitionSpec as P


LANES = 128
FINE = 64
FLOW = 32
SLOT = 40
LEVEL = 64
SHRINK = 0.25
WENO_EPS = 1e-06 * SHRINK * SHRINK
STEP_FINE = 0.3
STEP_FLOW = 0.2
SURFACE = 6.0
SPREAD = 1.5
IMPLICIT = 0.5
F32 = jnp.float32


def lane_ids(rows):
    return lax.broadcasted_iota(jnp.int32, (rows, LANES), 1)


def roll_lanes(value, shift):
    return pltpu.roll(value, shift % LANES, 1)


def exact_dot(left, right):
    return jnp.dot(left, right, precision=lax.Precision.HIGHEST, preferred_element_type=F32)


def folded(first, second, last):
    lanes = lane_ids(FINE)
    inside = jnp.logical_and(lanes >= 24, lanes < 104)
    return jnp.where(inside, first, roll_lanes(last, 80)), jnp.where(inside, second, roll_lanes(last, 32))


def unfolded(first, second):
    return jnp.where(lane_ids(FINE) < 72, roll_lanes(first, -80), roll_lanes(second, -32))


def lay(value, base, first, last, shift):
    lanes = lane_ids(value.shape[0])
    inside = jnp.logical_and(lanes >= first, lanes < last)
    if last > LANES:
        inside = jnp.logical_or(lanes >= first, lanes < last - LANES)
    return jnp.where(inside, roll_lanes(value, shift), base)


def parted(limits, parts):
    lanes = lane_ids(parts[0].shape[0])
    value = parts[-1]
    for limit, part in reversed(list(zip(limits, parts))):
        value = jnp.where(lanes < limit, part, value)
    return value


def sent_pressure(ref):
    return parted((16, 32), (roll_lanes(ref[64:96, :], -8), roll_lanes(ref[96:128, :], 8), roll_lanes(ref[128:160, :], -88)))


def sent_source(ref, row):
    at = row * FLOW
    rest = ref[192:224, :]
    return parted(
        (48, 64),
        (
            roll_lanes(ref[128 + at : 160 + at, :], -104),
            roll_lanes(ref[64 + at : 96 + at, :], 40),
            rest if row else roll_lanes(rest, 64),
        ),
    )


def sent_sweep(ref):
    return parted(
        (48, 96, 112),
        (
            roll_lanes(ref[128:160, :], -104),
            roll_lanes(ref[160:192, :], -56),
            roll_lanes(ref[64:96, :], -40),
            roll_lanes(ref[96:128, :], -24),
        ),
    )


def by_side(place_ref, first_ref, second_ref, left_ref, right_ref):
    odd = place_ref[0] % 2 == 1

    @pl.when(odd)
    def _():
        left_ref[...] = first_ref[...]
        right_ref[...] = second_ref[...]

    @pl.when(jnp.logical_not(odd))
    def _():
        left_ref[...] = second_ref[...]
        right_ref[...] = first_ref[...]


def pack_kernel(flow_ref, level_ref, band_ref, nozzle_ref, raw_ref, mark_ref):
    for row in range(2):
        raw_ref[row * FLOW : (row + 1) * FLOW, :] = flow_ref[:, row, :]
    for row in range(4):
        block = level_ref[:, row, :] * SHRINK
        raw_ref[LEVEL + row * FINE : LEVEL + (row + 1) * FINE, :] = block[:, :LANES]
        raw_ref[LEVEL + (row + 4) * FINE : LEVEL + (row + 5) * FINE, :] = block[:, LANES:]
    spread_tiles = jnp.where(
        lax.broadcasted_iota(jnp.int32, (16, 256), 1) // 16 == lax.broadcasted_iota(jnp.int32, (16, 256), 0), 1.0, 0.0
    )
    flags = exact_dot(band_ref[...].astype(F32), spread_tiles)
    phases = nozzle_ref[...].astype(F32)
    for half in range(2):
        part = slice(half * LANES, (half + 1) * LANES)
        mark_ref[half, 0:8, :] = flags[:, part]
        mark_ref[half, 8:12, :] = phases[:, part]
        mark_ref[half, 12:16, :] = jnp.zeros((4, LANES), F32)


def level_rows(ref, tile, row):
    at = LEVEL + (4 * tile + row) * FINE
    return ref[at : at + FINE, :]


def split_kernel(group_ref, raw_ref, other_ref, mark_ref, half_ref, edge_ref):
    group = group_ref[0]
    lanes = lane_ids(FINE)
    half_ref[0:64, :] = raw_ref[0:64, :]

    for core in range(2):
        level, (lower, upper) = (
            (raw_ref, (other_ref, raw_ref)) if core else (other_ref, (raw_ref, other_ref))
        )

        @pl.when(group % 2 == core)
        def _(core=core, level=level, lower=lower, upper=upper):
            for row in range(2):
                half_ref[64 + row * FINE : 64 + (row + 1) * FINE, :] = level_rows(level, 0, 2 * core + row)
            beyond = level_rows(level, 1, 0)
            for row in range(1, 4):
                beyond = jnp.where(lanes < 16 * row, beyond, roll_lanes(level_rows(level, 1, row), 16 * row))
            half_ref[192:256, :] = beyond

            def edges(tile, level_start, field_start):
                packed = roll_lanes(level_rows(level, tile, 0), -level_start)
                for row in range(1, 4):
                    turned = roll_lanes(level_rows(level, tile, row), 16 * row - level_start)
                    packed = jnp.where(lanes < 16 * row, packed, turned)
                packed = jnp.where(lanes < 64, packed, roll_lanes(lower[0:64, :], 64 - field_start))
                packed = jnp.where(lanes < 72, packed, roll_lanes(upper[0:64, :], 72 - field_start))
                edge_ref[0:64, :] = packed
                edge_ref[64:80, :] = mark_ref[tile]

            ahead = jnp.logical_or(group == 0, group == 3)

            @pl.when(ahead)
            def _():
                edges(1, 112, 120)

            @pl.when(jnp.logical_not(ahead))
            def _():
                edges(0, 0, 0)


def join_kernel(half_ref, edge_ref, out_ref):
    out_ref[0:256, :] = half_ref[...]
    out_ref[256:336, :] = edge_ref[...]


def assemble_kernel(
    group_ref, place_ref, raw_ref, other_ref, mark_ref, half_ref, far_half_ref,
    fixed_ref, first_ref, second_ref, up_ref, down_ref,
):
    group = group_ref[0]
    lanes = lane_ids(64)

    def assemble(own):
        core, first, last = own % 2, own == 0, own == 3
        local = (raw_ref, other_ref) if core == 0 else (other_ref, raw_ref)
        remote = (half_ref, far_half_ref) if core == 0 else (far_half_ref, half_ref)
        fields = [ref[0:64, :] for ref in ((*local, *remote) if own < 2 else (*remote, *local))]
        near, far = half_ref[256:320, :], far_half_ref[256:320, :]

        def placed(index, lane):
            value = roll_lanes(fields[index], lane + 4 - 32 * own)
            edge = (near, near, far, far)[index]
            source = 64 + 8 * (index % 2)
            if first:
                value = jnp.where(lanes < lane + 4, roll_lanes(edge, lane - source - 4), value)
            if last:
                value = jnp.where(lanes >= lane + 36, roll_lanes(edge, lane + 36 - source), value)
            return value

        parts = [placed(index, SLOT * index) for index in range(3)]
        moving = by_slot(lanes, *parts)
        pressure = placed(3, 0)
        fixed_ref[0:64, :] = moving
        fixed_ref[64:128, :] = pressure
        level_tiles = []
        for row in range(4):
            if own < 2:
                low = remote[row // 2][64 + (row % 2) * FINE : 64 + (row % 2 + 1) * FINE, :]
                high = roll_lanes(far_half_ref[192:256, :] if core == 0 else half_ref[192:256, :], -16 * row)
            else:
                level = raw_ref if core else other_ref
                low, high = level_rows(level, 0, row), level_rows(level, 1, row)
            value = {
                0: lambda: jnp.where(lanes < 32, roll_lanes(far, 16 - 16 * row), roll_lanes(low, 32)),
                1: lambda: roll_lanes(jnp.where(lanes < 32, high, low), 96),
                2: lambda: roll_lanes(jnp.where(lanes < 96, high, low), 32),
                3: lambda: jnp.where(lanes < 96, roll_lanes(high, 96), roll_lanes(far, 96 - 16 * row)),
            }[own]()
            fixed_ref[128 + row * FINE : 128 + (row + 1) * FINE, :] = value
            level_tiles.append(value)
        for out_ref, (near, next_row, far_row) in ((up_ref, (2, 3, 1)), (down_ref, (0, 1, 2))):
            pair = folded(level_tiles[near], level_tiles[next_row], level_tiles[far_row])
            out_ref[0:64, :] = pair[0]
            row = 1 if near else 0
            push = pressure[row * FLOW : (row + 1) * FLOW, :]
            out_ref[64:96, :] = lay(push, pair[1][0:32, :], 8, 24, 8)
            out_ref[96:128, :] = lay(push, pair[1][32:64, :], 8, 24, -8)
            out_ref[128:160, :] = lay(push, moving[row * FLOW : (row + 1) * FLOW, :], 120, 128, 88)
        low, high, beside, few = mark_ref[0], mark_ref[1], half_ref[320:336, :], lane_ids(16)
        marks = {
            0: lambda: roll_lanes(jnp.where(few < 96, low, beside), 32),
            1: lambda: roll_lanes(jnp.where(few < 32, high, low), 96),
            2: lambda: roll_lanes(jnp.where(few < 96, high, low), 32),
            3: lambda: roll_lanes(jnp.where(few < 32, beside, high), 96),
        }[own]()
        fixed_ref[384:400, :] = marks
        for out_ref in (up_ref, down_ref):
            out_ref[160:176, :] = marks

    for own in range(4):

        @pl.when(group == own)
        def _(own=own):
            assemble(own)

    by_side(place_ref, down_ref, up_ref, first_ref, second_ref)


def bent(below, here, above):
    return (above - here) - (here - below)


def mixed(smooth_one, smooth_two, smooth_three, curve_one, curve_two, curve_three):
    both_three = smooth_one * smooth_two
    both_two = smooth_one * smooth_three
    both_one = smooth_two * smooth_three
    one = both_one * both_one
    three = both_three * both_three
    bottom = (one + 6.0 * (both_two * both_two)) + 3.0 * three
    top = one * ((curve_one - curve_two) * (1.0 / 3.0)) + three * ((curve_two - curve_three) * 0.5)
    return top / bottom - curve_two * (1.0 / 6.0)


THIRDS = 4.0 / 3.0


def upwind_part(far_low, low, mid, high, far_high, slope, speed):
    ahead = speed >= 0.0
    one = jnp.where(ahead, far_low, far_high)
    two = jnp.where(ahead, low, high)
    four = jnp.where(ahead, high, low)
    curve_one = two - one
    curve_two = mid - two
    curve_three = four - mid
    smooth_one = (two * two + WENO_EPS) + curve_one * (THIRDS * curve_one + two)
    smooth_two = (two * mid + WENO_EPS) + THIRDS * (curve_two * curve_two)
    smooth_three = (mid * mid + WENO_EPS) + curve_three * (THIRDS * curve_three - mid)
    rest = mixed(smooth_one, smooth_two, smooth_three, curve_one, curve_two, curve_three)
    return speed * slope + jnp.abs(speed) * rest


def pair_terms(low, high, low_square, high_square):
    change = high - low
    wide = THIRDS * change
    rising = high_square + change * (wide + high)
    falling = low_square + change * (wide - low)
    level = (low * high + WENO_EPS) + change * wide
    return change, rising, falling, level


def upwind_pairs(one, two, three, four, slope, speed):
    ahead = speed >= 0.0
    rest = mixed(
        jnp.where(ahead, one[1], four[2]),
        jnp.where(ahead, two[3], three[3]),
        jnp.where(ahead, three[2], two[1]),
        jnp.where(ahead, one[0], four[0]),
        jnp.where(ahead, two[0], three[0]),
        jnp.where(ahead, three[0], two[0]),
    )
    return speed * (slope + rest)


def fill_wrapped(wrapped, index, source, at):
    wrapped[index, 8:72, :] = source[at : at + FINE, :]
    wrapped[index, 0:8, :] = source[at + 56 : at + 64, :]
    wrapped[index, 72:80, :] = source[at : at + 8, :]


def load(place, z):
    ref, at = place
    return ref[pl.ds(at + z, 8), :]


def speed_loader(own_ref, rim_ref, first_row):
    def speed(component, index, z):
        row = (first_row + index) // 2
        ref, at = (own_ref, row) if 0 <= row < 2 else (rim_ref, 0 if row < 0 else 1)
        return ref[component, at, pl.ds(z, 8), :]

    return speed


def across(here, wrapped, index, z, speed_y, speed_z):
    after = roll_lanes(here, -1)
    before = roll_lanes(here, 1)
    mid = bent(before, here, after)
    shifts = [roll_lanes(mid, 2), roll_lanes(mid, 1), mid, roll_lanes(mid, -1), roll_lanes(mid, -2)]
    rate = upwind_part(*shifts, (after - before) * 0.5, speed_y)
    column = [wrapped[index, pl.ds(z + 8 + offset, 8), :] for offset in range(-3, 4)]
    column[3] = here
    column_bends = [bent(column[k - 1], column[k], column[k + 1]) for k in range(1, 6)]
    return rate + upwind_part(*column_bends, (column[4] - column[2]) * 0.5, speed_z)


def across_rows(places, speed, wrapped, rate_ref):
    for index, place in enumerate(places):
        fill_wrapped(wrapped, index, *place)

    def work(z):
        for index, place in enumerate(places):
            rate = across(load(place, z), wrapped, index, z, speed(1, index, z), speed(2, index, z))
            rate_ref[pl.ds(index * FINE + z, 8), :] = rate

    in_pairs(work)


def section(current, initial, speed, rates, wrapped, keep, blend, store):
    rows = len(rates)
    for index in range(rows):
        if rates[index] is None:
            fill_wrapped(wrapped, index, *current[index + 3])

    def work(z):
        values = [load(place, z) for place in current]
        steps = [values[k + 1] - values[k] for k in range(rows + 5)]
        bends = [steps[k + 1] - steps[k] for k in range(rows + 4)]
        squares = [value * value + WENO_EPS for value in bends]
        pairs = {}
        for index in range(rows):
            for k in range(index, index + 4):
                if k not in pairs:
                    pairs[k] = pair_terms(bends[k], bends[k + 1], squares[k], squares[k + 1])
            here = values[index + 3]
            slope = (steps[index + 3] + steps[index + 2]) * 0.5
            rate = upwind_pairs(*(pairs[k] for k in range(index, index + 4)), slope, speed(0, index, z))
            if rates[index] is None:
                rate = rate + across(here, wrapped, index, z, speed(1, index, z), speed(2, index, z))
            else:
                rate = rate + load(rates[index], z)
            moved = blend * (here - STEP_FINE * rate)
            if keep:
                moved = moved + keep * load(initial[index], z)
            store(index, z, moved)

    in_pairs(work)


def spread_speeds(stacked, speed_ref):
    source_lane = lax.broadcasted_iota(jnp.int32, (LANES, LANES), 0)
    fine_lane = lax.broadcasted_iota(jnp.int32, (LANES, LANES), 1)
    covered = jnp.logical_and(fine_lane >= 24, fine_lane < 104)
    for component in range(3):
        pick = jnp.logical_and(source_lane == SLOT * component + fine_lane // 2 - 12, covered)
        spread = exact_dot(stacked, jnp.where(pick, 1.0, 0.0))
        for row in range(2):
            part = spread[row * FLOW : (row + 1) * FLOW, :]
            speed_ref[component, row, pl.ds(0, FLOW, stride=2), :] = part
            speed_ref[component, row, pl.ds(1, FLOW, stride=2), :] = part


def in_pairs(work, parts=4):
    def body(step, carry):
        for part in range(parts):
            work(pl.multiple_of((step * parts + part) * 8, 8))
        return carry

    lax.fori_loop(0, 8 // parts, body, 0)


def centred(below, above):
    return (above - below) * 0.5


def planes(value):
    return pltpu.roll(value, FLOW - 1, 0), pltpu.roll(value, 1, 0)


def by_slot(lanes, first, second, third):
    return jnp.where(lanes < SLOT, first, jnp.where(lanes < 2 * SLOT, second, third))


def sweep(below, here, above, source):
    up, down = planes(here)
    beside = below + above + roll_lanes(here, 1) + roll_lanes(here, -1) + up + down
    return (source + IMPLICIT * beside) / (1.0 + 6.0 * IMPLICIT)


def inner_kernel(fixed_ref, speed_ref, rate_ref, wrapped):
    spread_speeds(fixed_ref[0:64, :], speed_ref)
    places = [(fixed_ref, 128 + FINE * row) for row in range(4)]
    across_rows(places, speed_loader(speed_ref, None, 0), wrapped, rate_ref)


def first_kernel(
    place_ref, fixed_ref, one_ref, two_ref, speed_ref, rate_ref, out_ref, send_ref, left_ref, right_ref, spare
):
    by_side(place_ref, one_ref, two_ref, left_ref, right_ref)
    moving = [
        left_ref[128:160, :],
        fixed_ref[0:32, :],
        fixed_ref[32:64, :],
        right_ref[128:160, :],
    ]
    lanes = lane_ids(FLOW)
    pressure = [
        sent_pressure(left_ref),
        fixed_ref[64:96, :],
        fixed_ref[96:128, :],
        sent_pressure(right_ref),
    ]
    pressure = [by_slot(lanes, p, roll_lanes(p, 40), roll_lanes(p, 80)) for p in pressure]
    for row in range(2):
        here, push = moving[row + 1], pressure[row + 1]
        back, further = roll_lanes(here, 88), roll_lanes(here, 40)
        along_x = by_slot(lanes, here, further, roll_lanes(here, 80))
        along_y = by_slot(lanes, back, here, further)
        along_z = by_slot(lanes, roll_lanes(here, 48), back, here)
        up, down = planes(here)
        push_up, push_down = planes(push)
        advect = -(
            along_x * centred(moving[row], moving[row + 2])
            + along_y * centred(roll_lanes(here, 1), roll_lanes(here, -1))
            + along_z * centred(down, up)
        )
        gradient = by_slot(
            lanes,
            centred(pressure[row], pressure[row + 2]),
            centred(roll_lanes(push, 1), roll_lanes(push, -1)),
            centred(push_down, push_up),
        )
        out_ref[256 + row * FLOW : 256 + (row + 1) * FLOW, :] = here + STEP_FLOW * (advect - gradient)

    spare[0:64, :] = unfolded(left_ref[0:64, :], left_ref[64:128, :])
    spare[64:128, :] = unfolded(right_ref[0:64, :], right_ref[64:128, :])
    places = (
        [(spare, 0), (left_ref, 0), (left_ref, 64)]
        + [(fixed_ref, 128 + FINE * row) for row in range(4)]
        + [(right_ref, 0), (right_ref, 64), (spare, 64)]
    )

    def store(index, z, value):
        out_ref[pl.ds(index * FINE + z, 8), :] = value

    rates = [(rate_ref, FINE * row) for row in range(4)]
    section(places, None, speed_loader(speed_ref, None, 0), rates, None, 0.0, 1.0, store)
    source = out_ref[256:320, :]
    send_ref[0:64, :], beside = folded(out_ref[0:64, :], out_ref[64:128, :], out_ref[192:256, :])
    send_ref[64:128, :] = lay(source, beside, 8, 24, -40)
    send_ref[128:192, :] = lay(source, out_ref[128:192, :], 104, 152, 104)
    send_ref[192:224, :] = lay(source[0:32, :], source[32:64, :], 0, 64, 64)


def middle_kernel(own_ref, old_left, old_right, speed_ref, rim_ref, rate_ref, wrapped):
    spread_speeds(jnp.concatenate([old_left[128:160, :], old_right[128:160, :]], axis=0), rim_ref)
    places = [(own_ref, FINE * row) for row in range(4)]
    across_rows(places, speed_loader(speed_ref, None, 0), wrapped, rate_ref)


def second_kernel(
    place_ref, own_ref, one_ref, two_ref, fixed_ref, old_left, old_right, speed_ref, rim_ref, rate_ref,
    out_ref, first_ref, second_ref, wrapped, spare, left_ref, right_ref, up_ref, down_ref,
):
    by_side(place_ref, one_ref, two_ref, left_ref, right_ref)
    source = [sent_source(left_ref, row) for row in range(2)]
    source += [own_ref[256 + row * FLOW : 256 + (row + 1) * FLOW, :] for row in range(2)]
    source += [sent_source(right_ref, row) for row in range(2)]
    out_ref[512:544, :], out_ref[544:576, :] = source[1], source[4]
    for row in range(4):
        done = sweep(source[row], source[row + 1], source[row + 2], source[row + 1])
        out_ref[384 + row * FLOW : 384 + (row + 1) * FLOW, :] = done
    spare[0:64, :] = unfolded(left_ref[0:64, :], left_ref[64:128, :])
    spare[64:128, :] = unfolded(right_ref[0:64, :], right_ref[64:128, :])
    places = (
        [(left_ref, FINE * row) for row in range(3)]
        + [(spare, 0)]
        + [(own_ref, FINE * row) for row in range(4)]
        + [(right_ref, FINE * row) for row in range(3)]
        + [(spare, 64)]
    )
    initial = [(old_left, 64)] + [(fixed_ref, 128 + FINE * row) for row in range(4)] + [(old_right, 0)]

    def store(index, z, value):
        out_ref[pl.ds(index * FINE + z, 8), :] = value

    rates = [None] + [(rate_ref, FINE * row) for row in range(4)] + [None]
    section(places, initial, speed_loader(speed_ref, rim_ref, -1), rates, wrapped, 0.75, 0.25, store)
    for to_ref, at in ((up_ref, 0), (down_ref, 128)):
        last = out_ref[at + 192 : at + 256, :]
        to_ref[0:64, :], beside = folded(out_ref[at : at + 64, :], out_ref[at + 64 : at + 128, :], last)
        done = out_ref[448:480, :] if at else out_ref[416:448, :]
        to_ref[64:96, :] = lay(done, beside[0:32, :], 8, 24, 40)
        to_ref[96:128, :] = lay(done, beside[32:64, :], 8, 16, 24)
        to_ref[128:160, :] = lay(done, out_ref[at + 128 : at + 160, :], 104, 152, 104)
        to_ref[160:192, :] = lay(done, out_ref[at + 160 : at + 192, :], 104, 152, 56)
    by_side(place_ref, down_ref, up_ref, first_ref, second_ref)


def late_kernel(own_ref, speed_ref, rim_ref, rate_ref, wrapped):
    places = [(own_ref, FINE * row) for row in range(6)]
    across_rows(places, speed_loader(speed_ref, rim_ref, -1), wrapped, rate_ref)


def third_kernel(
    place_ref, own_ref, one_ref, two_ref, older, fixed_ref, old_left, old_right,
    speed_ref, rim_ref, rate_ref,
    out_ref, wrapped, shaped, normal_x, normal_z, summed, spare, left_ref, right_ref,
):
    by_side(place_ref, one_ref, two_ref, left_ref, right_ref)
    spare[0:64, :] = unfolded(left_ref[0:64, :], left_ref[64:128, :])
    spare[64:128, :] = unfolded(right_ref[0:64, :], right_ref[64:128, :])
    places = (
        [(left_ref, FINE * row) for row in range(3)]
        + [(spare, 0)]
        + [(own_ref, FINE * row) for row in range(6)]
        + [(right_ref, FINE * row) for row in range(3)]
        + [(spare, 64)]
    )
    initial = (
        [(old_left, 0), (old_left, 64)]
        + [(fixed_ref, 128 + FINE * row) for row in range(4)]
        + [(old_right, 0), (old_right, 64)]
    )
    marks = [(old_left, 160)] * 2 + [(fixed_ref, 384)] * 4 + [(old_right, 160)] * 2

    def store(index, z, value):
        ref, at = initial[index]
        mark_ref, mark_at = marks[index]
        flag = mark_ref[pl.ds(mark_at + z // 8, 1), :]
        value = jnp.where(flag > 0.5, value, ref[pl.ds(at + z, 8), :]) * (1.0 / SHRINK)
        shaped[index, pl.ds(8 + z, 8), :] = value

    rates = [None] + [(rate_ref, FINE * row) for row in range(6)] + [None]
    section(places, initial, speed_loader(speed_ref, rim_ref, -2), rates, wrapped, 1.0 / 3.0, 2.0 / 3.0, store)
    for index, (mark_ref, mark_at) in enumerate(marks):
        at = mark_at + 8 + (index + 2) % 4
        phase = mark_ref[at : at + 1, :]
        inflow = jnp.where(phase == 2.0, SPREAD, jnp.where(phase == 1.0, -SPREAD, shaped[index, 8:9, :]))
        shaped[index, 8:9, :] = inflow
        shaped[index, 0:8, :] = shaped[index, 64:72, :]
        shaped[index, 72:80, :] = shaped[index, 8:16, :]

    def normals(z):
        middle = [shaped[k, pl.ds(8 + z, 8), :] for k in range(8)]
        for row in range(6):
            here = middle[row + 1]
            slope_x = (middle[row + 2] - middle[row]) * 0.5
            slope_y = (roll_lanes(here, -1) - roll_lanes(here, 1)) * 0.5
            slope_z = (shaped[row + 1, pl.ds(9 + z, 8), :] - shaped[row + 1, pl.ds(7 + z, 8), :]) * 0.5
            inverse = lax.rsqrt(slope_x * slope_x + slope_y * slope_y + slope_z * slope_z + 1.0)
            normal_x[row, pl.ds(z, 8), :] = slope_x * inverse
            if 0 < row < 5:
                wrapped[row, pl.ds(z, 8), :] = slope_y * inverse
                normal_z[row - 1, pl.ds(8 + z, 8), :] = slope_z * inverse

    in_pairs(normals)
    for row in range(4):
        normal_z[row, 0:8, :] = normal_z[row, 64:72, :]
        normal_z[row, 72:80, :] = normal_z[row, 8:16, :]

    def forces(z):
        for half in range(2):
            total = None
            for row in (2 * half, 2 * half + 1):
                level = shaped[row + 2, pl.ds(8 + z, 8), :]
                here_x = normal_x[row + 1, pl.ds(z, 8), :]
                here_y = wrapped[row + 1, pl.ds(z, 8), :]
                here_z = normal_z[row, pl.ds(8 + z, 8), :]
                curvature = (normal_x[row + 2, pl.ds(z, 8), :] - normal_x[row, pl.ds(z, 8), :]) * 0.5
                curvature = curvature + (roll_lanes(here_y, -1) - roll_lanes(here_y, 1)) * 0.5
                curvature = (
                    curvature + (normal_z[row, pl.ds(9 + z, 8), :] - normal_z[row, pl.ds(7 + z, 8), :]) * 0.5
                )
                delta = jnp.exp(level * level * (-1.0 / (2.0 * SPREAD * SPREAD))) * (1.0 / (SPREAD * 2.5066282746310002))
                strength = SURFACE * curvature * delta
                fraction = 0.5 + 0.5 * jnp.tanh(level * (1.0 / SPREAD))
                terms = (here_x * strength, here_y * strength, here_z * strength, fraction)
                total = terms if total is None else tuple(a + b for a, b in zip(total, terms))
            for component in range(4):
                summed[component, pl.ds(half * FINE + z, 8), :] = total[component]

    in_pairs(forces)

    source = [own_ref[512:544, :], older[256:288, :], older[288:320, :], own_ref[544:576, :]]
    once = [sent_sweep(left_ref)] + [own_ref[384 + row * FLOW : 384 + (row + 1) * FLOW, :] for row in range(4)]
    once = once + [sent_sweep(right_ref)]
    twice = [sweep(once[row], once[row + 1], once[row + 2], source[row]) for row in range(4)]
    thrice = [sweep(twice[row], twice[row + 1], twice[row + 2], source[row + 1]) for row in range(2)]

    source_lane = lax.broadcasted_iota(jnp.int32, (LANES, LANES), 0)
    out_lane = lax.broadcasted_iota(jnp.int32, (LANES, LANES), 1)
    part, column = out_lane // FLOW, out_lane % FLOW
    take = jnp.logical_and(source_lane == SLOT * part + 4 + column, part < 3)
    done = exact_dot(jnp.concatenate(thrice, axis=0), jnp.where(take, 1.0, 0.0))
    for component in range(4):
        take = jnp.logical_and((source_lane - 32) // 2 == column, part == component)
        take = jnp.logical_and(take, jnp.logical_and(source_lane >= 32, source_lane < 96))
        scale = 0.125 * STEP_FLOW if component < 3 else 0.125
        pairs = jnp.concatenate(
            [
                summed[component, pl.ds(half * FINE, FLOW, stride=2), :]
                + summed[component, pl.ds(half * FINE + 1, FLOW, stride=2), :]
                for half in range(2)
            ],
            axis=0,
        )
        done = done + exact_dot(pairs * scale, jnp.where(take, 1.0, 0.0))
    out_ref[...] = done


def sort_kernel(group_ref, own_ref, other_ref, keep_ref, send_ref):
    group = group_ref[0]
    lanes = lane_ids(64)
    beside = group + 1 - 2 * (group % 2)
    sorted_parts = []
    for target in (group, (group + 2) % 4):
        own = pltpu.roll(own_ref[...], (32 * group - 32 * target + LANES) % LANES, 1)
        other = pltpu.roll(other_ref[...], (32 * beside - 32 * target + LANES) % LANES, 1)
        sorted_parts.append(jnp.where(lanes // 32 == group, own, other))
    keep_ref[...], send = sorted_parts
    here = lane_ids(FLOW) // 64 == group // 2
    send_ref[...] = jnp.where(here, send[0:FLOW, :], roll_lanes(send[FLOW:64, :], 64))


def merge_kernel(group_ref, keep_ref, far_ref, out_ref):
    here = lane_ids(FLOW) // 64 == group_ref[0] // 2
    far = far_ref[...]
    for row, part in enumerate((far, roll_lanes(far, 64))):
        out_ref[:, row, :] = jnp.where(here, keep_ref[row * FLOW : (row + 1) * FLOW, :], part)


def call(kernel, outs, scratch, *args, scalars=0, outer=False, last=False):
    vmem = pl.BlockSpec(memory_space=pltpu.VMEM)
    smem = pl.BlockSpec(memory_space=pltpu.SMEM)
    shapes = [jax.ShapeDtypeStruct(shape, F32) if last else pltpu.VMEM(shape, F32) for shape in outs]
    held = list(args[scalars:])
    if not outer:
        held = [pltpu.with_memory_space_constraint(value, pltpu.VMEM) for value in held]
    return pl.pallas_call(
        kernel,
        out_shape=shapes if len(shapes) > 1 else shapes[0],
        in_specs=[smem] * scalars + [vmem] * len(held),
        out_specs=[vmem] * len(shapes) if len(shapes) > 1 else vmem,
        scratch_shapes=[pltpu.VMEM(shape, F32) for shape in scratch],
    )(*args[:scalars], *held)


def swapped(first, second):
    count = lax.axis_size("gx")
    near = [(i, i ^ 1) for i in range(count)]
    far = [(i, (i + (1 if i % 2 else -1)) % count) for i in range(count)]
    first = lax.ppermute(first, "gx", near)
    second = lax.ppermute(second, "gx", far)
    return first, second


def crossed(value, bit):
    return lax.ppermute(value, "grp", [(i, i ^ bit) for i in range(lax.axis_size("grp"))])


def to_next_blocks(value):
    blocks = lax.axis_size("gy")
    pairs = []
    for source, target, step in ((0, 0, 1), (1, 3, -1), (2, 2, -1), (3, 1, 1)):
        pairs += [(source * blocks + j, target * blocks + (j + step) % blocks) for j in range(blocks)]
    return lax.ppermute(value, ("grp", "gy"), pairs)


def on_device(flow_fields, level_set, band_tiles, nozzle_phase):
    group = lax.axis_index("grp").astype(jnp.int32)[None]
    place = lax.axis_index("gx").astype(jnp.int32)[None]
    raw, marks = call(
        pack_kernel,
        [(LEVEL + 8 * FINE, LANES), (2, 16, LANES)],
        [],
        flow_fields[0],
        level_set[0],
        band_tiles[:, 0, :],
        nozzle_phase,
        outer=True,
    )
    other = crossed(raw, 1)
    half, edge = call(split_kernel, [(256, LANES), (80, LANES)], [], group, raw, other, marks, scalars=1)
    half = call(join_kernel, [(336, LANES)], [], crossed(half, 2), to_next_blocks(edge))
    far_half = crossed(half, 1)
    fixed, first, second = call(
        assemble_kernel,
        [(400, LANES), (176, LANES), (176, LANES)],
        [(176, LANES), (176, LANES)],
        group,
        place,
        raw,
        other,
        marks,
        half,
        far_half,
        scalars=2,
    )
    speed_shape = (3, 2, FINE, LANES)
    first, second = swapped(first, second)
    speeds, rates = call(inner_kernel, [speed_shape, (256, LANES)], [(4, 80, LANES)], fixed)
    own, send, old_left, old_right = call(
        first_kernel,
        [(320, LANES), (224, LANES), (176, LANES), (176, LANES)],
        [(128, LANES)],
        place,
        fixed,
        first,
        second,
        speeds,
        rates,
        scalars=1,
    )
    first, second = swapped(send, send)
    rim, rates = call(
        middle_kernel, [speed_shape, (256, LANES)], [(4, 80, LANES)], own, old_left, old_right, speeds
    )
    newer, first, second = call(
        second_kernel,
        [(576, LANES), (192, LANES), (192, LANES)],
        [(6, 80, LANES), (128, LANES), (224, LANES), (224, LANES), (192, LANES), (192, LANES)],
        place,
        own,
        first,
        second,
        fixed,
        old_left,
        old_right,
        speeds,
        rim,
        rates,
        scalars=1,
    )
    first, second = swapped(first, second)
    rates = call(late_kernel, [(384, LANES)], [(6, 80, LANES)], newer, speeds, rim)
    result = call(
        third_kernel,
        [(64, LANES)],
        [
            (8, 80, LANES),
            (8, 80, LANES),
            (6, FINE, LANES),
            (4, 80, LANES),
            (4, 2 * FINE, LANES),
            (128, LANES),
            (192, LANES),
            (192, LANES),
        ],
        place,
        newer,
        first,
        second,
        own,
        fixed,
        old_left,
        old_right,
        speeds,
        rim,
        rates,
        scalars=1,
    )
    keep, send = call(
        sort_kernel, [(64, LANES), (FLOW, LANES)], [], group, result, crossed(result, 1), scalars=1
    )
    return call(merge_kernel, [(FLOW, 2, LANES)], [], group, keep, crossed(send, 2), scalars=1, last=True)[None]


def solution(mesh):
    placed = (
        P("grp", None, "gx", "gy"),
        P("grp", None, "gx", "gy"),
        P(None, "gx", "gy"),
        P("gx", "gy"),
    )
    return jax.shard_map(
        on_device, mesh=mesh, in_specs=placed, out_specs=P("grp", None, "gx", "gy"), check_vma=False
    )
```

```python
import jax
import jax.numpy as jnp
from jax import lax
from jax.experimental import pallas as pl
from jax.experimental.pallas import tpu as pltpu
from jax.sharding import PartitionSpec as P


LANES = 128
FINE = 64
FLOW = 32
SLOT = 40
LEVEL = 64
SHRINK = 0.25
WENO_EPS = 1e-06 * SHRINK * SHRINK
STEP_FINE = 0.3
STEP_FLOW = 0.2
SURFACE = 6.0
SPREAD = 1.5
IMPLICIT = 0.5
F32 = jnp.float32


def lane_ids(rows):
    return lax.broadcasted_iota(jnp.int32, (rows, LANES), 1)


def roll_lanes(value, shift):
    return pltpu.roll(value, shift % LANES, 1)


def exact_dot(left, right):
    return jnp.dot(left, right, precision=lax.Precision.HIGHEST, preferred_element_type=F32)


def folded(first, second, last):
    lanes = lane_ids(FINE)
    inside = jnp.logical_and(lanes >= 24, lanes < 104)
    return jnp.where(inside, first, roll_lanes(last, 80)), jnp.where(inside, second, roll_lanes(last, 32))


def unfolded(first, second):
    return jnp.where(lane_ids(FINE) < 72, roll_lanes(first, -80), roll_lanes(second, -32))


def lay(value, base, first, last, shift):
    lanes = lane_ids(value.shape[0])
    inside = jnp.logical_and(lanes >= first, lanes < last)
    if last > LANES:
        inside = jnp.logical_or(lanes >= first, lanes < last - LANES)
    return jnp.where(inside, roll_lanes(value, shift), base)


def parted(limits, parts):
    lanes = lane_ids(parts[0].shape[0])
    value = parts[-1]
    for limit, part in reversed(list(zip(limits, parts))):
        value = jnp.where(lanes < limit, part, value)
    return value


def sent_pressure(ref):
    return parted((16, 32), (roll_lanes(ref[64:96, :], -8), roll_lanes(ref[96:128, :], 8), roll_lanes(ref[128:160, :], -88)))


def sent_source(ref, row):
    at = row * FLOW
    rest = ref[192:224, :]
    return parted(
        (48, 64),
        (
            roll_lanes(ref[128 + at : 160 + at, :], -104),
            roll_lanes(ref[64 + at : 96 + at, :], 40),
            rest if row else roll_lanes(rest, 64),
        ),
    )


def sent_sweep(ref):
    return parted(
        (48, 96, 112),
        (
            roll_lanes(ref[128:160, :], -104),
            roll_lanes(ref[160:192, :], -56),
            roll_lanes(ref[64:96, :], -40),
            roll_lanes(ref[96:128, :], -24),
        ),
    )


def by_side(place_ref, first_ref, second_ref, left_ref, right_ref):
    odd = place_ref[0] % 2 == 1

    @pl.when(odd)
    def _():
        left_ref[...] = first_ref[...]
        right_ref[...] = second_ref[...]

    @pl.when(jnp.logical_not(odd))
    def _():
        left_ref[...] = second_ref[...]
        right_ref[...] = first_ref[...]


def pack_kernel(flow_ref, level_ref, band_ref, nozzle_ref, raw_ref, mark_ref):
    for row in range(2):
        raw_ref[row * FLOW : (row + 1) * FLOW, :] = flow_ref[:, row, :]
    for row in range(4):
        block = level_ref[:, row, :] * SHRINK
        raw_ref[LEVEL + row * FINE : LEVEL + (row + 1) * FINE, :] = block[:, :LANES]
        raw_ref[LEVEL + (row + 4) * FINE : LEVEL + (row + 5) * FINE, :] = block[:, LANES:]
    spread_tiles = jnp.where(
        lax.broadcasted_iota(jnp.int32, (16, 256), 1) // 16 == lax.broadcasted_iota(jnp.int32, (16, 256), 0), 1.0, 0.0
    )
    flags = exact_dot(band_ref[...].astype(F32), spread_tiles)
    phases = nozzle_ref[...].astype(F32)
    for half in range(2):
        part = slice(half * LANES, (half + 1) * LANES)
        mark_ref[half, 0:8, :] = flags[:, part]
        mark_ref[half, 8:12, :] = phases[:, part]
        mark_ref[half, 12:16, :] = jnp.zeros((4, LANES), F32)


def level_rows(ref, tile, row):
    at = LEVEL + (4 * tile + row) * FINE
    return ref[at : at + FINE, :]


def split_kernel(group_ref, raw_ref, other_ref, mark_ref, half_ref, edge_ref):
    group = group_ref[0]
    lanes = lane_ids(FINE)
    half_ref[0:64, :] = raw_ref[0:64, :]

    for core in range(2):
        level, (lower, upper) = (
            (raw_ref, (other_ref, raw_ref)) if core else (other_ref, (raw_ref, other_ref))
        )

        @pl.when(group % 2 == core)
        def _(core=core, level=level, lower=lower, upper=upper):
            for row in range(2):
                half_ref[64 + row * FINE : 64 + (row + 1) * FINE, :] = level_rows(level, 0, 2 * core + row)
            beyond = level_rows(level, 1, 0)
            for row in range(1, 4):
                beyond = jnp.where(lanes < 16 * row, beyond, roll_lanes(level_rows(level, 1, row), 16 * row))
            half_ref[192:256, :] = beyond

            def edges(tile, level_start, field_start):
                packed = roll_lanes(level_rows(level, tile, 0), -level_start)
                for row in range(1, 4):
                    turned = roll_lanes(level_rows(level, tile, row), 16 * row - level_start)
                    packed = jnp.where(lanes < 16 * row, packed, turned)
                packed = jnp.where(lanes < 64, packed, roll_lanes(lower[0:64, :], 64 - field_start))
                packed = jnp.where(lanes < 72, packed, roll_lanes(upper[0:64, :], 72 - field_start))
                edge_ref[0:64, :] = packed
                edge_ref[64:80, :] = mark_ref[tile]

            ahead = jnp.logical_or(group == 0, group == 3)

            @pl.when(ahead)
            def _():
                edges(1, 112, 120)

            @pl.when(jnp.logical_not(ahead))
            def _():
                edges(0, 0, 0)


def join_kernel(half_ref, edge_ref, out_ref):
    out_ref[0:256, :] = half_ref[...]
    out_ref[256:336, :] = edge_ref[...]


def assemble_kernel(
    group_ref, place_ref, raw_ref, other_ref, mark_ref, half_ref, far_half_ref,
    fixed_ref, first_ref, second_ref, up_ref, down_ref,
):
    group = group_ref[0]
    lanes = lane_ids(64)

    def assemble(own):
        core, first, last = own % 2, own == 0, own == 3
        local = (raw_ref, other_ref) if core == 0 else (other_ref, raw_ref)
        remote = (half_ref, far_half_ref) if core == 0 else (far_half_ref, half_ref)
        fields = [ref[0:64, :] for ref in ((*local, *remote) if own < 2 else (*remote, *local))]
        near, far = half_ref[256:320, :], far_half_ref[256:320, :]

        def placed(index, lane):
            value = roll_lanes(fields[index], lane + 4 - 32 * own)
            edge = (near, near, far, far)[index]
            source = 64 + 8 * (index % 2)
            if first:
                value = jnp.where(lanes < lane + 4, roll_lanes(edge, lane - source - 4), value)
            if last:
                value = jnp.where(lanes >= lane + 36, roll_lanes(edge, lane + 36 - source), value)
            return value

        parts = [placed(index, SLOT * index) for index in range(3)]
        moving = by_slot(lanes, *parts)
        pressure = placed(3, 0)
        fixed_ref[0:64, :] = moving
        fixed_ref[64:128, :] = pressure
        level_tiles = []
        for row in range(4):
            if own < 2:
                low = remote[row // 2][64 + (row % 2) * FINE : 64 + (row % 2 + 1) * FINE, :]
                high = roll_lanes(far_half_ref[192:256, :] if core == 0 else half_ref[192:256, :], -16 * row)
            else:
                level = raw_ref if core else other_ref
                low, high = level_rows(level, 0, row), level_rows(level, 1, row)
            value = {
                0: lambda: jnp.where(lanes < 32, roll_lanes(far, 16 - 16 * row), roll_lanes(low, 32)),
                1: lambda: roll_lanes(jnp.where(lanes < 32, high, low), 96),
                2: lambda: roll_lanes(jnp.where(lanes < 96, high, low), 32),
                3: lambda: jnp.where(lanes < 96, roll_lanes(high, 96), roll_lanes(far, 96 - 16 * row)),
            }[own]()
            fixed_ref[128 + row * FINE : 128 + (row + 1) * FINE, :] = value
            level_tiles.append(value)
        for out_ref, (near, next_row, far_row) in ((up_ref, (2, 3, 1)), (down_ref, (0, 1, 2))):
            pair = folded(level_tiles[near], level_tiles[next_row], level_tiles[far_row])
            out_ref[0:64, :] = pair[0]
            row = 1 if near else 0
            push = pressure[row * FLOW : (row + 1) * FLOW, :]
            out_ref[64:96, :] = lay(push, pair[1][0:32, :], 8, 24, 8)
            out_ref[96:128, :] = lay(push, pair[1][32:64, :], 8, 24, -8)
            out_ref[128:160, :] = lay(push, moving[row * FLOW : (row + 1) * FLOW, :], 120, 128, 88)
        low, high, beside, few = mark_ref[0], mark_ref[1], half_ref[320:336, :], lane_ids(16)
        marks = {
            0: lambda: roll_lanes(jnp.where(few < 96, low, beside), 32),
            1: lambda: roll_lanes(jnp.where(few < 32, high, low), 96),
            2: lambda: roll_lanes(jnp.where(few < 96, high, low), 32),
            3: lambda: roll_lanes(jnp.where(few < 32, beside, high), 96),
        }[own]()
        fixed_ref[384:400, :] = marks
        for out_ref in (up_ref, down_ref):
            out_ref[160:176, :] = marks

    for own in range(4):

        @pl.when(group == own)
        def _(own=own):
            assemble(own)

    by_side(place_ref, down_ref, up_ref, first_ref, second_ref)


def bent(below, here, above):
    return (above - here) - (here - below)


def mixed(smooth_one, smooth_two, smooth_three, curve_one, curve_two, curve_three):
    both_three = smooth_one * smooth_two
    both_two = smooth_one * smooth_three
    both_one = smooth_two * smooth_three
    one = both_one * both_one
    three = both_three * both_three
    bottom = (one + 6.0 * (both_two * both_two)) + 3.0 * three
    top = one * ((curve_one - curve_two) * (1.0 / 3.0)) + three * ((curve_two - curve_three) * 0.5)
    return top / bottom - curve_two * (1.0 / 6.0)


THIRDS = 4.0 / 3.0


def upwind_part(far_low, low, mid, high, far_high, slope, speed):
    ahead = speed >= 0.0
    one = jnp.where(ahead, far_low, far_high)
    two = jnp.where(ahead, low, high)
    four = jnp.where(ahead, high, low)
    curve_one = two - one
    curve_two = mid - two
    curve_three = four - mid
    smooth_one = (two * two + WENO_EPS) + curve_one * (THIRDS * curve_one + two)
    smooth_two = (two * mid + WENO_EPS) + THIRDS * (curve_two * curve_two)
    smooth_three = (mid * mid + WENO_EPS) + curve_three * (THIRDS * curve_three - mid)
    rest = mixed(smooth_one, smooth_two, smooth_three, curve_one, curve_two, curve_three)
    return speed * slope + jnp.abs(speed) * rest


def pair_terms(low, high, low_square, high_square):
    change = high - low
    wide = THIRDS * change
    rising = high_square + change * (wide + high)
    falling = low_square + change * (wide - low)
    level = (low * high + WENO_EPS) + change * wide
    return change, rising, falling, level


def upwind_pairs(one, two, three, four, slope, speed):
    ahead = speed >= 0.0
    rest = mixed(
        jnp.where(ahead, one[1], four[2]),
        jnp.where(ahead, two[3], three[3]),
        jnp.where(ahead, three[2], two[1]),
        jnp.where(ahead, one[0], four[0]),
        jnp.where(ahead, two[0], three[0]),
        jnp.where(ahead, three[0], two[0]),
    )
    return speed * (slope + rest)


def fill_wrapped(wrapped, index, source, at):
    wrapped[index, 8:72, :] = source[at : at + FINE, :]
    wrapped[index, 0:8, :] = source[at + 56 : at + 64, :]
    wrapped[index, 72:80, :] = source[at : at + 8, :]


def load(place, z):
    ref, at = place
    return ref[pl.ds(at + z, 8), :]


def speed_loader(own_ref, rim_ref, first_row):
    def speed(component, index, z):
        row = (first_row + index) // 2
        ref, at = (own_ref, row) if 0 <= row < 2 else (rim_ref, 0 if row < 0 else 1)
        return ref[component, at, pl.ds(z, 8), :]

    return speed


def across(here, wrapped, index, z, speed_y, speed_z):
    after = roll_lanes(here, -1)
    before = roll_lanes(here, 1)
    mid = bent(before, here, after)
    shifts = [roll_lanes(mid, 2), roll_lanes(mid, 1), mid, roll_lanes(mid, -1), roll_lanes(mid, -2)]
    rate = upwind_part(*shifts, (after - before) * 0.5, speed_y)
    column = [wrapped[index, pl.ds(z + 8 + offset, 8), :] for offset in range(-3, 4)]
    column[3] = here
    column_bends = [bent(column[k - 1], column[k], column[k + 1]) for k in range(1, 6)]
    return rate + upwind_part(*column_bends, (column[4] - column[2]) * 0.5, speed_z)


def across_rows(places, speed, wrapped, rate_ref):
    for index, place in enumerate(places):
        fill_wrapped(wrapped, index, *place)

    def work(z):
        for index, place in enumerate(places):
            rate = across(load(place, z), wrapped, index, z, speed(1, index, z), speed(2, index, z))
            rate_ref[pl.ds(index * FINE + z, 8), :] = rate

    in_pairs(work)


def section(current, initial, speed, rates, wrapped, keep, blend, store):
    rows = len(rates)
    for index in range(rows):
        if rates[index] is None:
            fill_wrapped(wrapped, index, *current[index + 3])

    def work(z):
        values = [load(place, z) for place in current]
        steps = [values[k + 1] - values[k] for k in range(rows + 5)]
        bends = [steps[k + 1] - steps[k] for k in range(rows + 4)]
        squares = [value * value + WENO_EPS for value in bends]
        pairs = {}
        for index in range(rows):
            for k in range(index, index + 4):
                if k not in pairs:
                    pairs[k] = pair_terms(bends[k], bends[k + 1], squares[k], squares[k + 1])
            here = values[index + 3]
            slope = (steps[index + 3] + steps[index + 2]) * 0.5
            rate = upwind_pairs(*(pairs[k] for k in range(index, index + 4)), slope, speed(0, index, z))
            if rates[index] is None:
                rate = rate + across(here, wrapped, index, z, speed(1, index, z), speed(2, index, z))
            else:
                rate = rate + load(rates[index], z)
            moved = blend * (here - STEP_FINE * rate)
            if keep:
                moved = moved + keep * load(initial[index], z)
            store(index, z, moved)

    in_pairs(work)


def spread_speeds(stacked, speed_ref):
    source_lane = lax.broadcasted_iota(jnp.int32, (LANES, LANES), 0)
    fine_lane = lax.broadcasted_iota(jnp.int32, (LANES, LANES), 1)
    covered = jnp.logical_and(fine_lane >= 24, fine_lane < 104)
    for component in range(3):
        pick = jnp.logical_and(source_lane == SLOT * component + fine_lane // 2 - 12, covered)
        spread = exact_dot(stacked, jnp.where(pick, 1.0, 0.0))
        for row in range(2):
            part = spread[row * FLOW : (row + 1) * FLOW, :]
            speed_ref[component, row, pl.ds(0, FLOW, stride=2), :] = part
            speed_ref[component, row, pl.ds(1, FLOW, stride=2), :] = part


def in_pairs(work):
    for part in range(8):
        work(part * 8)


def centred(below, above):
    return (above - below) * 0.5


def planes(value):
    return pltpu.roll(value, FLOW - 1, 0), pltpu.roll(value, 1, 0)


def by_slot(lanes, first, second, third):
    return jnp.where(lanes < SLOT, first, jnp.where(lanes < 2 * SLOT, second, third))


def sweep(below, here, above, source):
    up, down = planes(here)
    beside = below + above + roll_lanes(here, 1) + roll_lanes(here, -1) + up + down
    return (source + IMPLICIT * beside) / (1.0 + 6.0 * IMPLICIT)


def inner_kernel(fixed_ref, speed_ref, rate_ref, wrapped):
    spread_speeds(fixed_ref[0:64, :], speed_ref)
    places = [(fixed_ref, 128 + FINE * row) for row in range(4)]
    across_rows(places, speed_loader(speed_ref, None, 0), wrapped, rate_ref)


def first_kernel(
    place_ref, fixed_ref, one_ref, two_ref, speed_ref, rate_ref, out_ref, send_ref, left_ref, right_ref, spare
):
    by_side(place_ref, one_ref, two_ref, left_ref, right_ref)
    moving = [
        left_ref[128:160, :],
        fixed_ref[0:32, :],
        fixed_ref[32:64, :],
        right_ref[128:160, :],
    ]
    lanes = lane_ids(FLOW)
    pressure = [
        sent_pressure(left_ref),
        fixed_ref[64:96, :],
        fixed_ref[96:128, :],
        sent_pressure(right_ref),
    ]
    pressure = [by_slot(lanes, p, roll_lanes(p, 40), roll_lanes(p, 80)) for p in pressure]
    for row in range(2):
        here, push = moving[row + 1], pressure[row + 1]
        back, further = roll_lanes(here, 88), roll_lanes(here, 40)
        along_x = by_slot(lanes, here, further, roll_lanes(here, 80))
        along_y = by_slot(lanes, back, here, further)
        along_z = by_slot(lanes, roll_lanes(here, 48), back, here)
        up, down = planes(here)
        push_up, push_down = planes(push)
        advect = -(
            along_x * centred(moving[row], moving[row + 2])
            + along_y * centred(roll_lanes(here, 1), roll_lanes(here, -1))
            + along_z * centred(down, up)
        )
        gradient = by_slot(
            lanes,
            centred(pressure[row], pressure[row + 2]),
            centred(roll_lanes(push, 1), roll_lanes(push, -1)),
            centred(push_down, push_up),
        )
        out_ref[256 + row * FLOW : 256 + (row + 1) * FLOW, :] = here + STEP_FLOW * (advect - gradient)

    spare[0:64, :] = unfolded(left_ref[0:64, :], left_ref[64:128, :])
    spare[64:128, :] = unfolded(right_ref[0:64, :], right_ref[64:128, :])
    places = (
        [(spare, 0), (left_ref, 0), (left_ref, 64)]
        + [(fixed_ref, 128 + FINE * row) for row in range(4)]
        + [(right_ref, 0), (right_ref, 64), (spare, 64)]
    )

    def store(index, z, value):
        out_ref[pl.ds(index * FINE + z, 8), :] = value

    rates = [(rate_ref, FINE * row) for row in range(4)]
    section(places, None, speed_loader(speed_ref, None, 0), rates, None, 0.0, 1.0, store)
    source = out_ref[256:320, :]
    send_ref[0:64, :], beside = folded(out_ref[0:64, :], out_ref[64:128, :], out_ref[192:256, :])
    send_ref[64:128, :] = lay(source, beside, 8, 24, -40)
    send_ref[128:192, :] = lay(source, out_ref[128:192, :], 104, 152, 104)
    send_ref[192:224, :] = lay(source[0:32, :], source[32:64, :], 0, 64, 64)


def middle_kernel(own_ref, old_left, old_right, speed_ref, rim_ref, rate_ref, wrapped):
    spread_speeds(jnp.concatenate([old_left[128:160, :], old_right[128:160, :]], axis=0), rim_ref)
    places = [(own_ref, FINE * row) for row in range(4)]
    across_rows(places, speed_loader(speed_ref, None, 0), wrapped, rate_ref)


def second_kernel(
    place_ref, own_ref, one_ref, two_ref, fixed_ref, old_left, old_right, speed_ref, rim_ref, rate_ref,
    out_ref, first_ref, second_ref, wrapped, spare, left_ref, right_ref, up_ref, down_ref,
):
    by_side(place_ref, one_ref, two_ref, left_ref, right_ref)
    source = [sent_source(left_ref, row) for row in range(2)]
    source += [own_ref[256 + row * FLOW : 256 + (row + 1) * FLOW, :] for row in range(2)]
    source += [sent_source(right_ref, row) for row in range(2)]
    out_ref[512:544, :], out_ref[544:576, :] = source[1], source[4]
    for row in range(4):
        done = sweep(source[row], source[row + 1], source[row + 2], source[row + 1])
        out_ref[384 + row * FLOW : 384 + (row + 1) * FLOW, :] = done
    spare[0:64, :] = unfolded(left_ref[0:64, :], left_ref[64:128, :])
    spare[64:128, :] = unfolded(right_ref[0:64, :], right_ref[64:128, :])
    places = (
        [(left_ref, FINE * row) for row in range(3)]
        + [(spare, 0)]
        + [(own_ref, FINE * row) for row in range(4)]
        + [(right_ref, FINE * row) for row in range(3)]
        + [(spare, 64)]
    )
    initial = [(old_left, 64)] + [(fixed_ref, 128 + FINE * row) for row in range(4)] + [(old_right, 0)]

    def store(index, z, value):
        out_ref[pl.ds(index * FINE + z, 8), :] = value

    rates = [None] + [(rate_ref, FINE * row) for row in range(4)] + [None]
    section(places, initial, speed_loader(speed_ref, rim_ref, -1), rates, wrapped, 0.75, 0.25, store)
    for to_ref, at in ((up_ref, 0), (down_ref, 128)):
        last = out_ref[at + 192 : at + 256, :]
        to_ref[0:64, :], beside = folded(out_ref[at : at + 64, :], out_ref[at + 64 : at + 128, :], last)
        done = out_ref[448:480, :] if at else out_ref[416:448, :]
        to_ref[64:96, :] = lay(done, beside[0:32, :], 8, 24, 40)
        to_ref[96:128, :] = lay(done, beside[32:64, :], 8, 16, 24)
        to_ref[128:160, :] = lay(done, out_ref[at + 128 : at + 160, :], 104, 152, 104)
        to_ref[160:192, :] = lay(done, out_ref[at + 160 : at + 192, :], 104, 152, 56)
    by_side(place_ref, down_ref, up_ref, first_ref, second_ref)


def late_kernel(own_ref, speed_ref, rim_ref, rate_ref, wrapped):
    places = [(own_ref, FINE * row) for row in range(6)]
    across_rows(places, speed_loader(speed_ref, rim_ref, -1), wrapped, rate_ref)


def third_kernel(
    place_ref, own_ref, one_ref, two_ref, older, fixed_ref, old_left, old_right,
    speed_ref, rim_ref, rate_ref,
    out_ref, wrapped, shaped, normal_x, normal_z, summed, spare, left_ref, right_ref,
):
    by_side(place_ref, one_ref, two_ref, left_ref, right_ref)
    spare[0:64, :] = unfolded(left_ref[0:64, :], left_ref[64:128, :])
    spare[64:128, :] = unfolded(right_ref[0:64, :], right_ref[64:128, :])
    places = (
        [(left_ref, FINE * row) for row in range(3)]
        + [(spare, 0)]
        + [(own_ref, FINE * row) for row in range(6)]
        + [(right_ref, FINE * row) for row in range(3)]
        + [(spare, 64)]
    )
    initial = (
        [(old_left, 0), (old_left, 64)]
        + [(fixed_ref, 128 + FINE * row) for row in range(4)]
        + [(old_right, 0), (old_right, 64)]
    )
    marks = [(old_left, 160)] * 2 + [(fixed_ref, 384)] * 4 + [(old_right, 160)] * 2

    def store(index, z, value):
        ref, at = initial[index]
        mark_ref, mark_at = marks[index]
        flag = mark_ref[pl.ds(mark_at + z // 8, 1), :]
        value = jnp.where(flag > 0.5, value, ref[pl.ds(at + z, 8), :]) * (1.0 / SHRINK)
        shaped[index, pl.ds(8 + z, 8), :] = value

    rates = [None] + [(rate_ref, FINE * row) for row in range(6)] + [None]
    section(places, initial, speed_loader(speed_ref, rim_ref, -2), rates, wrapped, 1.0 / 3.0, 2.0 / 3.0, store)
    for index, (mark_ref, mark_at) in enumerate(marks):
        at = mark_at + 8 + (index + 2) % 4
        phase = mark_ref[at : at + 1, :]
        inflow = jnp.where(phase == 2.0, SPREAD, jnp.where(phase == 1.0, -SPREAD, shaped[index, 8:9, :]))
        shaped[index, 8:9, :] = inflow
        shaped[index, 0:8, :] = shaped[index, 64:72, :]
        shaped[index, 72:80, :] = shaped[index, 8:16, :]

    def normals(z):
        middle = [shaped[k, pl.ds(8 + z, 8), :] for k in range(8)]
        for row in range(6):
            here = middle[row + 1]
            slope_x = (middle[row + 2] - middle[row]) * 0.5
            slope_y = (roll_lanes(here, -1) - roll_lanes(here, 1)) * 0.5
            slope_z = (shaped[row + 1, pl.ds(9 + z, 8), :] - shaped[row + 1, pl.ds(7 + z, 8), :]) * 0.5
            inverse = lax.rsqrt(slope_x * slope_x + slope_y * slope_y + slope_z * slope_z + 1.0)
            normal_x[row, pl.ds(z, 8), :] = slope_x * inverse
            if 0 < row < 5:
                wrapped[row, pl.ds(z, 8), :] = slope_y * inverse
                normal_z[row - 1, pl.ds(8 + z, 8), :] = slope_z * inverse

    in_pairs(normals)
    for row in range(4):
        normal_z[row, 0:8, :] = normal_z[row, 64:72, :]
        normal_z[row, 72:80, :] = normal_z[row, 8:16, :]

    def forces(z):
        for half in range(2):
            total = None
            for row in (2 * half, 2 * half + 1):
                level = shaped[row + 2, pl.ds(8 + z, 8), :]
                here_x = normal_x[row + 1, pl.ds(z, 8), :]
                here_y = wrapped[row + 1, pl.ds(z, 8), :]
                here_z = normal_z[row, pl.ds(8 + z, 8), :]
                curvature = (normal_x[row + 2, pl.ds(z, 8), :] - normal_x[row, pl.ds(z, 8), :]) * 0.5
                curvature = curvature + (roll_lanes(here_y, -1) - roll_lanes(here_y, 1)) * 0.5
                curvature = (
                    curvature + (normal_z[row, pl.ds(9 + z, 8), :] - normal_z[row, pl.ds(7 + z, 8), :]) * 0.5
                )
                delta = jnp.exp(level * level * (-1.0 / (2.0 * SPREAD * SPREAD))) * (1.0 / (SPREAD * 2.5066282746310002))
                strength = SURFACE * curvature * delta
                fraction = 0.5 + 0.5 * jnp.tanh(level * (1.0 / SPREAD))
                terms = (here_x * strength, here_y * strength, here_z * strength, fraction)
                total = terms if total is None else tuple(a + b for a, b in zip(total, terms))
            for component in range(4):
                summed[component, pl.ds(half * FINE + z, 8), :] = total[component]

    in_pairs(forces)

    source = [own_ref[512:544, :], older[256:288, :], older[288:320, :], own_ref[544:576, :]]
    once = [sent_sweep(left_ref)] + [own_ref[384 + row * FLOW : 384 + (row + 1) * FLOW, :] for row in range(4)]
    once = once + [sent_sweep(right_ref)]
    twice = [sweep(once[row], once[row + 1], once[row + 2], source[row]) for row in range(4)]
    thrice = [sweep(twice[row], twice[row + 1], twice[row + 2], source[row + 1]) for row in range(2)]

    source_lane = lax.broadcasted_iota(jnp.int32, (LANES, LANES), 0)
    out_lane = lax.broadcasted_iota(jnp.int32, (LANES, LANES), 1)
    part, column = out_lane // FLOW, out_lane % FLOW
    take = jnp.logical_and(source_lane == SLOT * part + 4 + column, part < 3)
    done = exact_dot(jnp.concatenate(thrice, axis=0), jnp.where(take, 1.0, 0.0))
    for component in range(4):
        take = jnp.logical_and((source_lane - 32) // 2 == column, part == component)
        take = jnp.logical_and(take, jnp.logical_and(source_lane >= 32, source_lane < 96))
        scale = 0.125 * STEP_FLOW if component < 3 else 0.125
        pairs = jnp.concatenate(
            [
                summed[component, pl.ds(half * FINE, FLOW, stride=2), :]
                + summed[component, pl.ds(half * FINE + 1, FLOW, stride=2), :]
                for half in range(2)
            ],
            axis=0,
        )
        done = done + exact_dot(pairs * scale, jnp.where(take, 1.0, 0.0))
    out_ref[...] = done


def sort_kernel(group_ref, own_ref, other_ref, keep_ref, send_ref):
    group = group_ref[0]
    lanes = lane_ids(64)
    beside = group + 1 - 2 * (group % 2)
    sorted_parts = []
    for target in (group, (group + 2) % 4):
        own = pltpu.roll(own_ref[...], (32 * group - 32 * target + LANES) % LANES, 1)
        other = pltpu.roll(other_ref[...], (32 * beside - 32 * target + LANES) % LANES, 1)
        sorted_parts.append(jnp.where(lanes // 32 == group, own, other))
    keep_ref[...], send = sorted_parts
    here = lane_ids(FLOW) // 64 == group // 2
    send_ref[...] = jnp.where(here, send[0:FLOW, :], roll_lanes(send[FLOW:64, :], 64))


def merge_kernel(group_ref, keep_ref, far_ref, out_ref):
    here = lane_ids(FLOW) // 64 == group_ref[0] // 2
    far = far_ref[...]
    for row, part in enumerate((far, roll_lanes(far, 64))):
        out_ref[:, row, :] = jnp.where(here, keep_ref[row * FLOW : (row + 1) * FLOW, :], part)


def call(kernel, outs, scratch, *args, scalars=0, outer=False, last=False):
    vmem = pl.BlockSpec(memory_space=pltpu.VMEM)
    smem = pl.BlockSpec(memory_space=pltpu.SMEM)
    shapes = [jax.ShapeDtypeStruct(shape, F32) if last else pltpu.VMEM(shape, F32) for shape in outs]
    held = list(args[scalars:])
    if not outer:
        held = [pltpu.with_memory_space_constraint(value, pltpu.VMEM) for value in held]
    return pl.pallas_call(
        kernel,
        out_shape=shapes if len(shapes) > 1 else shapes[0],
        in_specs=[smem] * scalars + [vmem] * len(held),
        out_specs=[vmem] * len(shapes) if len(shapes) > 1 else vmem,
        scratch_shapes=[pltpu.VMEM(shape, F32) for shape in scratch],
    )(*args[:scalars], *held)


def swapped(first, second):
    count = lax.axis_size("gx")
    near = [(i, i ^ 1) for i in range(count)]
    far = [(i, (i + (1 if i % 2 else -1)) % count) for i in range(count)]
    first = lax.ppermute(first, "gx", near)
    second = lax.ppermute(second, "gx", far)
    return first, second


def crossed(value, bit):
    return lax.ppermute(value, "grp", [(i, i ^ bit) for i in range(lax.axis_size("grp"))])


def to_next_blocks(value):
    blocks = lax.axis_size("gy")
    pairs = []
    for source, target, step in ((0, 0, 1), (1, 3, -1), (2, 2, -1), (3, 1, 1)):
        pairs += [(source * blocks + j, target * blocks + (j + step) % blocks) for j in range(blocks)]
    return lax.ppermute(value, ("grp", "gy"), pairs)


def on_device(flow_fields, level_set, band_tiles, nozzle_phase):
    group = lax.axis_index("grp").astype(jnp.int32)[None]
    place = lax.axis_index("gx").astype(jnp.int32)[None]
    raw, marks = call(
        pack_kernel,
        [(LEVEL + 8 * FINE, LANES), (2, 16, LANES)],
        [],
        flow_fields[0],
        level_set[0],
        band_tiles[:, 0, :],
        nozzle_phase,
        outer=True,
    )
    other = crossed(raw, 1)
    half, edge = call(split_kernel, [(256, LANES), (80, LANES)], [], group, raw, other, marks, scalars=1)
    half = call(join_kernel, [(336, LANES)], [], crossed(half, 2), to_next_blocks(edge))
    far_half = crossed(half, 1)
    fixed, first, second = call(
        assemble_kernel,
        [(400, LANES), (176, LANES), (176, LANES)],
        [(176, LANES), (176, LANES)],
        group,
        place,
        raw,
        other,
        marks,
        half,
        far_half,
        scalars=2,
    )
    speed_shape = (3, 2, FINE, LANES)
    first, second = swapped(first, second)
    speeds, rates = call(inner_kernel, [speed_shape, (256, LANES)], [(4, 80, LANES)], fixed)
    own, send, old_left, old_right = call(
        first_kernel,
        [(320, LANES), (224, LANES), (176, LANES), (176, LANES)],
        [(128, LANES)],
        place,
        fixed,
        first,
        second,
        speeds,
        rates,
        scalars=1,
    )
    first, second = swapped(send, send)
    rim, rates = call(
        middle_kernel, [speed_shape, (256, LANES)], [(4, 80, LANES)], own, old_left, old_right, speeds
    )
    newer, first, second = call(
        second_kernel,
        [(576, LANES), (192, LANES), (192, LANES)],
        [(6, 80, LANES), (128, LANES), (224, LANES), (224, LANES), (192, LANES), (192, LANES)],
        place,
        own,
        first,
        second,
        fixed,
        old_left,
        old_right,
        speeds,
        rim,
        rates,
        scalars=1,
    )
    first, second = swapped(first, second)
    rates = call(late_kernel, [(384, LANES)], [(6, 80, LANES)], newer, speeds, rim)
    result = call(
        third_kernel,
        [(64, LANES)],
        [
            (8, 80, LANES),
            (8, 80, LANES),
            (6, FINE, LANES),
            (4, 80, LANES),
            (4, 2 * FINE, LANES),
            (128, LANES),
            (192, LANES),
            (192, LANES),
        ],
        place,
        newer,
        first,
        second,
        own,
        fixed,
        old_left,
        old_right,
        speeds,
        rim,
        rates,
        scalars=1,
    )
    keep, send = call(
        sort_kernel, [(64, LANES), (FLOW, LANES)], [], group, result, crossed(result, 1), scalars=1
    )
    return call(merge_kernel, [(FLOW, 2, LANES)], [], group, keep, crossed(send, 2), scalars=1, last=True)[None]


def solution(mesh):
    placed = (
        P("grp", None, "gx", "gy"),
        P("grp", None, "gx", "gy"),
        P(None, "gx", "gy"),
        P("gx", "gy"),
    )
    return jax.shard_map(
        on_device, mesh=mesh, in_specs=placed, out_specs=P("grp", None, "gx", "gy"), check_vma=False
    )
```
